32 devices in a mesh: dp: 16 (over z, x, core), fsdp: 2 (over y).
Axes of the slice: x: 2, y: 2, z: 4, core: 2. Of those that a mesh axis runs over, the one named last changes fastest.
Arguments:
- inputs: bfloat16 [128, 256, 512], P(('dp', 'fsdp')), may hold values from -0.3125 to 0.3125
- out_grad: bfloat16 [128, 256, 512], P(('dp', 'fsdp')), may hold values from -6 to 6
- coeff_fixed: int32 [128, 16], P(('dp', 'fsdp')), may hold values from 0 to 4096
- atom_counts: int32 [128], P(('dp', 'fsdp')), may hold values from 64 to 256, as said below
- experts: bfloat16 [16, 512, 512], P(None, ('dp', 'fsdp')), may hold values from -0.125 to 0.125
Outputs:
- in_grad: bfloat16 [128, 256, 512], P(('dp', 'fsdp'))
- expert_grad: float32 [16, 512, 512], P(None, ('dp', 'fsdp'))
The draws below stay inside these ranges and needn't reach their ends.
Inputs may be any that keep to these rules, and one draw needn't show every extreme that they name: `atom_counts`: some system has exactly 256 atoms and some exactly 64.
All inputs are finite; a program needn't handle non-finite values.
Results may differ from the reference program's by a relative error of at most 0.0049.
Values may be sent and summed in bfloat16 or wider, within the bound.
A program may use at most 128 MiB of HBM per device.

```python
import jax
import jax.numpy as jnp
from jax import lax

D = 512
EXPERTS = 16
SYS_DEV = 4
MAX_ATOMS = 256
SYSTEMS = 128


def draw_atom_counts(key, part):
    first = jax.random.fold_in(key, 11)
    second = jax.random.fold_in(key, 12)
    counts = jax.random.randint(first, (SYSTEMS,), MAX_ATOMS // 4, MAX_ATOMS + 1, dtype=jnp.int32)
    where = jax.random.randint(second, (), 0, SYSTEMS, dtype=jnp.int32)
    counts = counts.at[where].set(MAX_ATOMS)
    counts = counts.at[(where + 1) % SYSTEMS].set(MAX_ATOMS // 4)
    return counts


def touch_ends(array, rng, smallest, largest):
    dims = array.shape
    place = [jax.random.randint(jax.random.fold_in(rng, axis), (), 0, dims[axis]) for axis in range(len(dims))]
    array = array.at[tuple(place)].set(smallest)
    longest = dims.index(max(dims))
    place[longest] = (place[longest] + 1) % dims[longest]
    return array.at[tuple(place)].set(largest)


def spiked(result, own_key, source, target, blocks, factor):
    owner, partner = [(jnp.arange(result.shape[dim]) // (result.shape[dim] // blocks)).reshape([-1 if axis == dim else 1 for axis in range(result.ndim)]) for dim in (source, target)]
    chosen = jax.random.permutation(own_key, blocks)[partner]
    strong = (owner == chosen) | (owner == (partner + blocks // 2) % blocks)
    return jnp.where(strong, factor * result, result)


def shard_levels(rng, dims, cuts, low, top_value):
    gain, own = 1.0, jax.random.fold_in(rng, 6)
    for position, shards_of in cuts:
        draws = jnp.exp(jax.random.uniform(jax.random.fold_in(own, position), (shards_of,), jnp.float32, low / len(cuts), top_value / len(cuts)))
        gain = gain * jnp.repeat(draws, dims[position] // shards_of).reshape([-1 if axis == position else 1 for axis in range(len(dims))])
    return gain


def noise(stream_key, shape, deviation, most, split=(), kind=jnp.bfloat16):
    array = deviation * jax.random.normal(stream_key, shape, jnp.float32)
    if split:
        array = array * shard_levels(stream_key, shape, split, -0.22, 0.18)
    return jnp.clip(array, -most, most).astype(kind)


def heavy_noise(own_key, dims, scale, reach, split, heavy, held_as=jnp.bfloat16):
    entries = scale * jax.random.normal(own_key, dims, jnp.float32)
    if split:
        entries = entries * shard_levels(own_key, dims, split, -0.22, 0.18)
    return jnp.clip(spiked(entries, jax.random.fold_in(own_key, 3), *heavy), -reach, reach).astype(held_as)


def setup_inputs(seed: int = 0) -> dict:
    streams_of = jax.random.split(jax.random.key(seed), 6)
    inputs = heavy_noise(streams_of[0], (SYSTEMS, MAX_ATOMS, D), (2.0 / (SYSTEMS * MAX_ATOMS) ** 0.5), 0.3125, ((0, 32),), (0, 2, 32, 2.75))
    out_grad = noise(streams_of[1], (SYSTEMS, MAX_ATOMS, D), 1.0, 6.0, ((0, 32),))
    coeff_fixed = touch_ends(jax.random.randint(streams_of[2], (SYSTEMS, EXPERTS), 0, 4097), jax.random.fold_in(streams_of[2], 1), 0, 4096).astype(jnp.int32)
    atom_counts = draw_atom_counts(jax.random.fold_in(streams_of[5], 71), 0)
    experts = noise(streams_of[4], (EXPERTS, D, D), (4 * D) ** -0.5, 0.125, ((1, 32),))
    return dict(inputs=inputs, out_grad=out_grad, coeff_fixed=coeff_fixed, atom_counts=atom_counts, experts=experts)


HIGH = lax.Precision.HIGHEST


def reference(inputs, out_grad, coeff_fixed, atom_counts, experts):
    nsys = inputs.shape[0]
    blocks = nsys // SYS_DEV
    flat_experts = experts.astype(jnp.float32).reshape(EXPERTS, D * D)
    xs = inputs.reshape(blocks, SYS_DEV, MAX_ATOMS, D)
    gs = out_grad.reshape(blocks, SYS_DEV, MAX_ATOMS, D)
    qs = coeff_fixed.reshape(blocks, SYS_DEV, EXPERTS)
    ns = atom_counts.reshape(blocks, SYS_DEV)

    def step(total, block):
        acts, grads, fixed, counts = block
        coeffs = fixed.astype(jnp.float32) / 4096.0
        valid = jnp.arange(MAX_ATOMS, dtype=jnp.int32)[None, :] < counts[:, None]
        masked = jnp.where(valid[:, :, None], grads, jnp.zeros_like(grads)).astype(jnp.float32)
        merged = jnp.dot(coeffs, flat_experts, precision=HIGH).reshape(SYS_DEV, D, D)
        merged = lax.optimization_barrier(merged.astype(jnp.bfloat16)).astype(jnp.float32)
        in_grad = jnp.einsum("smj,sij->smi", masked, merged, precision=HIGH).astype(jnp.bfloat16)
        per_system = jnp.einsum("smi,smj->sij", acts.astype(jnp.float32), masked, precision=HIGH)
        total = total + jnp.einsum("se,sij->eij", coeffs, per_system, precision=HIGH)
        return total, in_grad

    total, in_grads = lax.scan(step, jnp.zeros((EXPERTS, D, D), jnp.float32), (xs, gs, qs, ns))
    return in_grads.reshape(nsys, MAX_ATOMS, D), total
```

```python
import functools

import jax
import jax.numpy as jnp
from jax import lax
from jax.experimental import pallas as pl
from jax.experimental.pallas import tpu as pltpu
from jax.sharding import PartitionSpec as P

HIGH = lax.Precision.HIGHEST
MESH = pl.DeviceIdType.MESH
BF16 = jnp.bfloat16
F32 = jnp.float32
NEAR_ORDER = (5, 7, 4, 1, 6, 3, 2)


def dot(a, b, ca, cb):
    return lax.dot_general(a, b, (((ca,), (cb,)), ((), ())), preferred_element_type=F32)


def kernel(nz, n_sys, n_exp, rows, width,
           counts_ref, co_ref, in_ref, og_ref, ex_ref,
           ig_ref, eg_ref,
           mk, cl, ca, ka, kt, kp, kq, pb, g, pc, gc, eo, zs, zr, xg, mb, mc, mr, ps, pr,
           loc, ka_s, ka_r, xp_s, xp_r, xz_s, xz_r, pb_s, pb_r, pc_s, pc_r, zs_s, zs_r,
           mb_s, mb_r, mc_s, mc_r, ps_s, ps_r):
    dp = lax.axis_index("dp")
    y = lax.axis_index("fsdp")
    z = dp // 4
    x = lax.rem(dp // 2, 2)
    c = lax.rem(dp, 2)
    me = x * 4 + c * 2 + y
    sr = n_sys * rows
    half_w = width // 2
    span = 8 * rows
    lo_cols, hi_cols = pl.ds(0, half_w), pl.ds(half_w, half_w)

    def flip(v, d):
        return lax.rem(v + d, 2)

    def place(fx, fc, fy):
        xx, cc, yy = flip(x, fx), flip(c, fc), flip(y, fy)
        return xx * 4 + cc * 2 + yy, ((z * 2 + xx) * 2 + cc, yy)

    def near(j):
        return place(j // 4, j // 2 % 2, j % 2)

    def turned(fp, fq, fc):
        return place(fp * (1 - c) + fq * c, fc, fq * (1 - c) + fp * c)

    p_at = x * (1 - c) + y * c
    q_at = y * (1 - c) + x * c

    half = z // 2
    zm = z + half * (3 - 2 * z)
    mid = zm == 1

    def actual(v):
        return v + half * (3 - 2 * v)

    def line(v):
        return (actual(v) * 2 + x) * 2 + c, y

    def arrival(n):
        return actual((zm, 1 - zm, 2, 3)[n])

    def target(n):
        return actual((3, 2, 1 - zm, zm)[n])

    plane = NEAR_ORDER
    peers = [near(j)[1] for j in plane] + [((lax.rem(z + k, nz) * 2 + x) * 2 + c, y) for k in range(1, nz)]
    barrier = pltpu.get_barrier_semaphore()
    for peer in peers:
        pl.semaphore_signal(barrier, inc=1, device_id=peer, device_id_type=MESH)

    col = lax.broadcasted_iota(jnp.int32, cl.shape[1:], 1)
    row = lax.broadcasted_iota(jnp.int32, cl.shape[1:], 0)
    fixed = jnp.zeros(cl.shape[1:], jnp.int32)
    for s in range(n_sys):
        for e in range(n_exp):
            fixed = jnp.where((row == s) & (col == e), co_ref[s, e], fixed)
    cl[0] = ((fixed >> 6).astype(F32) / 64.0).astype(BF16)
    cl[1] = ((fixed & 63).astype(F32) / 4096.0).astype(BF16)
    pl.semaphore_wait(barrier, len(peers))

    def remote(src, dst, s, r, peer):
        return pltpu.make_async_remote_copy(
            src_ref=src, dst_ref=dst, send_sem=s, recv_sem=r, device_id=peer, device_id_type=MESH
        )

    sent = []

    def send(src, dst, s, r, peer):
        copy = remote(src, dst, s, r, peer)
        copy.start()
        sent.append(copy)
        return copy

    n_loc = [0]

    def local(src, dst):
        copy = pltpu.make_async_copy(src, dst, loc.at[n_loc[0]])
        n_loc[0] += 1
        copy.start()
        return copy

    def own(i):
        return ex_ref.at[:, (lo_cols, hi_cols)[i]] if i < 2 else xg.at[2, z]

    def relay(i, src, block, n, to):
        return remote(src, xg.at[i, block], xz_s.at[i, n], xz_r.at[i, block], to)

    def offer(i):
        relay(i, own(i), z, 0, line(1 - zm)).start()

        @pl.when(mid)
        def _():
            relay(i, own(i), z, nz, line(2)).start()

    xp = send(own(1), xg.at[2, z], xp_s.at[0], xp_r.at[0], turned(1, 0, 0)[1])
    offer(0)
    offer(1)
    ca_c = [send(cl, ca.at[me], ka_s.at[j - 1], ka_r.at[j - 1], near(j)[1]) for j in plane]
    ca_own = local(cl, ca.at[me])

    for s in range(n_sys):
        slot = lax.broadcasted_iota(jnp.int32, og_ref.shape[1:], 0)
        mk[s] = jnp.where(slot < counts_ref[s], og_ref[s], jnp.zeros(og_ref.shape[1:], BF16))

    pb_c, g_own, pc_c, gc_own = {}, {}, {}, {}
    takers = (((0, 0, 0), (1, 0, 0)), ((0, 0, 1), (0, 1, 1)), ((0, 1, 0), (1, 1, 0)), ((1, 0, 1), (1, 1, 1)))

    def produce(k):
        lanes = pl.ds(pl.multiple_of(target(k) * span, span), span)
        for s in range(n_sys):
            prod = dot(in_ref[s, :, lanes], mk[s], 0, 0).astype(BF16)
            for b in range(8):
                pb[b, k, s * rows:(s + 1) * rows, :] = prod[b * rows:(b + 1) * rows, :half_w]
                pc[b, k, s * rows:(s + 1) * rows, :] = prod[b * rows:(b + 1) * rows, half_w:]
        for v in (2, 3, 1):
            at = (p_at if v % 2 else q_at) * 2 + c
            for i in (1, 0):
                src = pc.at[turned(*takers[v][i])[0], k]
                pc_c[k, v, i] = send(src, gc.at[k, i, at], pc_s.at[k, v - 1, i], pc_r.at[k, v - 1, i],
                                     turned(*takers[v][0])[1])
        for j in plane:
            to, peer = near(j)
            pb_c[k, j] = send(pb.at[to, k], g.at[k, me], pb_s.at[k, j - 1], pb_r.at[k, j - 1], peer)
        g_own[k] = local(pb.at[me, k], g.at[k, me])
        for i in range(2):
            gc_own[k, i] = local(pc.at[turned(*takers[0][i])[0], k], gc.at[k, i, q_at * 2 + c])

    mb_c, m_own, mc_c, mc_own = {}, {}, {}, {}

    def merge(k):
        zz = arrival(k)

        def block(i):
            return ex_ref[:, (lo_cols, hi_cols)[i]] if k == 0 and i < 2 else xg[i, zz]

        for i in (1, 2):
            mc[k, i - 1] = (dot(kp[0], block(i), 1, 0) + dot(kp[1], block(i), 1, 0)).astype(BF16).reshape(
                4, n_sys, rows, half_w)
            owner = turned(i - 1, 0, 0)[0]
            for v, (fq, fc) in ((2, (1, 0)), (3, (1, 1)), (1, (0, 1))):
                u = flip(q_at, fq) * 2 + flip(c, fc)
                mc_c[k, v, i] = send(mc.at[k, i - 1, u], mr.at[:, zz, owner, :, hi_cols],
                                     mc_s.at[k, v - 1, i - 1], mc_r.at[k, v - 1, i - 1], turned(0, fq, fc)[1])
            mc_own[k, i] = local(mc.at[k, i - 1, q_at * 2 + c], mr.at[:, zz, owner, :, hi_cols])
        mb[k] = (dot(ka[0], block(0), 1, 0) + dot(ka[1], block(0), 1, 0)).astype(BF16).reshape(
            8, n_sys, rows, half_w)
        for j in plane:
            to, peer = near(j)
            mb_c[k, j] = send(mb.at[k, to], mr.at[:, zz, me, :, lo_cols], mb_s.at[k, j - 1], mb_r.at[k, j - 1], peer)
        m_own[k] = local(mb.at[k, me], mr.at[:, zz, me, :, lo_cols])

    def landed(slot, i):
        remote(zs.at[0, i], zr.at[slot, i], zs_s.at[0, i], zs_r.at[slot, i], line(1 - zm)).wait_recv()
        return zr[slot, i].astype(F32)

    def reduce(k):
        for i in range(2):
            gc_own[k, i].wait()
            for v in (1, 2, 3):
                pc_c[k, v, i].wait_recv()
        for i in (1, 0):
            block = gc[k, i].reshape(4 * sr, half_w)
            eo[k, i + 1] = dot(kq[0], block, 1, 0) + dot(kq[1], block, 1, 0)
            begin(k, i + 1)
        g_own[k].wait()
        for j in plane:
            pb_c[k, j].wait_recv()
        block = g[k].reshape(8 * sr, half_w)
        eo[k, 0] = dot(kt[0], block, 1, 0) + dot(kt[1], block, 1, 0)
        begin(k, 0)

    def onward(k, i):
        slot = (2 * zm, 1 + 3 * zm, 3)[k]
        return remote(zs.at[k, i], zr.at[slot, i], zs_s.at[k, i], zs_r.at[slot, i],
                      line((zm + 1, zm + 1, 1 - zm)[k]))

    def begin(k, i):
        if k < nz - 1:
            @pl.when(zm == 0)
            def _():
                zs[k, i] = eo[k, i].astype(BF16)
                onward(k, i).start()

    def proceed(k, i):
        @pl.when(mid)
        def _():
            zs[k, i] = (eo[k, i] + landed(k, i)).astype(BF16)
            onward(k, i).start()

    def finish(k):
        m_own[k].wait()
        for j in plane:
            mb_c[k, j].wait_recv()
        for i in (1, 2):
            mc_own[k, i].wait()
            for v in (1, 2, 3):
                mc_c[k, v, i].wait_recv()
        zz = arrival(k)
        lanes = pl.ds(pl.multiple_of(zz * span, span), span)
        for s in range(n_sys):
            ig_ref[s, :, lanes] = dot(mk[s], mr[s, zz].reshape(span, width), 1, 1).astype(BF16)

    def came(n, i):
        block = arrival(n)
        relay(i, own(0), block, n, line(1 - zm)).wait_recv()

    def handed(n, i):
        block = arrival(n)

        @pl.when(mid)
        def _():
            came(n, i)
            relay(i, xg.at[i, block], block, n, line(2 if n == 1 else 0)).start()

    def awaited(n):
        @pl.when(zm == 0)
        def _():
            for i in range(3):
                came(n, i)

    produce(0)
    xp.wait_recv()
    offer(2)
    for k in range(1, nz):
        produce(k)

    ca_own.wait()
    for copy in ca_c:
        copy.wait_recv()
    er_rows = n_exp * rows
    lane = lax.broadcasted_iota(jnp.int32, (cl.shape[2], er_rows), 1)
    first = lax.broadcasted_iota(jnp.int32, (cl.shape[2], er_rows), 0) * rows
    pick = jnp.where((lane >= first) & (lane < first + rows), 1.0, 0.0).astype(BF16)
    wide = dot(ca[...].reshape(16 * cl.shape[1], cl.shape[2]), pick, 1, 0)
    across = lax.broadcasted_iota(jnp.int32, (rows, er_rows), 1) % rows
    diagonal = across == lax.broadcasted_iota(jnp.int32, (rows, er_rows), 0)
    for d in range(8):
        for h in range(2):
            for s in range(n_sys):
                at = (d * 2 + h) * cl.shape[1] + s
                value = jnp.broadcast_to(wide[at:at + 1, :], (rows, er_rows))
                spot = (d * n_sys + s) * rows
                ka[h, spot:spot + rows, :] = jnp.where(diagonal, value, 0.0).astype(BF16)
    for h in range(2):
        for u in range(4):
            uq, uc = u // 2, u % 2
            at = (x * (1 - c) + uq * c) * 4 + uc * 2 + uq * (1 - c) + y * c
            kp[h, u * sr:(u + 1) * sr, :] = ka[h, pl.ds(pl.multiple_of(at * sr, sr), sr), :]
    merge(0)
    for h in range(2):
        kt[h] = ka[h].T
        kq[h] = kp[h].T

    for i in range(2):
        handed(1, i)
        handed(2, i)
    reduce(0)
    handed(1, 2)
    handed(2, 2)
    reduce(1)
    awaited(1)
    merge(1)
    handed(3, 0)
    proceed(0, 2)
    handed(3, 1)
    proceed(0, 1)
    reduce(2)
    handed(3, 2)
    proceed(0, 0)
    awaited(2)
    merge(2)
    reduce(3)
    awaited(3)
    merge(3)
    for i in (2, 1, 0):
        proceed(1, i)
        proceed(2, i)
    finish(0)
    finish(1)

    def total(i):
        eo[nz - 1, i] += landed(3, i)

        @pl.when(mid)
        def _():
            eo[nz - 1, i] += landed(4, i)

    total(2)
    ps[...] = eo[nz - 1, 2].astype(BF16)
    ps_c = send(ps, pr, ps_s.at[0], ps_r.at[0], turned(1, 0, 0)[1])
    total(1)
    finish(2)
    total(0)
    eg_ref[:, lo_cols] = eo[nz - 1, 0]
    finish(3)
    ps_c.wait_recv()
    eg_ref[:, hi_cols] = eo[nz - 1, 1] + pr[...].astype(F32)

    for i in range(3):
        relay(i, own(0), z, 0, line(1 - zm)).wait_send()
        for k in range(nz - 1):
            onward(k, i).wait_send()

        @pl.when(mid)
        def _():
            relay(i, own(0), z, nz, line(2)).wait_send()
            for n in range(1, nz):
                relay(i, own(0), z, n, line(0)).wait_send()

    for copy in sent:
        copy.wait_send()


def fused(inputs, out_grad, coeff_fixed, atom_counts, experts, nz):
    n_sys, n_slots, width = inputs.shape
    n_exp, rows, _ = experts.shape
    sr, er_rows = n_sys * rows, n_exp * rows
    half_w = width // 2
    vmem = pl.BlockSpec(memory_space=pltpu.VMEM)
    smem = pl.BlockSpec(memory_space=pltpu.SMEM)
    dma = pltpu.SemaphoreType.DMA
    in_grad, expert_grad = pl.pallas_call(
        functools.partial(kernel, nz, n_sys, n_exp, rows, width),
        out_shape=(
            jax.ShapeDtypeStruct(inputs.shape, BF16),
            jax.ShapeDtypeStruct((er_rows, width), F32),
        ),
        in_specs=[smem, smem, vmem, vmem, vmem],
        out_specs=(vmem, vmem),
        scratch_shapes=[
            pltpu.VMEM(out_grad.shape, BF16),
            pltpu.VMEM((2, 16, 128), BF16),
            pltpu.VMEM((8, 2, 16, 128), BF16),
            pltpu.VMEM((2, 8 * sr, er_rows), BF16),
            pltpu.VMEM((2, er_rows, 8 * sr), BF16),
            pltpu.VMEM((2, 4 * sr, er_rows), BF16),
            pltpu.VMEM((2, er_rows, 4 * sr), BF16),
            pltpu.VMEM((8, nz, sr, half_w), BF16),
            pltpu.VMEM((nz, 8, sr, half_w), BF16),
            pltpu.VMEM((8, nz, sr, half_w), BF16),
            pltpu.VMEM((nz, 2, 4, sr, half_w), BF16),
            pltpu.VMEM((nz, 3, er_rows, half_w), F32),
            pltpu.VMEM((nz - 1, 3, er_rows, half_w), BF16),
            pltpu.VMEM((nz + 1, 3, er_rows, half_w), BF16),
            pltpu.VMEM((3, nz, er_rows, half_w), BF16),
            pltpu.VMEM((nz, 8, n_sys, rows, half_w), BF16),
            pltpu.VMEM((nz, 2, 4, n_sys, rows, half_w), BF16),
            pltpu.VMEM((n_sys, nz, 8, rows, width), BF16),
            pltpu.VMEM((er_rows, half_w), BF16),
            pltpu.VMEM((er_rows, half_w), BF16),
            dma((1 + 6 * nz,)),
            dma((7,)), dma((7,)), dma((1,)), dma((1,)), dma((3, nz + 1)), dma((3, nz)),
            dma((nz, 7)), dma((nz, 7)), dma((nz, 3, 2)), dma((nz, 3, 2)),
            dma((nz - 1, 3)), dma((nz + 1, 3)),
            dma((nz, 7)), dma((nz, 7)), dma((nz, 3, 2)), dma((nz, 3, 2)), dma((1,)), dma((1,)),
        ],
        compiler_params=pltpu.CompilerParams(collective_id=0, has_side_effects=True),
    )(atom_counts, coeff_fixed, inputs, out_grad, experts.reshape(er_rows, width))
    return in_grad, expert_grad.reshape(n_exp, rows, width)


def plain(inputs, out_grad, coeff_fixed, atom_counts, experts):
    both = ("dp", "fsdp")
    n_sys, n_slots, width = inputs.shape
    n_exp, rows, _ = experts.shape
    coeffs = lax.all_gather(coeff_fixed, both, axis=0, tiled=True).astype(F32) / 4096.0
    valid = lax.broadcasted_iota(jnp.int32, (n_sys, n_slots), 1) < atom_counts[:, None]
    masked = jnp.where(valid[:, :, None], out_grad, jnp.zeros_like(out_grad))
    merged = jnp.einsum("se,eij->sij", coeffs, experts.astype(F32), precision=HIGH).astype(BF16)
    merged = lax.all_to_all(merged, both, split_axis=0, concat_axis=1, tiled=True)
    per_system = jnp.einsum("smi,smj->sij", inputs, masked, preferred_element_type=F32)
    per_system = lax.all_to_all(per_system, both, split_axis=1, concat_axis=0, tiled=True)
    expert_grad = jnp.einsum("se,sij->eij", coeffs, per_system, precision=HIGH)
    in_grad = jnp.einsum("smj,sij->smi", masked, merged, preferred_element_type=F32).astype(BF16)
    return in_grad, expert_grad


def solution(mesh):
    n_dp, n_fsdp = mesh.shape["dp"], mesh.shape["fsdp"]

    def shards(inputs, out_grad, coeff_fixed, atom_counts, experts):
        n_sys, _, width = inputs.shape
        n_exp, rows, _ = experts.shape
        if n_dp == 16 and n_fsdp == 2 and rows % 16 == 0 and n_sys <= 16 and n_exp <= 128 and width % 256 == 0:
            return fused(inputs, out_grad, coeff_fixed, atom_counts, experts, n_dp // 4)
        return plain(inputs, out_grad, coeff_fixed, atom_counts, experts)

    placed = (
        P(("dp", "fsdp"), None, None),
        P(("dp", "fsdp"), None, None),
        P(("dp", "fsdp"), None),
        P(("dp", "fsdp")),
        P(None, ("dp", "fsdp"), None),
    )
    return jax.shard_map(
        shards,
        mesh=mesh,
        in_specs=placed,
        out_specs=(P(("dp", "fsdp"), None, None), P(None, ("dp", "fsdp"), None)),
        check_vma=False,
    )
```

```python
import functools

import jax
import jax.numpy as jnp
from jax import lax
from jax.experimental import pallas as pl
from jax.experimental.pallas import tpu as pltpu
from jax.sharding import PartitionSpec as P

HIGH = lax.Precision.HIGHEST
MESH = pl.DeviceIdType.MESH
BF16 = jnp.bfloat16
F32 = jnp.float32
NEAR_ORDER = (5, 7, 4, 1, 6, 3, 2)


def dot(a, b, ca, cb):
    return lax.dot_general(a, b, (((ca,), (cb,)), ((), ())), preferred_element_type=F32)


def kernel(nz, n_sys, n_exp, rows, width,
           counts_hbm, co_hbm, in_hbm, og_hbm, ex_hbm,
           ig_ref, eg_ref,
           counts_ref, co_ref, in_ref, ex_ref, mk, cl, ca, ka, kt, kp, kq, pb, g, pc, gc, eo, zs, zr, xg, mb, mc, mr, ps, pr,
           ld, loc, ka_s, ka_r, xp_s, xp_r, xz_s, xz_r, pb_s, pb_r, pc_s, pc_r, zs_s, zs_r,
           mb_s, mb_r, mc_s, mc_r, ps_s, ps_r):
    dp = lax.axis_index("dp")
    y = lax.axis_index("fsdp")
    z = dp // 4
    x = lax.rem(dp // 2, 2)
    c = lax.rem(dp, 2)
    me = x * 4 + c * 2 + y
    sr = n_sys * rows
    half_w = width // 2
    span = 8 * rows
    lo_cols, hi_cols = pl.ds(0, half_w), pl.ds(half_w, half_w)

    def flip(v, d):
        return lax.rem(v + d, 2)

    def place(fx, fc, fy):
        xx, cc, yy = flip(x, fx), flip(c, fc), flip(y, fy)
        return xx * 4 + cc * 2 + yy, ((z * 2 + xx) * 2 + cc, yy)

    def near(j):
        return place(j // 4, j // 2 % 2, j % 2)

    def turned(fp, fq, fc):
        return place(fp * (1 - c) + fq * c, fc, fq * (1 - c) + fp * c)

    p_at = x * (1 - c) + y * c
    q_at = y * (1 - c) + x * c

    half = z // 2
    zm = z + half * (3 - 2 * z)
    mid = zm == 1

    def actual(v):
        return v + half * (3 - 2 * v)

    def line(v):
        return (actual(v) * 2 + x) * 2 + c, y

    def arrival(n):
        return actual((zm, 1 - zm, 2, 3)[n])

    def target(n):
        return actual((3, 2, 1 - zm, zm)[n])

    plane = NEAR_ORDER
    peers = [near(j)[1] for j in plane] + [((lax.rem(z + k, nz) * 2 + x) * 2 + c, y) for k in range(1, nz)]
    barrier = pltpu.get_barrier_semaphore()
    for peer in peers:
        pl.semaphore_signal(barrier, inc=1, device_id=peer, device_id_type=MESH)

    def load(n, src, dst):
        copy = pltpu.make_async_copy(src, dst, ld.at[n])
        copy.start()
        return copy

    co_c = load(1 + 2 * n_sys, co_hbm, co_ref)
    counts_c = load(2 + 2 * n_sys, counts_hbm, counts_ref)
    ex_c = load(0, ex_hbm, ex_ref)
    og_c = [load(1 + s, og_hbm.at[s], mk.at[s]) for s in range(n_sys)]
    in_c = [load(1 + n_sys + s, in_hbm.at[s], in_ref.at[s]) for s in range(n_sys)]

    col = lax.broadcasted_iota(jnp.int32, cl.shape[1:], 1)
    row = lax.broadcasted_iota(jnp.int32, cl.shape[1:], 0)
    fixed = jnp.zeros(cl.shape[1:], jnp.int32)
    co_c.wait()
    counts_c.wait()
    for s in range(n_sys):
        for e in range(n_exp):
            fixed = jnp.where((row == s) & (col == e), co_ref[s, e], fixed)
    cl[0] = ((fixed >> 6).astype(F32) / 64.0).astype(BF16)
    cl[1] = ((fixed & 63).astype(F32) / 4096.0).astype(BF16)
    ex_c.wait()
    pl.semaphore_wait(barrier, len(peers))

    def remote(src, dst, s, r, peer):
        return pltpu.make_async_remote_copy(
            src_ref=src, dst_ref=dst, send_sem=s, recv_sem=r, device_id=peer, device_id_type=MESH
        )

    sent = []

    def send(src, dst, s, r, peer):
        copy = remote(src, dst, s, r, peer)
        copy.start()
        sent.append(copy)
        return copy

    n_loc = [0]

    def local(src, dst):
        copy = pltpu.make_async_copy(src, dst, loc.at[n_loc[0]])
        n_loc[0] += 1
        copy.start()
        return copy

    def own(i):
        return ex_ref.at[:, (lo_cols, hi_cols)[i]] if i < 2 else xg.at[2, z]

    def relay(i, src, block, n, to):
        return remote(src, xg.at[i, block], xz_s.at[i, n], xz_r.at[i, block], to)

    def offer(i):
        relay(i, own(i), z, 0, line(1 - zm)).start()

        @pl.when(mid)
        def _():
            relay(i, own(i), z, nz, line(2)).start()

    xp = send(own(1), xg.at[2, z], xp_s.at[0], xp_r.at[0], turned(1, 0, 0)[1])
    offer(0)
    offer(1)
    ca_c = [send(cl, ca.at[me], ka_s.at[j - 1], ka_r.at[j - 1], near(j)[1]) for j in plane]
    ca_own = local(cl, ca.at[me])

    for s in range(n_sys):
        og_c[s].wait()
        slot = lax.broadcasted_iota(jnp.int32, mk.shape[1:], 0)
        mk[s] = jnp.where(slot < counts_ref[s], mk[s], jnp.zeros(mk.shape[1:], BF16))
    for copy in in_c:
        copy.wait()

    pb_c, g_own, pc_c, gc_own = {}, {}, {}, {}
    takers = (((0, 0, 0), (1, 0, 0)), ((0, 0, 1), (0, 1, 1)), ((0, 1, 0), (1, 1, 0)), ((1, 0, 1), (1, 1, 1)))

    def produce(k):
        lanes = pl.ds(pl.multiple_of(target(k) * span, span), span)
        for s in range(n_sys):
            prod = dot(in_ref[s, :, lanes], mk[s], 0, 0).astype(BF16)
            for b in range(8):
                pb[b, k, s * rows:(s + 1) * rows, :] = prod[b * rows:(b + 1) * rows, :half_w]
                pc[b, k, s * rows:(s + 1) * rows, :] = prod[b * rows:(b + 1) * rows, half_w:]
        for v in (2, 3, 1):
            at = (p_at if v % 2 else q_at) * 2 + c
            for i in (1, 0):
                src = pc.at[turned(*takers[v][i])[0], k]
                pc_c[k, v, i] = send(src, gc.at[k, i, at], pc_s.at[k, v - 1, i], pc_r.at[k, v - 1, i],
                                     turned(*takers[v][0])[1])
        for j in plane:
            to, peer = near(j)
            pb_c[k, j] = send(pb.at[to, k], g.at[k, me], pb_s.at[k, j - 1], pb_r.at[k, j - 1], peer)
        g_own[k] = local(pb.at[me, k], g.at[k, me])
        for i in range(2):
            gc_own[k, i] = local(pc.at[turned(*takers[0][i])[0], k], gc.at[k, i, q_at * 2 + c])

    mb_c, m_own, mc_c, mc_own = {}, {}, {}, {}

    def merge(k):
        zz = arrival(k)

        def block(i):
            return ex_ref[:, (lo_cols, hi_cols)[i]] if k == 0 and i < 2 else xg[i, zz]

        for i in (1, 2):
            mc[k, i - 1] = (dot(kp[0], block(i), 1, 0) + dot(kp[1], block(i), 1, 0)).astype(BF16).reshape(
                4, n_sys, rows, half_w)
            owner = turned(i - 1, 0, 0)[0]
            for v, (fq, fc) in ((2, (1, 0)), (3, (1, 1)), (1, (0, 1))):
                u = flip(q_at, fq) * 2 + flip(c, fc)
                mc_c[k, v, i] = send(mc.at[k, i - 1, u], mr.at[:, zz, owner, :, hi_cols],
                                     mc_s.at[k, v - 1, i - 1], mc_r.at[k, v - 1, i - 1], turned(0, fq, fc)[1])
            mc_own[k, i] = local(mc.at[k, i - 1, q_at * 2 + c], mr.at[:, zz, owner, :, hi_cols])
        mb[k] = (dot(ka[0], block(0), 1, 0) + dot(ka[1], block(0), 1, 0)).astype(BF16).reshape(
            8, n_sys, rows, half_w)
        for j in plane:
            to, peer = near(j)
            mb_c[k, j] = send(mb.at[k, to], mr.at[:, zz, me, :, lo_cols], mb_s.at[k, j - 1], mb_r.at[k, j - 1], peer)
        m_own[k] = local(mb.at[k, me], mr.at[:, zz, me, :, lo_cols])

    def landed(slot, i):
        remote(zs.at[0, i], zr.at[slot, i], zs_s.at[0, i], zs_r.at[slot, i], line(1 - zm)).wait_recv()
        return zr[slot, i].astype(F32)

    def reduce(k):
        for i in range(2):
            gc_own[k, i].wait()
            for v in (1, 2, 3):
                pc_c[k, v, i].wait_recv()
        for i in (1, 0):
            block = gc[k, i].reshape(4 * sr, half_w)
            eo[k, i + 1] = dot(kq[0], block, 1, 0) + dot(kq[1], block, 1, 0)
            begin(k, i + 1)
        g_own[k].wait()
        for j in plane:
            pb_c[k, j].wait_recv()
        block = g[k].reshape(8 * sr, half_w)
        eo[k, 0] = dot(kt[0], block, 1, 0) + dot(kt[1], block, 1, 0)
        begin(k, 0)

    def onward(k, i):
        slot = (2 * zm, 1 + 3 * zm, 3)[k]
        return remote(zs.at[k, i], zr.at[slot, i], zs_s.at[k, i], zs_r.at[slot, i],
                      line((zm + 1, zm + 1, 1 - zm)[k]))

    def begin(k, i):
        if k < nz - 1:
            @pl.when(zm == 0)
            def _():
                zs[k, i] = eo[k, i].astype(BF16)
                onward(k, i).start()

    def proceed(k, i):
        @pl.when(mid)
        def _():
            zs[k, i] = (eo[k, i] + landed(k, i)).astype(BF16)
            onward(k, i).start()

    def finish(k):
        m_own[k].wait()
        for j in plane:
            mb_c[k, j].wait_recv()
        for i in (1, 2):
            mc_own[k, i].wait()
            for v in (1, 2, 3):
                mc_c[k, v, i].wait_recv()
        zz = arrival(k)
        lanes = pl.ds(pl.multiple_of(zz * span, span), span)
        for s in range(n_sys):
            ig_ref[s, :, lanes] = dot(mk[s], mr[s, zz].reshape(span, width), 1, 1).astype(BF16)

    def came(n, i):
        block = arrival(n)
        relay(i, own(0), block, n, line(1 - zm)).wait_recv()

    def handed(n, i):
        block = arrival(n)

        @pl.when(mid)
        def _():
            came(n, i)
            relay(i, xg.at[i, block], block, n, line(2 if n == 1 else 0)).start()

    def awaited(n):
        @pl.when(zm == 0)
        def _():
            for i in range(3):
                came(n, i)

    produce(0)
    xp.wait_recv()
    offer(2)
    for k in range(1, nz):
        produce(k)

    ca_own.wait()
    for copy in ca_c:
        copy.wait_recv()
    er_rows = n_exp * rows
    lane = lax.broadcasted_iota(jnp.int32, (cl.shape[2], er_rows), 1)
    first = lax.broadcasted_iota(jnp.int32, (cl.shape[2], er_rows), 0) * rows
    pick = jnp.where((lane >= first) & (lane < first + rows), 1.0, 0.0).astype(BF16)
    wide = dot(ca[...].reshape(16 * cl.shape[1], cl.shape[2]), pick, 1, 0)
    across = lax.broadcasted_iota(jnp.int32, (rows, er_rows), 1) % rows
    diagonal = across == lax.broadcasted_iota(jnp.int32, (rows, er_rows), 0)
    for d in range(8):
        for h in range(2):
            for s in range(n_sys):
                at = (d * 2 + h) * cl.shape[1] + s
                value = jnp.broadcast_to(wide[at:at + 1, :], (rows, er_rows))
                spot = (d * n_sys + s) * rows
                ka[h, spot:spot + rows, :] = jnp.where(diagonal, value, 0.0).astype(BF16)
    for h in range(2):
        for u in range(4):
            uq, uc = u // 2, u % 2
            at = (x * (1 - c) + uq * c) * 4 + uc * 2 + uq * (1 - c) + y * c
            kp[h, u * sr:(u + 1) * sr, :] = ka[h, pl.ds(pl.multiple_of(at * sr, sr), sr), :]
    merge(0)
    for h in range(2):
        kt[h] = ka[h].T
        kq[h] = kp[h].T

    for i in range(2):
        handed(1, i)
        handed(2, i)
    reduce(0)
    handed(1, 2)
    handed(2, 2)
    reduce(1)
    awaited(1)
    merge(1)
    handed(3, 0)
    proceed(0, 2)
    handed(3, 1)
    proceed(0, 1)
    reduce(2)
    handed(3, 2)
    proceed(0, 0)
    awaited(2)
    merge(2)
    reduce(3)
    awaited(3)
    merge(3)
    for i in (2, 1, 0):
        proceed(1, i)
        proceed(2, i)
    finish(0)
    finish(1)

    def total(i):
        eo[nz - 1, i] += landed(3, i)

        @pl.when(mid)
        def _():
            eo[nz - 1, i] += landed(4, i)

    total(2)
    ps[...] = eo[nz - 1, 2].astype(BF16)
    ps_c = send(ps, pr, ps_s.at[0], ps_r.at[0], turned(1, 0, 0)[1])
    total(1)
    finish(2)
    total(0)
    eg_ref[:, lo_cols] = eo[nz - 1, 0]
    finish(3)
    ps_c.wait_recv()
    eg_ref[:, hi_cols] = eo[nz - 1, 1] + pr[...].astype(F32)

    for i in range(3):
        relay(i, own(0), z, 0, line(1 - zm)).wait_send()
        for k in range(nz - 1):
            onward(k, i).wait_send()

        @pl.when(mid)
        def _():
            relay(i, own(0), z, nz, line(2)).wait_send()
            for n in range(1, nz):
                relay(i, own(0), z, n, line(0)).wait_send()

    for copy in sent:
        copy.wait_send()


def settle(ig_ref, eg_ref, ig_hbm, eg_hbm, done):
    copies = [pltpu.make_async_copy(ig_ref, ig_hbm, done.at[0]), pltpu.make_async_copy(eg_ref, eg_hbm, done.at[1])]
    for copy in copies:
        copy.start()
    for copy in copies:
        copy.wait()


def fused(inputs, out_grad, coeff_fixed, atom_counts, experts, nz):
    n_sys, n_slots, width = inputs.shape
    n_exp, rows, _ = experts.shape
    sr, er_rows = n_sys * rows, n_exp * rows
    half_w = width // 2
    vmem = pl.BlockSpec(memory_space=pltpu.VMEM)
    hbm = pl.BlockSpec(memory_space=pltpu.HBM)
    dma = pltpu.SemaphoreType.DMA
    in_grad, expert_grad = pl.pallas_call(
        functools.partial(kernel, nz, n_sys, n_exp, rows, width),
        out_shape=(
            pltpu.VMEM(inputs.shape, BF16),
            pltpu.VMEM((er_rows, width), F32),
        ),
        in_specs=[hbm] * 5,
        out_specs=(vmem, vmem),
        scratch_shapes=[
            pltpu.SMEM(atom_counts.shape, jnp.int32),
            pltpu.SMEM(coeff_fixed.shape, jnp.int32),
            pltpu.VMEM(inputs.shape, BF16),
            pltpu.VMEM((er_rows, width), BF16),
            pltpu.VMEM(out_grad.shape, BF16),
            pltpu.VMEM((2, 16, 128), BF16),
            pltpu.VMEM((8, 2, 16, 128), BF16),
            pltpu.VMEM((2, 8 * sr, er_rows), BF16),
            pltpu.VMEM((2, er_rows, 8 * sr), BF16),
            pltpu.VMEM((2, 4 * sr, er_rows), BF16),
            pltpu.VMEM((2, er_rows, 4 * sr), BF16),
            pltpu.VMEM((8, nz, sr, half_w), BF16),
            pltpu.VMEM((nz, 8, sr, half_w), BF16),
            pltpu.VMEM((8, nz, sr, half_w), BF16),
            pltpu.VMEM((nz, 2, 4, sr, half_w), BF16),
            pltpu.VMEM((nz, 3, er_rows, half_w), F32),
            pltpu.VMEM((nz - 1, 3, er_rows, half_w), BF16),
            pltpu.VMEM((nz + 1, 3, er_rows, half_w), BF16),
            pltpu.VMEM((3, nz, er_rows, half_w), BF16),
            pltpu.VMEM((nz, 8, n_sys, rows, half_w), BF16),
            pltpu.VMEM((nz, 2, 4, n_sys, rows, half_w), BF16),
            pltpu.VMEM((n_sys, nz, 8, rows, width), BF16),
            pltpu.VMEM((er_rows, half_w), BF16),
            pltpu.VMEM((er_rows, half_w), BF16),
            dma((3 + 2 * n_sys,)), dma((1 + 6 * nz,)),
            dma((7,)), dma((7,)), dma((1,)), dma((1,)), dma((3, nz + 1)), dma((3, nz)),
            dma((nz, 7)), dma((nz, 7)), dma((nz, 3, 2)), dma((nz, 3, 2)),
            dma((nz - 1, 3)), dma((nz + 1, 3)),
            dma((nz, 7)), dma((nz, 7)), dma((nz, 3, 2)), dma((nz, 3, 2)), dma((1,)), dma((1,)),
        ],
        compiler_params=pltpu.CompilerParams(
            collective_id=0, has_side_effects=True, vmem_limit_bytes=48 * 1024 * 1024),
    )(*(
        pltpu.with_memory_space_constraint(a, pltpu.HBM)
        for a in (atom_counts, coeff_fixed, inputs, out_grad, experts.reshape(er_rows, width))))
    held = [pltpu.with_memory_space_constraint(a, pltpu.VMEM) for a in (in_grad, expert_grad)]
    in_grad, expert_grad = pl.pallas_call(
        settle,
        out_shape=(
            jax.ShapeDtypeStruct(inputs.shape, BF16),
            jax.ShapeDtypeStruct((er_rows, width), F32),
        ),
        in_specs=[vmem, vmem],
        out_specs=(hbm, hbm),
        scratch_shapes=[dma((2,))],
        compiler_params=pltpu.CompilerParams(vmem_limit_bytes=16 * 1024 * 1024),
    )(*held)
    return in_grad, expert_grad.reshape(n_exp, rows, width)


def plain(inputs, out_grad, coeff_fixed, atom_counts, experts):
    both = ("dp", "fsdp")
    n_sys, n_slots, width = inputs.shape
    n_exp, rows, _ = experts.shape
    coeffs = lax.all_gather(coeff_fixed, both, axis=0, tiled=True).astype(F32) / 4096.0
    valid = lax.broadcasted_iota(jnp.int32, (n_sys, n_slots), 1) < atom_counts[:, None]
    masked = jnp.where(valid[:, :, None], out_grad, jnp.zeros_like(out_grad))
    merged = jnp.einsum("se,eij->sij", coeffs, experts.astype(F32), precision=HIGH).astype(BF16)
    merged = lax.all_to_all(merged, both, split_axis=0, concat_axis=1, tiled=True)
    per_system = jnp.einsum("smi,smj->sij", inputs, masked, preferred_element_type=F32)
    per_system = lax.all_to_all(per_system, both, split_axis=1, concat_axis=0, tiled=True)
    expert_grad = jnp.einsum("se,sij->eij", coeffs, per_system, precision=HIGH)
    in_grad = jnp.einsum("smj,sij->smi", masked, merged, preferred_element_type=F32).astype(BF16)
    return in_grad, expert_grad


def solution(mesh):
    n_dp, n_fsdp = mesh.shape["dp"], mesh.shape["fsdp"]

    def shards(inputs, out_grad, coeff_fixed, atom_counts, experts):
        n_sys, _, width = inputs.shape
        n_exp, rows, _ = experts.shape
        if n_dp == 16 and n_fsdp == 2 and rows % 16 == 0 and n_sys <= 16 and n_exp <= 128 and width % 256 == 0:
            return fused(inputs, out_grad, coeff_fixed, atom_counts, experts, n_dp // 4)
        return plain(inputs, out_grad, coeff_fixed, atom_counts, experts)

    placed = (
        P(("dp", "fsdp"), None, None),
        P(("dp", "fsdp"), None, None),
        P(("dp", "fsdp"), None),
        P(("dp", "fsdp")),
        P(None, ("dp", "fsdp"), None),
    )
    return jax.shard_map(
        shards,
        mesh=mesh,
        in_specs=placed,
        out_specs=(P(("dp", "fsdp"), None, None), P(None, ("dp", "fsdp"), None)),
        check_vma=False,
    )
```

```python
import functools

import jax
import jax.numpy as jnp
from jax import lax
from jax.experimental import pallas as pl
from jax.experimental.pallas import tpu as pltpu
from jax.sharding import PartitionSpec as P

HIGH = lax.Precision.HIGHEST
MESH = pl.DeviceIdType.MESH
BF16 = jnp.bfloat16
F32 = jnp.float32
NEAR_ORDER = (5, 7, 4, 1, 6, 3, 2)


def dot(a, b, ca, cb):
    return lax.dot_general(a, b, (((ca,), (cb,)), ((), ())), preferred_element_type=F32)


def kernel(nz, n_sys, n_exp, rows, width,
           counts_hbm, co_hbm, in_hbm, og_hbm, ex_hbm,
           ig_ref, eg_ref,
           counts_ref, co_ref, in_ref, ex_ref, mk, cl, ca, ka, kt, kp, kq, pb, g, pc, gc, eo, zs, zr, xg, mb, mc, mr, mq, ps, pr,
           ld, loc, ka_s, ka_r, xp_s, xp_r, xz_s, xz_r, pb_s, pb_r, pc_s, pc_r, zs_s, zs_r,
           mb_s, mb_r, mc_s, mc_r, ps_s, ps_r):
    dp = lax.axis_index("dp")
    y = lax.axis_index("fsdp")
    z = dp // 4
    x = lax.rem(dp // 2, 2)
    c = lax.rem(dp, 2)
    me = x * 4 + c * 2 + y
    sr = n_sys * rows
    half_w = width // 2
    span = 8 * rows
    lo_cols, hi_cols = pl.ds(0, half_w), pl.ds(half_w, half_w)

    def flip(v, d):
        return lax.rem(v + d, 2)

    def place(fx, fc, fy):
        xx, cc, yy = flip(x, fx), flip(c, fc), flip(y, fy)
        return xx * 4 + cc * 2 + yy, ((z * 2 + xx) * 2 + cc, yy)

    def near(j):
        return place(j // 4, j // 2 % 2, j % 2)

    def turned(fp, fq, fc):
        return place(fp * (1 - c) + fq * c, fc, fq * (1 - c) + fp * c)

    p_at = x * (1 - c) + y * c
    q_at = y * (1 - c) + x * c

    half = z // 2
    zm = z + half * (3 - 2 * z)
    mid = zm == 1

    def actual(v):
        return v + half * (3 - 2 * v)

    def line(v):
        return (actual(v) * 2 + x) * 2 + c, y

    def arrival(n):
        return actual((zm, 1 - zm, 2, 3)[n])

    def target(n):
        return actual((3, 2, 1 - zm, zm)[n])

    plane = NEAR_ORDER
    peers = [near(j)[1] for j in plane] + [line(1 - zm)]
    barrier = pltpu.get_barrier_semaphore()
    for peer in peers:
        pl.semaphore_signal(barrier, inc=1, device_id=peer, device_id_type=MESH)

    @pl.when(mid)
    def _():
        pl.semaphore_signal(barrier, inc=1, device_id=line(2), device_id_type=MESH)

    def load(n, src, dst):
        copy = pltpu.make_async_copy(src, dst, ld.at[n])
        copy.start()
        return copy

    co_c = load(1 + 2 * n_sys, co_hbm, co_ref)
    counts_c = load(2 + 2 * n_sys, counts_hbm, counts_ref)
    ex_c = load(0, ex_hbm, ex_ref)
    og_c = [load(1 + s, og_hbm.at[s], mk.at[s]) for s in range(n_sys)]
    in_c = [load(1 + n_sys + s, in_hbm.at[s], in_ref.at[s]) for s in range(n_sys)]

    col = lax.broadcasted_iota(jnp.int32, cl.shape[1:], 1)
    row = lax.broadcasted_iota(jnp.int32, cl.shape[1:], 0)
    fixed = jnp.zeros(cl.shape[1:], jnp.int32)
    co_c.wait()
    counts_c.wait()
    for s in range(n_sys):
        for e in range(n_exp):
            fixed = jnp.where((row == s) & (col == e), co_ref[s, e], fixed)
    cl[0] = ((fixed >> 6).astype(F32) / 64.0).astype(BF16)
    cl[1] = ((fixed & 63).astype(F32) / 4096.0).astype(BF16)
    ex_c.wait()
    pl.semaphore_wait(barrier, len(peers) + zm)

    def remote(src, dst, s, r, peer):
        return pltpu.make_async_remote_copy(
            src_ref=src, dst_ref=dst, send_sem=s, recv_sem=r, device_id=peer, device_id_type=MESH
        )

    sent = []

    def send(src, dst, s, r, peer):
        copy = remote(src, dst, s, r, peer)
        copy.start()
        sent.append(copy)
        return copy

    n_loc = [0]

    def local(src, dst):
        copy = pltpu.make_async_copy(src, dst, loc.at[n_loc[0]])
        n_loc[0] += 1
        copy.start()
        return copy

    def own(i):
        return ex_ref.at[:, (lo_cols, hi_cols)[i]] if i < 2 else xg.at[2, z]

    def relay(i, src, block, n, to):
        return remote(src, xg.at[i, block], xz_s.at[i, n], xz_r.at[i, block], to)

    def offer(i):
        relay(i, own(i), z, 0, line(1 - zm)).start()

        @pl.when(mid)
        def _():
            relay(i, own(i), z, nz, line(2)).start()

    xp = send(own(1), xg.at[2, z], xp_s.at[0], xp_r.at[0], turned(1, 0, 0)[1])
    offer(0)
    offer(1)
    ca_c = [send(cl, ca.at[me], ka_s.at[j - 1], ka_r.at[j - 1], near(j)[1]) for j in plane]
    ca_own = local(cl, ca.at[me])

    for s in range(n_sys):
        og_c[s].wait()
        slot = lax.broadcasted_iota(jnp.int32, mk.shape[1:], 0)
        mk[s] = jnp.where(slot < counts_ref[s], mk[s], jnp.zeros(mk.shape[1:], BF16))
    for copy in in_c:
        copy.wait()

    pb_c, g_own, pc_c, gc_own = {}, {}, {}, {}
    takers = ((0, 0, 0), (0, 0, 1), (0, 1, 0), (1, 0, 1))

    def seat(b):
        fx, fc, fy = flip(x, b // 4), flip(c, b // 2 % 2), flip(y, b % 2)
        fp, fq = fx * (1 - c) + fy * c, fy * (1 - c) + fx * c
        return (1 - fc) * (4 * fq + fp) + fc * (2 + 4 * fp + fq)

    def produce(k):
        lanes = pl.ds(pl.multiple_of(target(k) * span, span), span)
        for s in range(n_sys):
            prod = dot(in_ref[s, :, lanes], mk[s], 0, 0).astype(BF16)
            for b in range(8):
                pb[b, k, s * rows:(s + 1) * rows, :] = prod[b * rows:(b + 1) * rows, :half_w]
                pc[k, seat(b), s * rows:(s + 1) * rows, :] = prod[b * rows:(b + 1) * rows, half_w:]
        for v in (2, 3, 1):
            at = (p_at if v % 2 else q_at) * 2 + c
            pc_c[k, v] = send(pc.at[k, 2 * v:2 * v + 2], gc.at[k, :, at], pc_s.at[k, v - 1], pc_r.at[k, v - 1],
                              turned(*takers[v])[1])
        gc_own[k] = local(pc.at[k, 0:2], gc.at[k, :, q_at * 2 + c])

    def deal(h):
        two = slice(2 * h, 2 * h + 2)
        for j in plane:
            to, peer = near(j)
            pb_c[h, j] = send(pb.at[to, two], g.at[two, me], pb_s.at[h, j - 1], pb_r.at[h, j - 1], peer)
        g_own[h] = local(pb.at[me, two], g.at[two, me])

    mb_c, m_own, mc_c, mc_own = {}, {}, {}, {}

    def held(k, i):
        return ex_ref[:, (lo_cols, hi_cols)[i]] if k == 0 and i < 2 else xg[i, arrival(k)]

    def merge(*ks):
        span_k = slice(ks[0], ks[-1] + 1)
        for k in ks:
            for i in (1, 2):
                piece = held(k, i)
                mc[:, :, k, flip(p_at, i - 1)] = (dot(kp[0], piece, 1, 0) + dot(kp[1], piece, 1, 0)).astype(
                    BF16).reshape(4, n_sys, rows, half_w)
        k = ks[-1]
        at = 2 * c + q_at
        for v, (fq, fc) in ((2, (1, 0)), (3, (1, 1)), (1, (0, 1))):
            u = flip(q_at, fq) * 2 + flip(c, fc)
            mc_c[k, v] = send(mc.at[u, :, span_k], mq.at[:, span_k, at], mc_s.at[k, v - 1], mc_r.at[k, v - 1],
                              turned(0, fq, fc)[1])
        mc_own[k] = local(mc.at[q_at * 2 + c, :, span_k], mq.at[:, span_k, at])
        for k in ks:
            piece = held(k, 0)
            mb[:, :, k] = (dot(ka[0], piece, 1, 0) + dot(ka[1], piece, 1, 0)).astype(BF16).reshape(
                8, n_sys, rows, half_w)
        for j in plane:
            to, peer = near(j)
            mb_c[k, j] = send(mb.at[to, :, span_k], mr.at[:, span_k, me], mb_s.at[k, j - 1], mb_r.at[k, j - 1], peer)
        m_own[k] = local(mb.at[me, :, span_k], mr.at[:, span_k, me])

    def landed(slot, i):
        remote(zs.at[0, i], zr.at[slot, i], zs_s.at[0, i], zs_r.at[slot, i], line(1 - zm)).wait_recv()
        return zr[slot, i].astype(F32)

    def reduce(k):
        gc_own[k].wait()
        for v in (1, 2, 3):
            pc_c[k, v].wait_recv()
        for i in (1, 0):
            block = gc[k, i].reshape(4 * sr, half_w)
            eo[k, i + 1] = dot(kq[0], block, 1, 0) + dot(kq[1], block, 1, 0)
            begin(k, i + 1)
        if k % 2 == 0:
            g_own[k // 2].wait()
            for j in plane:
                pb_c[k // 2, j].wait_recv()
        block = g[k].reshape(8 * sr, half_w)
        eo[k, 0] = dot(kt[0], block, 1, 0) + dot(kt[1], block, 1, 0)
        begin(k, 0)

    def onward(k, i):
        slot = (2 * zm, 1 + 3 * zm, 3)[k]
        return remote(zs.at[k, i], zr.at[slot, i], zs_s.at[k, i], zs_r.at[slot, i],
                      line((zm + 1, zm + 1, 1 - zm)[k]))

    def begin(k, i):
        if k < nz - 1:
            @pl.when(zm == 0)
            def _():
                zs[k, i] = eo[k, i].astype(BF16)
                onward(k, i).start()

    def proceed(k, i):
        @pl.when(mid)
        def _():
            zs[k, i] = (eo[k, i] + landed(k, i)).astype(BF16)
            onward(k, i).start()

    def finish(k):
        if k in m_own:
            m_own[k].wait()
            mc_own[k].wait()
            for j in plane:
                mb_c[k, j].wait_recv()
            for v in (1, 2, 3):
                mc_c[k, v].wait_recv()
        lanes = pl.ds(pl.multiple_of(arrival(k) * span, span), span)
        for s in range(n_sys):
            first = mr[s, k].reshape(span, half_w)
            last = jnp.concatenate([mq[s, k, (b % 2, 2 + b // 4)[b // 2 % 2], (b // 4, b % 2)[b // 2 % 2]]
                                    for b in range(8)], axis=0)
            ig_ref[s, :, lanes] = dot(mk[s], jnp.concatenate([first, last], axis=1), 1, 1).astype(BF16)

    def came(n, i):
        block = arrival(n)
        relay(i, own(0), block, n, line(1 - zm)).wait_recv()

    def handed(n, i):
        block = arrival(n)

        @pl.when(mid)
        def _():
            came(n, i)
            relay(i, xg.at[i, block], block, n, line(2 if n == 1 else 0)).start()

    def awaited(n):
        @pl.when(zm == 0)
        def _():
            for i in range(3):
                came(n, i)

    produce(0)
    xp.wait_recv()
    offer(2)
    produce(1)
    deal(0)
    produce(2)
    produce(3)
    deal(1)

    ca_own.wait()
    for copy in ca_c:
        copy.wait_recv()
    er_rows = n_exp * rows
    lane = lax.broadcasted_iota(jnp.int32, (cl.shape[2], er_rows), 1)
    first = lax.broadcasted_iota(jnp.int32, (cl.shape[2], er_rows), 0) * rows
    pick = jnp.where((lane >= first) & (lane < first + rows), 1.0, 0.0).astype(BF16)
    wide = dot(ca[...].reshape(16 * cl.shape[1], cl.shape[2]), pick, 1, 0)
    across = lax.broadcasted_iota(jnp.int32, (rows, er_rows), 1) % rows
    diagonal = across == lax.broadcasted_iota(jnp.int32, (rows, er_rows), 0)
    for d in range(8):
        for h in range(2):
            for s in range(n_sys):
                at = (d * 2 + h) * cl.shape[1] + s
                value = jnp.broadcast_to(wide[at:at + 1, :], (rows, er_rows))
                spot = (d * n_sys + s) * rows
                ka[h, spot:spot + rows, :] = jnp.where(diagonal, value, 0.0).astype(BF16)
    for h in range(2):
        for u in range(4):
            uq, uc = u // 2, u % 2
            at = (x * (1 - c) + uq * c) * 4 + uc * 2 + uq * (1 - c) + y * c
            kp[h, u * sr:(u + 1) * sr, :] = ka[h, pl.ds(pl.multiple_of(at * sr, sr), sr), :]
    for h in range(2):
        kt[h] = ka[h].T
        kq[h] = kp[h].T

    for i in range(2):
        handed(1, i)
        handed(2, i)
    reduce(0)
    handed(1, 2)
    handed(2, 2)
    reduce(1)
    awaited(1)
    merge(0, 1)
    handed(3, 0)
    proceed(0, 2)
    handed(3, 1)
    proceed(0, 1)
    reduce(2)
    handed(3, 2)
    proceed(0, 0)
    awaited(2)
    merge(2)
    reduce(3)
    awaited(3)
    merge(3)
    for i in (2, 1, 0):
        proceed(1, i)
        proceed(2, i)
    finish(1)
    finish(0)

    def total(i):
        eo[nz - 1, i] += landed(3, i)

        @pl.when(mid)
        def _():
            eo[nz - 1, i] += landed(4, i)

    total(2)
    ps[...] = eo[nz - 1, 2].astype(BF16)
    ps_c = send(ps, pr, ps_s.at[0], ps_r.at[0], turned(1, 0, 0)[1])
    total(1)
    finish(2)
    total(0)
    eg_ref[:, lo_cols] = eo[nz - 1, 0]
    finish(3)
    ps_c.wait_recv()
    eg_ref[:, hi_cols] = eo[nz - 1, 1] + pr[...].astype(F32)

    for i in range(3):
        relay(i, own(0), z, 0, line(1 - zm)).wait_send()
        for k in range(nz - 1):
            onward(k, i).wait_send()

        @pl.when(mid)
        def _():
            relay(i, own(0), z, nz, line(2)).wait_send()
            for n in range(1, nz):
                relay(i, own(0), z, n, line(0)).wait_send()

    for copy in sent:
        copy.wait_send()


def settle(ig_ref, eg_ref, ig_hbm, eg_hbm, done):
    copies = [pltpu.make_async_copy(ig_ref, ig_hbm, done.at[0]), pltpu.make_async_copy(eg_ref, eg_hbm, done.at[1])]
    for copy in copies:
        copy.start()
    for copy in copies:
        copy.wait()


def fused(inputs, out_grad, coeff_fixed, atom_counts, experts, nz):
    n_sys, n_slots, width = inputs.shape
    n_exp, rows, _ = experts.shape
    sr, er_rows = n_sys * rows, n_exp * rows
    half_w = width // 2
    vmem = pl.BlockSpec(memory_space=pltpu.VMEM)
    hbm = pl.BlockSpec(memory_space=pltpu.HBM)
    dma = pltpu.SemaphoreType.DMA
    in_grad, expert_grad = pl.pallas_call(
        functools.partial(kernel, nz, n_sys, n_exp, rows, width),
        out_shape=(
            pltpu.VMEM(inputs.shape, BF16),
            pltpu.VMEM((er_rows, width), F32),
        ),
        in_specs=[hbm] * 5,
        out_specs=(vmem, vmem),
        scratch_shapes=[
            pltpu.SMEM(atom_counts.shape, jnp.int32),
            pltpu.SMEM(coeff_fixed.shape, jnp.int32),
            pltpu.VMEM(inputs.shape, BF16),
            pltpu.VMEM((er_rows, width), BF16),
            pltpu.VMEM(out_grad.shape, BF16),
            pltpu.VMEM((2, 16, 128), BF16),
            pltpu.VMEM((8, 2, 16, 128), BF16),
            pltpu.VMEM((2, 8 * sr, er_rows), BF16),
            pltpu.VMEM((2, er_rows, 8 * sr), BF16),
            pltpu.VMEM((2, 4 * sr, er_rows), BF16),
            pltpu.VMEM((2, er_rows, 4 * sr), BF16),
            pltpu.VMEM((8, nz, sr, half_w), BF16),
            pltpu.VMEM((nz, 8, sr, half_w), BF16),
            pltpu.VMEM((nz, 8, sr, half_w), BF16),
            pltpu.VMEM((nz, 2, 4, sr, half_w), BF16),
            pltpu.VMEM((nz, 3, er_rows, half_w), F32),
            pltpu.VMEM((nz - 1, 3, er_rows, half_w), BF16),
            pltpu.VMEM((nz + 1, 3, er_rows, half_w), BF16),
            pltpu.VMEM((3, nz, er_rows, half_w), BF16),
            pltpu.VMEM((8, n_sys, nz, rows, half_w), BF16),
            pltpu.VMEM((4, n_sys, nz, 2, rows, half_w), BF16),
            pltpu.VMEM((n_sys, nz, 8, rows, half_w), BF16),
            pltpu.VMEM((n_sys, nz, 4, 2, rows, half_w), BF16),
            pltpu.VMEM((er_rows, half_w), BF16),
            pltpu.VMEM((er_rows, half_w), BF16),
            dma((3 + 2 * n_sys,)), dma((1 + 4 * nz,)),
            dma((7,)), dma((7,)), dma((1,)), dma((1,)), dma((3, nz + 1)), dma((3, nz)),
            dma((nz // 2, 7)), dma((nz // 2, 7)), dma((nz, 3)), dma((nz, 3)),
            dma((nz - 1, 3)), dma((nz + 1, 3)),
            dma((nz, 7)), dma((nz, 7)), dma((nz, 3)), dma((nz, 3)), dma((1,)), dma((1,)),
        ],
        compiler_params=pltpu.CompilerParams(
            collective_id=0, has_side_effects=True, vmem_limit_bytes=48 * 1024 * 1024),
    )(*(
        pltpu.with_memory_space_constraint(a, pltpu.HBM)
        for a in (atom_counts, coeff_fixed, inputs, out_grad, experts.reshape(er_rows, width))))
    held = [pltpu.with_memory_space_constraint(a, pltpu.VMEM) for a in (in_grad, expert_grad)]
    in_grad, expert_grad = pl.pallas_call(
        settle,
        out_shape=(
            jax.ShapeDtypeStruct(inputs.shape, BF16),
            jax.ShapeDtypeStruct((er_rows, width), F32),
        ),
        in_specs=[vmem, vmem],
        out_specs=(hbm, hbm),
        scratch_shapes=[dma((2,))],
        compiler_params=pltpu.CompilerParams(vmem_limit_bytes=16 * 1024 * 1024),
    )(*held)
    return in_grad, expert_grad.reshape(n_exp, rows, width)


def plain(inputs, out_grad, coeff_fixed, atom_counts, experts):
    both = ("dp", "fsdp")
    n_sys, n_slots, width = inputs.shape
    n_exp, rows, _ = experts.shape
    coeffs = lax.all_gather(coeff_fixed, both, axis=0, tiled=True).astype(F32) / 4096.0
    valid = lax.broadcasted_iota(jnp.int32, (n_sys, n_slots), 1) < atom_counts[:, None]
    masked = jnp.where(valid[:, :, None], out_grad, jnp.zeros_like(out_grad))
    merged = jnp.einsum("se,eij->sij", coeffs, experts.astype(F32), precision=HIGH).astype(BF16)
    merged = lax.all_to_all(merged, both, split_axis=0, concat_axis=1, tiled=True)
    per_system = jnp.einsum("smi,smj->sij", inputs, masked, preferred_element_type=F32)
    per_system = lax.all_to_all(per_system, both, split_axis=1, concat_axis=0, tiled=True)
    expert_grad = jnp.einsum("se,sij->eij", coeffs, per_system, precision=HIGH)
    in_grad = jnp.einsum("smj,sij->smi", masked, merged, preferred_element_type=F32).astype(BF16)
    return in_grad, expert_grad


def solution(mesh):
    n_dp, n_fsdp = mesh.shape["dp"], mesh.shape["fsdp"]

    def shards(inputs, out_grad, coeff_fixed, atom_counts, experts):
        n_sys, _, width = inputs.shape
        n_exp, rows, _ = experts.shape
        if n_dp == 16 and n_fsdp == 2 and rows % 16 == 0 and n_sys <= 16 and n_exp <= 128 and width % 256 == 0:
            return fused(inputs, out_grad, coeff_fixed, atom_counts, experts, n_dp // 4)
        return plain(inputs, out_grad, coeff_fixed, atom_counts, experts)

    placed = (
        P(("dp", "fsdp"), None, None),
        P(("dp", "fsdp"), None, None),
        P(("dp", "fsdp"), None),
        P(("dp", "fsdp")),
        P(None, ("dp", "fsdp"), None),
    )
    return jax.shard_map(
        shards,
        mesh=mesh,
        in_specs=placed,
        out_specs=(P(("dp", "fsdp"), None, None), P(None, ("dp", "fsdp"), None)),
        check_vma=False,
    )
```

```python
import functools

import jax
import jax.numpy as jnp
from jax import lax
from jax.experimental import pallas as pl
from jax.experimental.pallas import tpu as pltpu
from jax.sharding import PartitionSpec as P

HIGH = lax.Precision.HIGHEST
MESH = pl.DeviceIdType.MESH
BF16 = jnp.bfloat16
F32 = jnp.float32
NEAR_ORDER = (5, 7, 4, 1, 6, 3, 2)


def dot(a, b, ca, cb):
    return lax.dot_general(a, b, (((ca,), (cb,)), ((), ())), preferred_element_type=F32)


def kernel(nz, n_sys, n_exp, rows, width,
           counts_hbm, co_hbm, in_hbm, og_hbm, ex_hbm,
           ig_ref, eg_ref,
           counts_ref, co_ref, in_ref, ex_ref, mk, cl, ca, ka, kt, kp, kq, pb, g, pc, gc, eo, ec, zs, zr, zc, xg, xq, mb, mc, mr, mq, ps, pr,
           ld, loc, ka_s, ka_r, xp_s, xp_r, xz_s, xz_r, pb_s, pb_r, pc_s, pc_r, zs_s, zs_r,
           mb_s, mb_r, mc_s, mc_r, ps_s, ps_r):
    dp = lax.axis_index("dp")
    y = lax.axis_index("fsdp")
    z = dp // 4
    x = lax.rem(dp // 2, 2)
    c = lax.rem(dp, 2)
    me = x * 4 + c * 2 + y
    sr = n_sys * rows
    half_w, quarter_w = width // 2, width // 4
    span = 8 * rows
    lo_cols, hi_cols = pl.ds(0, half_w), pl.ds(half_w, half_w)
    second = slice(quarter_w, half_w)

    def cut(near_z):
        return quarter_w if near_z else half_w

    def rest(near_z):
        return slice(cut(near_z) - quarter_w, width - quarter_w)

    def flip(v, d):
        return lax.rem(v + d, 2)

    def place(fx, fc, fy):
        xx, cc, yy = flip(x, fx), flip(c, fc), flip(y, fy)
        return xx * 4 + cc * 2 + yy, ((z * 2 + xx) * 2 + cc, yy)

    def near(j):
        return place(j // 4, j // 2 % 2, j % 2)

    def turned(fp, fq, fc):
        return place(fp * (1 - c) + fq * c, fc, fq * (1 - c) + fp * c)

    p_at = x * (1 - c) + y * c
    q_at = y * (1 - c) + x * c

    half = z // 2
    zm = z + half * (3 - 2 * z)
    mid = zm == 1

    def actual(v):
        return v + half * (3 - 2 * v)

    def line(v):
        return (actual(v) * 2 + x) * 2 + c, y

    def arrival(n):
        return actual((zm, 1 - zm, 2, 3)[n])

    def target(n):
        return actual((3, 2, 1 - zm, zm)[n])

    plane = NEAR_ORDER
    peers = [near(j)[1] for j in plane] + [line(1 - zm)]
    barrier = pltpu.get_barrier_semaphore()
    for peer in peers:
        pl.semaphore_signal(barrier, inc=1, device_id=peer, device_id_type=MESH)

    @pl.when(mid)
    def _():
        pl.semaphore_signal(barrier, inc=1, device_id=line(2), device_id_type=MESH)

    def load(n, src, dst):
        copy = pltpu.make_async_copy(src, dst, ld.at[n])
        copy.start()
        return copy

    co_c = load(1 + 2 * n_sys, co_hbm, co_ref)
    counts_c = load(2 + 2 * n_sys, counts_hbm, counts_ref)
    ex_c = load(0, ex_hbm, ex_ref)
    og_c = [load(1 + s, og_hbm.at[s], mk.at[s]) for s in range(n_sys)]
    in_c = [load(1 + n_sys + s, in_hbm.at[s], in_ref.at[s]) for s in range(n_sys)]

    col = lax.broadcasted_iota(jnp.int32, cl.shape[1:], 1)
    row = lax.broadcasted_iota(jnp.int32, cl.shape[1:], 0)
    fixed = jnp.zeros(cl.shape[1:], jnp.int32)
    co_c.wait()
    counts_c.wait()
    for s in range(n_sys):
        for e in range(n_exp):
            fixed = jnp.where((row == s) & (col == e), co_ref[s, e], fixed)
    cl[0] = ((fixed >> 6).astype(F32) / 64.0).astype(BF16)
    cl[1] = ((fixed & 63).astype(F32) / 4096.0).astype(BF16)
    ex_c.wait()
    pl.semaphore_wait(barrier, len(peers) + zm)

    def remote(src, dst, s, r, peer):
        return pltpu.make_async_remote_copy(
            src_ref=src, dst_ref=dst, send_sem=s, recv_sem=r, device_id=peer, device_id_type=MESH
        )

    sent = []

    def send(src, dst, s, r, peer):
        copy = remote(src, dst, s, r, peer)
        copy.start()
        sent.append(copy)
        return copy

    n_loc = [0]

    def local(src, dst):
        copy = pltpu.make_async_copy(src, dst, loc.at[n_loc[0]])
        n_loc[0] += 1
        copy.start()
        return copy

    def own(i):
        return ex_ref.at[:, (lo_cols, hi_cols)[i]] if i < 2 else xg.at[2, z]

    def relay(i, src, block, n, to):
        return remote(src, xg.at[i, block], xz_s.at[i, n], xz_r.at[i, block], to)

    def offer(i):
        relay(i, own(i), z, 0, line(1 - zm)).start()

        @pl.when(mid)
        def _():
            relay(i, own(i), z, nz, line(2)).start()

    xp = send(own(1), xg.at[2, z], xp_s.at[0], xp_r.at[0], turned(1, 0, 0)[1])
    offer(0)
    offer(1)
    xq_c = send(ex_ref.at[:, second], xq.at[0], xp_s.at[1], xp_r.at[1], turned(1, 0, 0)[1])
    ca_c = [send(cl, ca.at[me], ka_s.at[j - 1], ka_r.at[j - 1], near(j)[1]) for j in plane]
    ca_own = local(cl, ca.at[me])

    for s in range(n_sys):
        og_c[s].wait()
        slot = lax.broadcasted_iota(jnp.int32, mk.shape[1:], 0)
        mk[s] = jnp.where(slot < counts_ref[s], mk[s], jnp.zeros(mk.shape[1:], BF16))
    for copy in in_c:
        copy.wait()

    pb_c, g_own, pc_c, gc_own = {}, {}, {}, {}
    takers = ((0, 0, 0), (0, 0, 1), (0, 1, 0), (1, 0, 1))

    def seat(b):
        fx, fc, fy = flip(x, b // 4), flip(c, b // 2 % 2), flip(y, b % 2)
        fp, fq = fx * (1 - c) + fy * c, fy * (1 - c) + fx * c
        return (1 - fc) * (4 * fq + fp) + fc * (2 + 4 * fp + fq)

    def produce(k):
        lanes = pl.ds(pl.multiple_of(target(k) * span, span), span)
        n, others = cut(k >= 2), rest(k >= 2)
        for s in range(n_sys):
            prod = dot(in_ref[s, :, lanes], mk[s], 0, 0).astype(BF16)
            for b in range(8):
                pb[b, k, s * rows:(s + 1) * rows, :n] = prod[b * rows:(b + 1) * rows, :n]
                pc[k, seat(b), s * rows:(s + 1) * rows, others] = prod[b * rows:(b + 1) * rows, n:]
        for v in (2, 3, 1):
            at = (p_at if v % 2 else q_at) * 2 + c
            pc_c[k, v] = send(pc.at[k, 2 * v:2 * v + 2, :, others], gc.at[k, :, at, :, others], pc_s.at[k, v - 1], pc_r.at[k, v - 1],
                              turned(*takers[v])[1])
        gc_own[k] = local(pc.at[k, 0:2, :, others], gc.at[k, :, q_at * 2 + c, :, others])

    def deal(h):
        two, n = slice(2 * h, 2 * h + 2), cut(h == 1)
        for j in plane:
            to, peer = near(j)
            pb_c[h, j] = send(pb.at[to, two, :, :n], g.at[two, me, :, :n], pb_s.at[h, j - 1], pb_r.at[h, j - 1], peer)
        g_own[h] = local(pb.at[me, two, :, :n], g.at[two, me, :, :n])

    mb_c, m_own, mc_c, mc_own = {}, {}, {}, {}

    def held(k, i):
        return ex_ref[:, (lo_cols, hi_cols)[i]] if k == 0 and i < 2 else xg[i, arrival(k)]

    def mixed(weights, block):
        return (dot(weights[0], block, 1, 0) + dot(weights[1], block, 1, 0)).astype(BF16)

    def merge(*ks):
        span_k = slice(ks[0], ks[-1] + 1)
        close = ks[0] < 2
        n, others = cut(close), rest(close)
        for k in ks:
            for i in (1, 2):
                to = flip(p_at, i - 1)
                mc[:, :, k, to, :, quarter_w:] = mixed(kp, held(k, i)).reshape(4, n_sys, rows, half_w)
                if close:
                    piece = xq[k] if i == 2 else held(k, 0)[:, second]
                    mc[:, :, k, to, :, :quarter_w] = mixed(kp, piece).reshape(4, n_sys, rows, quarter_w)
        k = ks[-1]
        at = 2 * c + q_at
        for v, (fq, fc) in ((2, (1, 0)), (3, (1, 1)), (1, (0, 1))):
            u = flip(q_at, fq) * 2 + flip(c, fc)
            mc_c[k, v] = send(mc.at[u, :, span_k, :, :, others], mq.at[:, span_k, at, :, :, others],
                              mc_s.at[k, v - 1], mc_r.at[k, v - 1], turned(0, fq, fc)[1])
        mc_own[k] = local(mc.at[q_at * 2 + c, :, span_k, :, :, others], mq.at[:, span_k, at, :, :, others])
        for k in ks:
            mb[:, :, k, :, :n] = mixed(ka, held(k, 0)[:, :n]).reshape(8, n_sys, rows, n)
        for j in plane:
            to, peer = near(j)
            mb_c[k, j] = send(mb.at[to, :, span_k, :, :n], mr.at[:, span_k, me, :, :n],
                              mb_s.at[k, j - 1], mb_r.at[k, j - 1], peer)
        m_own[k] = local(mb.at[me, :, span_k, :, :n], mr.at[:, span_k, me, :, :n])

    def landed(slot, i):
        remote(zs.at[0, i], zr.at[slot, i], zs_s.at[0, i], zs_r.at[slot, i], line(1 - zm)).wait_recv()
        return zr[slot, i].astype(F32)

    zc_c = []

    def reduce(k):
        gc_own[k].wait()
        for v in (1, 2, 3):
            pc_c[k, v].wait_recv()
        for i in (1, 0):
            block = gc[k, i, :, :, quarter_w:].reshape(4 * sr, half_w)
            eo[k, i + 1] = dot(kq[0], block, 1, 0) + dot(kq[1], block, 1, 0)
            begin(k, i + 1)
            if k >= 2:
                block = gc[k, i, :, :, :quarter_w].reshape(4 * sr, quarter_w)
                part = dot(kq[0], block, 1, 0) + dot(kq[1], block, 1, 0)
                if i == 0:
                    eo[k, 0, :, second] = part
                elif k == 2:
                    zc[0] = part.astype(BF16)
                    zc_c.append(send(zc.at[0], zc.at[1], xp_s.at[3], xp_r.at[3], line(1 - zm)))
                else:
                    ec[...] = part
        if k % 2 == 0:
            g_own[k // 2].wait()
            for j in plane:
                pb_c[k // 2, j].wait_recv()
        n = cut(k >= 2)
        block = g[k, :, :, :n].reshape(8 * sr, n)
        eo[k, 0, :, :n] = dot(kt[0], block, 1, 0) + dot(kt[1], block, 1, 0)
        begin(k, 0)

    def onward(k, i):
        slot = (2 * zm, 1 + 3 * zm, 3)[k]
        return remote(zs.at[k, i], zr.at[slot, i], zs_s.at[k, i], zs_r.at[slot, i],
                      line((zm + 1, zm + 1, 1 - zm)[k]))

    def begin(k, i):
        if k < nz - 1:
            @pl.when(zm == 0)
            def _():
                zs[k, i] = eo[k, i].astype(BF16)
                onward(k, i).start()

    def proceed(k, i):
        @pl.when(mid)
        def _():
            zs[k, i] = (eo[k, i] + landed(k, i)).astype(BF16)
            onward(k, i).start()

    def finish(k):
        if k in m_own:
            m_own[k].wait()
            mc_own[k].wait()
            for j in plane:
                mb_c[k, j].wait_recv()
            for v in (1, 2, 3):
                mc_c[k, v].wait_recv()
        lanes = pl.ds(pl.multiple_of(arrival(k) * span, span), span)
        for s in range(n_sys):
            first = mr[s, k, :, :, :cut(k < 2)].reshape(span, cut(k < 2))
            last = jnp.concatenate(
                [mq[s, k, (b % 2, 2 + b // 4)[b // 2 % 2], (b // 4, b % 2)[b // 2 % 2], :, rest(k < 2)]
                 for b in range(8)], axis=0)
            ig_ref[s, :, lanes] = dot(mk[s], jnp.concatenate([first, last], axis=1), 1, 1).astype(BF16)

    def came(n, i):
        block = arrival(n)
        relay(i, own(0), block, n, line(1 - zm)).wait_recv()

    def handed(n, i):
        block = arrival(n)

        @pl.when(mid)
        def _():
            came(n, i)
            relay(i, xg.at[i, block], block, n, line(2 if n == 1 else 0)).start()

    def awaited(n):
        @pl.when(zm == 0)
        def _():
            for i in range(3):
                came(n, i)

    produce(0)
    xp.wait_recv()
    offer(2)
    produce(1)
    deal(0)
    produce(2)
    produce(3)
    deal(1)
    xq_c.wait_recv()
    xq_n = send(xq.at[0], xq.at[1], xp_s.at[2], xp_r.at[2], line(1 - zm))

    ca_own.wait()
    for copy in ca_c:
        copy.wait_recv()
    er_rows = n_exp * rows
    lane = lax.broadcasted_iota(jnp.int32, (cl.shape[2], er_rows), 1)
    first = lax.broadcasted_iota(jnp.int32, (cl.shape[2], er_rows), 0) * rows
    pick = jnp.where((lane >= first) & (lane < first + rows), 1.0, 0.0).astype(BF16)
    wide = dot(ca[...].reshape(16 * cl.shape[1], cl.shape[2]), pick, 1, 0)
    across = lax.broadcasted_iota(jnp.int32, (rows, er_rows), 1) % rows
    diagonal = across == lax.broadcasted_iota(jnp.int32, (rows, er_rows), 0)
    for d in range(8):
        for h in range(2):
            for s in range(n_sys):
                at = (d * 2 + h) * cl.shape[1] + s
                value = jnp.broadcast_to(wide[at:at + 1, :], (rows, er_rows))
                spot = (d * n_sys + s) * rows
                ka[h, spot:spot + rows, :] = jnp.where(diagonal, value, 0.0).astype(BF16)
    for h in range(2):
        for u in range(4):
            uq, uc = u // 2, u % 2
            at = (x * (1 - c) + uq * c) * 4 + uc * 2 + uq * (1 - c) + y * c
            kp[h, u * sr:(u + 1) * sr, :] = ka[h, pl.ds(pl.multiple_of(at * sr, sr), sr), :]
    for h in range(2):
        kt[h] = ka[h].T
        kq[h] = kp[h].T

    for i in range(2):
        handed(1, i)
        handed(2, i)
    reduce(0)
    handed(1, 2)
    handed(2, 2)
    reduce(1)
    awaited(1)
    xq_n.wait_recv()
    merge(0, 1)
    handed(3, 0)
    proceed(0, 2)
    handed(3, 1)
    proceed(0, 1)
    reduce(2)
    handed(3, 2)
    proceed(0, 0)
    awaited(2)
    merge(2)
    reduce(3)
    awaited(3)
    merge(3)
    for i in (2, 1, 0):
        proceed(1, i)
        proceed(2, i)
    finish(1)
    finish(0)

    def total(i):
        eo[nz - 1, i] += landed(3, i)

        @pl.when(mid)
        def _():
            eo[nz - 1, i] += landed(4, i)

    total(2)
    zc_c[0].wait_recv()
    ps[:, :quarter_w] = (ec[...] + zc[1].astype(F32)).astype(BF16)
    ps[:, quarter_w:] = eo[nz - 1, 2].astype(BF16)
    ps_c = send(ps, pr, ps_s.at[0], ps_r.at[0], turned(1, 0, 0)[1])
    total(1)
    finish(2)
    total(0)
    eg_ref[:, :quarter_w] = eo[nz - 1, 0, :, :quarter_w]
    finish(3)
    ps_c.wait_recv()
    eg_ref[:, second] = eo[nz - 1, 0, :, second] + pr[:, :quarter_w].astype(F32)
    eg_ref[:, hi_cols] = eo[nz - 1, 1] + pr[:, quarter_w:].astype(F32)

    for i in range(3):
        relay(i, own(0), z, 0, line(1 - zm)).wait_send()
        for k in range(nz - 1):
            onward(k, i).wait_send()

        @pl.when(mid)
        def _():
            relay(i, own(0), z, nz, line(2)).wait_send()
            for n in range(1, nz):
                relay(i, own(0), z, n, line(0)).wait_send()

    for copy in sent:
        copy.wait_send()


def settle(ig_ref, eg_ref, ig_hbm, eg_hbm, done):
    copies = [pltpu.make_async_copy(ig_ref, ig_hbm, done.at[0]), pltpu.make_async_copy(eg_ref, eg_hbm, done.at[1])]
    for copy in copies:
        copy.start()
    for copy in copies:
        copy.wait()


def fused(inputs, out_grad, coeff_fixed, atom_counts, experts, nz):
    n_sys, n_slots, width = inputs.shape
    n_exp, rows, _ = experts.shape
    sr, er_rows = n_sys * rows, n_exp * rows
    half_w, quarter_w = width // 2, width // 4
    most_w = width - quarter_w
    vmem = pl.BlockSpec(memory_space=pltpu.VMEM)
    hbm = pl.BlockSpec(memory_space=pltpu.HBM)
    dma = pltpu.SemaphoreType.DMA
    in_grad, expert_grad = pl.pallas_call(
        functools.partial(kernel, nz, n_sys, n_exp, rows, width),
        out_shape=(
            pltpu.VMEM(inputs.shape, BF16),
            pltpu.VMEM((er_rows, width), F32),
        ),
        in_specs=[hbm] * 5,
        out_specs=(vmem, vmem),
        scratch_shapes=[
            pltpu.SMEM(atom_counts.shape, jnp.int32),
            pltpu.SMEM(coeff_fixed.shape, jnp.int32),
            pltpu.VMEM(inputs.shape, BF16),
            pltpu.VMEM((er_rows, width), BF16),
            pltpu.VMEM(out_grad.shape, BF16),
            pltpu.VMEM((2, 16, 128), BF16),
            pltpu.VMEM((8, 2, 16, 128), BF16),
            pltpu.VMEM((2, 8 * sr, er_rows), BF16),
            pltpu.VMEM((2, er_rows, 8 * sr), BF16),
            pltpu.VMEM((2, 4 * sr, er_rows), BF16),
            pltpu.VMEM((2, er_rows, 4 * sr), BF16),
            pltpu.VMEM((8, nz, sr, half_w), BF16),
            pltpu.VMEM((nz, 8, sr, half_w), BF16),
            pltpu.VMEM((nz, 8, sr, most_w), BF16),
            pltpu.VMEM((nz, 2, 4, sr, most_w), BF16),
            pltpu.VMEM((nz, 3, er_rows, half_w), F32),
            pltpu.VMEM((er_rows, quarter_w), F32),
            pltpu.VMEM((nz - 1, 3, er_rows, half_w), BF16),
            pltpu.VMEM((nz + 1, 3, er_rows, half_w), BF16),
            pltpu.VMEM((2, er_rows, quarter_w), BF16),
            pltpu.VMEM((3, nz, er_rows, half_w), BF16),
            pltpu.VMEM((2, er_rows, quarter_w), BF16),
            pltpu.VMEM((8, n_sys, nz, rows, half_w), BF16),
            pltpu.VMEM((4, n_sys, nz, 2, rows, most_w), BF16),
            pltpu.VMEM((n_sys, nz, 8, rows, half_w), BF16),
            pltpu.VMEM((n_sys, nz, 4, 2, rows, most_w), BF16),
            pltpu.VMEM((er_rows, most_w), BF16),
            pltpu.VMEM((er_rows, most_w), BF16),
            dma((3 + 2 * n_sys,)), dma((1 + 4 * nz,)),
            dma((7,)), dma((7,)), dma((4,)), dma((4,)), dma((3, nz + 1)), dma((3, nz)),
            dma((nz // 2, 7)), dma((nz // 2, 7)), dma((nz, 3)), dma((nz, 3)),
            dma((nz - 1, 3)), dma((nz + 1, 3)),
            dma((nz, 7)), dma((nz, 7)), dma((nz, 3)), dma((nz, 3)), dma((1,)), dma((1,)),
        ],
        compiler_params=pltpu.CompilerParams(
            collective_id=0, has_side_effects=True, vmem_limit_bytes=48 * 1024 * 1024),
    )(*(
        pltpu.with_memory_space_constraint(a, pltpu.HBM)
        for a in (atom_counts, coeff_fixed, inputs, out_grad, experts.reshape(er_rows, width))))
    held = [pltpu.with_memory_space_constraint(a, pltpu.VMEM) for a in (in_grad, expert_grad)]
    in_grad, expert_grad = pl.pallas_call(
        settle,
        out_shape=(
            jax.ShapeDtypeStruct(inputs.shape, BF16),
            jax.ShapeDtypeStruct((er_rows, width), F32),
        ),
        in_specs=[vmem, vmem],
        out_specs=(hbm, hbm),
        scratch_shapes=[dma((2,))],
        compiler_params=pltpu.CompilerParams(vmem_limit_bytes=16 * 1024 * 1024),
    )(*held)
    return in_grad, expert_grad.reshape(n_exp, rows, width)


def plain(inputs, out_grad, coeff_fixed, atom_counts, experts):
    both = ("dp", "fsdp")
    n_sys, n_slots, width = inputs.shape
    n_exp, rows, _ = experts.shape
    coeffs = lax.all_gather(coeff_fixed, both, axis=0, tiled=True).astype(F32) / 4096.0
    valid = lax.broadcasted_iota(jnp.int32, (n_sys, n_slots), 1) < atom_counts[:, None]
    masked = jnp.where(valid[:, :, None], out_grad, jnp.zeros_like(out_grad))
    merged = jnp.einsum("se,eij->sij", coeffs, experts.astype(F32), precision=HIGH).astype(BF16)
    merged = lax.all_to_all(merged, both, split_axis=0, concat_axis=1, tiled=True)
    per_system = jnp.einsum("smi,smj->sij", inputs, masked, preferred_element_type=F32)
    per_system = lax.all_to_all(per_system, both, split_axis=1, concat_axis=0, tiled=True)
    expert_grad = jnp.einsum("se,sij->eij", coeffs, per_system, precision=HIGH)
    in_grad = jnp.einsum("smj,sij->smi", masked, merged, preferred_element_type=F32).astype(BF16)
    return in_grad, expert_grad


def solution(mesh):
    n_dp, n_fsdp = mesh.shape["dp"], mesh.shape["fsdp"]

    def shards(inputs, out_grad, coeff_fixed, atom_counts, experts):
        n_sys, _, width = inputs.shape
        n_exp, rows, _ = experts.shape
        if n_dp == 16 and n_fsdp == 2 and rows % 16 == 0 and n_sys <= 16 and n_exp <= 128 and width % 512 == 0:
            return fused(inputs, out_grad, coeff_fixed, atom_counts, experts, n_dp // 4)
        return plain(inputs, out_grad, coeff_fixed, atom_counts, experts)

    placed = (
        P(("dp", "fsdp"), None, None),
        P(("dp", "fsdp"), None, None),
        P(("dp", "fsdp"), None),
        P(("dp", "fsdp")),
        P(None, ("dp", "fsdp"), None),
    )
    return jax.shard_map(
        shards,
        mesh=mesh,
        in_specs=placed,
        out_specs=(P(("dp", "fsdp"), None, None), P(None, ("dp", "fsdp"), None)),
        check_vma=False,
    )
```

```python
import functools

import jax
import jax.numpy as jnp
from jax import lax
from jax.experimental import pallas as pl
from jax.experimental.pallas import tpu as pltpu
from jax.sharding import PartitionSpec as P

HIGH = lax.Precision.HIGHEST
MESH = pl.DeviceIdType.MESH
BF16 = jnp.bfloat16
F32 = jnp.float32
NEAR_ORDER = (5, 7, 4, 1, 6, 3, 2)


def dot(a, b, ca, cb):
    return lax.dot_general(a, b, (((ca,), (cb,)), ((), ())), preferred_element_type=F32)


def kernel(nz, n_sys, n_exp, rows, width,
           counts_hbm, co_hbm, in_hbm, og_hbm, ex_hbm,
           ig_ref, eg_ref,
           counts_ref, co_ref, in_ref, ex_ref, mk, cl, ca, ka, kt, kp, kq, pb, g, pc, gc, eo, ec, zs, zr, zc, xg, xq, mb, mc, mr, mq, ps, pr,
           ld, loc, ka_s, ka_r, xp_s, xp_r, xz_s, xz_r, pb_s, pb_r, pc_s, pc_r, zs_s, zs_r,
           mb_s, mb_r, mc_s, mc_r, ps_s, ps_r):
    dp = lax.axis_index("dp")
    y = lax.axis_index("fsdp")
    z = dp // 4
    x = lax.rem(dp // 2, 2)
    c = lax.rem(dp, 2)
    me = x * 4 + c * 2 + y
    sr = n_sys * rows
    half_w, quarter_w = width // 2, width // 4
    span = 8 * rows
    lo_cols, hi_cols = pl.ds(0, half_w), pl.ds(half_w, half_w)
    second = slice(quarter_w, half_w)

    def cut(near_z):
        return quarter_w if near_z else half_w

    def rest(near_z):
        return slice(cut(near_z) - quarter_w, width - quarter_w)

    def flip(v, d):
        return lax.rem(v + d, 2)

    def place(fx, fc, fy):
        xx, cc, yy = flip(x, fx), flip(c, fc), flip(y, fy)
        return xx * 4 + cc * 2 + yy, ((z * 2 + xx) * 2 + cc, yy)

    def near(j):
        return place(j // 4, j // 2 % 2, j % 2)

    def turned(fp, fq, fc):
        return place(fp * (1 - c) + fq * c, fc, fq * (1 - c) + fp * c)

    p_at = x * (1 - c) + y * c
    q_at = y * (1 - c) + x * c

    half = z // 2
    zm = z + half * (3 - 2 * z)
    mid = zm == 1

    def actual(v):
        return v + half * (3 - 2 * v)

    def line(v):
        return (actual(v) * 2 + x) * 2 + c, y

    def arrival(n):
        return actual((zm, 1 - zm, 2, 3)[n])

    def target(n):
        return actual((3, 2, 1 - zm, zm)[n])

    plane = NEAR_ORDER
    peers = [near(j)[1] for j in plane] + [line(1 - zm)]
    barrier = pltpu.get_barrier_semaphore()
    for peer in peers:
        pl.semaphore_signal(barrier, inc=1, device_id=peer, device_id_type=MESH)

    @pl.when(mid)
    def _():
        pl.semaphore_signal(barrier, inc=1, device_id=line(2), device_id_type=MESH)

    def load(n, src, dst):
        copy = pltpu.make_async_copy(src, dst, ld.at[n])
        copy.start()
        return copy

    co_c = load(1 + 2 * n_sys, co_hbm, co_ref)
    counts_c = load(2 + 2 * n_sys, counts_hbm, counts_ref)
    ex_c = load(0, ex_hbm, ex_ref)
    og_c = [load(1 + s, og_hbm.at[s], mk.at[s]) for s in range(n_sys)]
    in_c = [load(1 + n_sys + s, in_hbm.at[s], in_ref.at[s]) for s in range(n_sys)]

    ex_c.wait()
    pl.semaphore_wait(barrier, len(peers) + zm)

    def remote(src, dst, s, r, peer):
        return pltpu.make_async_remote_copy(
            src_ref=src, dst_ref=dst, send_sem=s, recv_sem=r, device_id=peer, device_id_type=MESH
        )

    sent = []

    def send(src, dst, s, r, peer):
        copy = remote(src, dst, s, r, peer)
        copy.start()
        sent.append(copy)
        return copy

    n_loc = [0]

    def local(src, dst):
        copy = pltpu.make_async_copy(src, dst, loc.at[n_loc[0]])
        n_loc[0] += 1
        copy.start()
        return copy

    def own(i):
        return ex_ref.at[:, (lo_cols, hi_cols)[i]] if i < 2 else xg.at[2, z]

    def relay(i, src, block, n, to):
        return remote(src, xg.at[i, block], xz_s.at[i, n], xz_r.at[i, block], to)

    def offer(i):
        relay(i, own(i), z, 0, line(1 - zm)).start()

        @pl.when(mid)
        def _():
            relay(i, own(i), z, nz, line(2)).start()

    xp = send(own(1), xg.at[2, z], xp_s.at[0], xp_r.at[0], turned(1, 0, 0)[1])
    offer(0)
    offer(1)
    xq_c = send(ex_ref.at[:, second], xq.at[0], xp_s.at[1], xp_r.at[1], turned(1, 0, 0)[1])
    col = lax.broadcasted_iota(jnp.int32, cl.shape[1:], 1)
    row = lax.broadcasted_iota(jnp.int32, cl.shape[1:], 0)
    fixed = jnp.zeros(cl.shape[1:], jnp.int32)
    co_c.wait()
    counts_c.wait()
    for s in range(n_sys):
        for e in range(n_exp):
            fixed = jnp.where((row == s) & (col == e), co_ref[s, e], fixed)
    cl[0] = ((fixed >> 6).astype(F32) / 64.0).astype(BF16)
    cl[1] = ((fixed & 63).astype(F32) / 4096.0).astype(BF16)
    ca_c = [send(cl, ca.at[me], ka_s.at[j - 1], ka_r.at[j - 1], near(j)[1]) for j in plane]
    ca_own = local(cl, ca.at[me])

    for s in range(n_sys):
        og_c[s].wait()
        slot = lax.broadcasted_iota(jnp.int32, mk.shape[1:], 0)
        mk[s] = jnp.where(slot < counts_ref[s], mk[s], jnp.zeros(mk.shape[1:], BF16))
    for copy in in_c:
        copy.wait()

    pb_c, g_own, pc_c, gc_own = {}, {}, {}, {}
    takers = ((0, 0, 0), (0, 0, 1), (0, 1, 0), (1, 0, 1))

    def seat(b):
        fx, fc, fy = flip(x, b // 4), flip(c, b // 2 % 2), flip(y, b % 2)
        fp, fq = fx * (1 - c) + fy * c, fy * (1 - c) + fx * c
        return (1 - fc) * (4 * fq + fp) + fc * (2 + 4 * fp + fq)

    def produce(k):
        lanes = pl.ds(pl.multiple_of(target(k) * span, span), span)
        n, others = cut(k >= 2), rest(k >= 2)
        for s in range(n_sys):
            prod = dot(in_ref[s, :, lanes], mk[s], 0, 0).astype(BF16)
            for b in range(8):
                pb[b, k, s * rows:(s + 1) * rows, :n] = prod[b * rows:(b + 1) * rows, :n]
                pc[k, seat(b), s * rows:(s + 1) * rows, others] = prod[b * rows:(b + 1) * rows, n:]
        for v in (2, 3, 1):
            at = (p_at if v % 2 else q_at) * 2 + c
            pc_c[k, v] = send(pc.at[k, 2 * v:2 * v + 2, :, others], gc.at[k, :, at, :, others], pc_s.at[k, v - 1], pc_r.at[k, v - 1],
                              turned(*takers[v])[1])
        gc_own[k] = local(pc.at[k, 0:2, :, others], gc.at[k, :, q_at * 2 + c, :, others])

    def deal(h):
        two, n = slice(2 * h, 2 * h + 2), cut(h == 1)
        for j in plane:
            to, peer = near(j)
            pb_c[h, j] = send(pb.at[to, two, :, :n], g.at[two, me, :, :n], pb_s.at[h, j - 1], pb_r.at[h, j - 1], peer)
        g_own[h] = local(pb.at[me, two, :, :n], g.at[two, me, :, :n])

    mb_c, m_own, mc_c, mc_own = {}, {}, {}, {}

    def held(k, i):
        return ex_ref[:, (lo_cols, hi_cols)[i]] if k == 0 and i < 2 else xg[i, arrival(k)]

    def mixed(weights, block):
        return (dot(weights[0], block, 1, 0) + dot(weights[1], block, 1, 0)).astype(BF16)

    def merge(*ks):
        span_k = slice(ks[0], ks[-1] + 1)
        close = ks[0] < 2
        n, others = cut(close), rest(close)
        for k in ks:
            for i in (1, 2):
                to = flip(p_at, i - 1)
                mc[:, :, k, to, :, quarter_w:] = mixed(kp, held(k, i)).reshape(4, n_sys, rows, half_w)
                if close:
                    piece = xq[k] if i == 2 else held(k, 0)[:, second]
                    mc[:, :, k, to, :, :quarter_w] = mixed(kp, piece).reshape(4, n_sys, rows, quarter_w)
        k = ks[-1]
        at = 2 * c + q_at
        for v, (fq, fc) in ((2, (1, 0)), (3, (1, 1)), (1, (0, 1))):
            u = flip(q_at, fq) * 2 + flip(c, fc)
            mc_c[k, v] = send(mc.at[u, :, span_k, :, :, others], mq.at[:, span_k, at, :, :, others],
                              mc_s.at[k, v - 1], mc_r.at[k, v - 1], turned(0, fq, fc)[1])
        mc_own[k] = local(mc.at[q_at * 2 + c, :, span_k, :, :, others], mq.at[:, span_k, at, :, :, others])
        for k in ks:
            mb[:, :, k, :, :n] = mixed(ka, held(k, 0)[:, :n]).reshape(8, n_sys, rows, n)
        for j in plane:
            to, peer = near(j)
            mb_c[k, j] = send(mb.at[to, :, span_k, :, :n], mr.at[:, span_k, me, :, :n],
                              mb_s.at[k, j - 1], mb_r.at[k, j - 1], peer)
        m_own[k] = local(mb.at[me, :, span_k, :, :n], mr.at[:, span_k, me, :, :n])

    def landed(slot, i):
        remote(zs.at[0, i], zr.at[slot, i], zs_s.at[0, i], zs_r.at[slot, i], line(1 - zm)).wait_recv()
        return zr[slot, i].astype(F32)

    zc_c = []

    def reduce(k):
        gc_own[k].wait()
        for v in (1, 2, 3):
            pc_c[k, v].wait_recv()
        for i in (1, 0):
            block = gc[k, i, :, :, quarter_w:].reshape(4 * sr, half_w)
            eo[k, i + 1] = dot(kq[0], block, 1, 0) + dot(kq[1], block, 1, 0)
            begin(k, i + 1)
            if k >= 2:
                block = gc[k, i, :, :, :quarter_w].reshape(4 * sr, quarter_w)
                part = dot(kq[0], block, 1, 0) + dot(kq[1], block, 1, 0)
                if i == 0:
                    eo[k, 0, :, second] = part
                elif k == 2:
                    zc[0] = part.astype(BF16)
                    zc_c.append(send(zc.at[0], zc.at[1], xp_s.at[3], xp_r.at[3], line(1 - zm)))
                else:
                    ec[...] = part
        if k % 2 == 0:
            g_own[k // 2].wait()
            for j in plane:
                pb_c[k // 2, j].wait_recv()
        n = cut(k >= 2)
        block = g[k, :, :, :n].reshape(8 * sr, n)
        eo[k, 0, :, :n] = dot(kt[0], block, 1, 0) + dot(kt[1], block, 1, 0)
        begin(k, 0)

    def onward(k, i):
        slot = (2 * zm, 1 + 3 * zm, 3)[k]
        return remote(zs.at[k, i], zr.at[slot, i], zs_s.at[k, i], zs_r.at[slot, i],
                      line((zm + 1, zm + 1, 1 - zm)[k]))

    def begin(k, i):
        if k < nz - 1:
            @pl.when(zm == 0)
            def _():
                zs[k, i] = eo[k, i].astype(BF16)
                onward(k, i).start()

    def proceed(k, i):
        @pl.when(mid)
        def _():
            zs[k, i] = (eo[k, i] + landed(k, i)).astype(BF16)
            onward(k, i).start()

    def finish(k):
        if k in m_own:
            m_own[k].wait()
            mc_own[k].wait()
            for j in plane:
                mb_c[k, j].wait_recv()
            for v in (1, 2, 3):
                mc_c[k, v].wait_recv()
        lanes = pl.ds(pl.multiple_of(arrival(k) * span, span), span)
        for s in range(n_sys):
            first = mr[s, k, :, :, :cut(k < 2)].reshape(span, cut(k < 2))
            last = jnp.concatenate(
                [mq[s, k, (b % 2, 2 + b // 4)[b // 2 % 2], (b // 4, b % 2)[b // 2 % 2], :, rest(k < 2)]
                 for b in range(8)], axis=0)
            ig_ref[s, :, lanes] = dot(mk[s], jnp.concatenate([first, last], axis=1), 1, 1).astype(BF16)

    def came(n, i):
        block = arrival(n)
        relay(i, own(0), block, n, line(1 - zm)).wait_recv()

    def handed(n, i):
        block = arrival(n)

        @pl.when(mid)
        def _():
            came(n, i)
            relay(i, xg.at[i, block], block, n, line(2 if n == 1 else 0)).start()

    def awaited(n):
        @pl.when(zm == 0)
        def _():
            for i in range(3):
                came(n, i)

    produce(0)
    xp.wait_recv()
    offer(2)
    produce(1)
    deal(0)
    produce(2)
    produce(3)
    deal(1)
    xq_c.wait_recv()
    xq_n = send(xq.at[0], xq.at[1], xp_s.at[2], xp_r.at[2], line(1 - zm))

    ca_own.wait()
    for copy in ca_c:
        copy.wait_recv()
    er_rows = n_exp * rows
    lane = lax.broadcasted_iota(jnp.int32, (cl.shape[2], er_rows), 1)
    first = lax.broadcasted_iota(jnp.int32, (cl.shape[2], er_rows), 0) * rows
    pick = jnp.where((lane >= first) & (lane < first + rows), 1.0, 0.0).astype(BF16)
    wide = dot(ca[...].reshape(16 * cl.shape[1], cl.shape[2]), pick, 1, 0)
    across = lax.broadcasted_iota(jnp.int32, (rows, er_rows), 1) % rows
    diagonal = across == lax.broadcasted_iota(jnp.int32, (rows, er_rows), 0)
    for d in range(8):
        for h in range(2):
            for s in range(n_sys):
                at = (d * 2 + h) * cl.shape[1] + s
                value = jnp.broadcast_to(wide[at:at + 1, :], (rows, er_rows))
                spot = (d * n_sys + s) * rows
                ka[h, spot:spot + rows, :] = jnp.where(diagonal, value, 0.0).astype(BF16)
    for h in range(2):
        for u in range(4):
            uq, uc = u // 2, u % 2
            at = (x * (1 - c) + uq * c) * 4 + uc * 2 + uq * (1 - c) + y * c
            kp[h, u * sr:(u + 1) * sr, :] = ka[h, pl.ds(pl.multiple_of(at * sr, sr), sr), :]
    for h in range(2):
        kt[h] = ka[h].T
        kq[h] = kp[h].T

    for i in range(2):
        handed(1, i)
        handed(2, i)
    reduce(0)
    handed(1, 2)
    handed(2, 2)
    reduce(1)
    awaited(1)
    xq_n.wait_recv()
    merge(0, 1)
    handed(3, 0)
    proceed(0, 2)
    handed(3, 1)
    proceed(0, 1)
    reduce(2)
    handed(3, 2)
    proceed(0, 0)
    awaited(2)
    merge(2)
    reduce(3)
    awaited(3)
    merge(3)
    for i in (2, 1, 0):
        proceed(1, i)
        proceed(2, i)
    finish(1)
    finish(0)

    def total(i):
        eo[nz - 1, i] += landed(3, i)

        @pl.when(mid)
        def _():
            eo[nz - 1, i] += landed(4, i)

    total(2)
    zc_c[0].wait_recv()
    ps[:, :quarter_w] = (ec[...] + zc[1].astype(F32)).astype(BF16)
    ps[:, quarter_w:] = eo[nz - 1, 2].astype(BF16)
    ps_c = send(ps, pr, ps_s.at[0], ps_r.at[0], turned(1, 0, 0)[1])
    total(1)
    finish(2)
    finish(3)
    total(0)
    eg_ref[:, :quarter_w] = eo[nz - 1, 0, :, :quarter_w]
    ps_c.wait_recv()
    eg_ref[:, second] = eo[nz - 1, 0, :, second] + pr[:, :quarter_w].astype(F32)
    eg_ref[:, hi_cols] = eo[nz - 1, 1] + pr[:, quarter_w:].astype(F32)

    for i in range(3):
        relay(i, own(0), z, 0, line(1 - zm)).wait_send()
        for k in range(nz - 1):
            onward(k, i).wait_send()

        @pl.when(mid)
        def _():
            relay(i, own(0), z, nz, line(2)).wait_send()
            for n in range(1, nz):
                relay(i, own(0), z, n, line(0)).wait_send()

    for copy in sent:
        copy.wait_send()


def settle(ig_ref, eg_ref, ig_hbm, eg_hbm, done):
    copies = [pltpu.make_async_copy(ig_ref, ig_hbm, done.at[0]), pltpu.make_async_copy(eg_ref, eg_hbm, done.at[1])]
    for copy in copies:
        copy.start()
    for copy in copies:
        copy.wait()


def fused(inputs, out_grad, coeff_fixed, atom_counts, experts, nz):
    n_sys, n_slots, width = inputs.shape
    n_exp, rows, _ = experts.shape
    sr, er_rows = n_sys * rows, n_exp * rows
    half_w, quarter_w = width // 2, width // 4
    most_w = width - quarter_w
    vmem = pl.BlockSpec(memory_space=pltpu.VMEM)
    hbm = pl.BlockSpec(memory_space=pltpu.HBM)
    dma = pltpu.SemaphoreType.DMA
    in_grad, expert_grad = pl.pallas_call(
        functools.partial(kernel, nz, n_sys, n_exp, rows, width),
        out_shape=(
            pltpu.VMEM(inputs.shape, BF16),
            pltpu.VMEM((er_rows, width), F32),
        ),
        in_specs=[hbm] * 5,
        out_specs=(vmem, vmem),
        scratch_shapes=[
            pltpu.SMEM(atom_counts.shape, jnp.int32),
            pltpu.SMEM(coeff_fixed.shape, jnp.int32),
            pltpu.VMEM(inputs.shape, BF16),
            pltpu.VMEM((er_rows, width), BF16),
            pltpu.VMEM(out_grad.shape, BF16),
            pltpu.VMEM((2, 16, 128), BF16),
            pltpu.VMEM((8, 2, 16, 128), BF16),
            pltpu.VMEM((2, 8 * sr, er_rows), BF16),
            pltpu.VMEM((2, er_rows, 8 * sr), BF16),
            pltpu.VMEM((2, 4 * sr, er_rows), BF16),
            pltpu.VMEM((2, er_rows, 4 * sr), BF16),
            pltpu.VMEM((8, nz, sr, half_w), BF16),
            pltpu.VMEM((nz, 8, sr, half_w), BF16),
            pltpu.VMEM((nz, 8, sr, most_w), BF16),
            pltpu.VMEM((nz, 2, 4, sr, most_w), BF16),
            pltpu.VMEM((nz, 3, er_rows, half_w), F32),
            pltpu.VMEM((er_rows, quarter_w), F32),
            pltpu.VMEM((nz - 1, 3, er_rows, half_w), BF16),
            pltpu.VMEM((nz + 1, 3, er_rows, half_w), BF16),
            pltpu.VMEM((2, er_rows, quarter_w), BF16),
            pltpu.VMEM((3, nz, er_rows, half_w), BF16),
            pltpu.VMEM((2, er_rows, quarter_w), BF16),
            pltpu.VMEM((8, n_sys, nz, rows, half_w), BF16),
            pltpu.VMEM((4, n_sys, nz, 2, rows, most_w), BF16),
            pltpu.VMEM((n_sys, nz, 8, rows, half_w), BF16),
            pltpu.VMEM((n_sys, nz, 4, 2, rows, most_w), BF16),
            pltpu.VMEM((er_rows, most_w), BF16),
            pltpu.VMEM((er_rows, most_w), BF16),
            dma((3 + 2 * n_sys,)), dma((1 + 4 * nz,)),
            dma((7,)), dma((7,)), dma((4,)), dma((4,)), dma((3, nz + 1)), dma((3, nz)),
            dma((nz // 2, 7)), dma((nz // 2, 7)), dma((nz, 3)), dma((nz, 3)),
            dma((nz - 1, 3)), dma((nz + 1, 3)),
            dma((nz, 7)), dma((nz, 7)), dma((nz, 3)), dma((nz, 3)), dma((1,)), dma((1,)),
        ],
        compiler_params=pltpu.CompilerParams(
            collective_id=0, has_side_effects=True, vmem_limit_bytes=48 * 1024 * 1024),
    )(*(
        pltpu.with_memory_space_constraint(a, pltpu.HBM)
        for a in (atom_counts, coeff_fixed, inputs, out_grad, experts.reshape(er_rows, width))))
    held = [pltpu.with_memory_space_constraint(a, pltpu.VMEM) for a in (in_grad, expert_grad)]
    in_grad, expert_grad = pl.pallas_call(
        settle,
        out_shape=(
            jax.ShapeDtypeStruct(inputs.shape, BF16),
            jax.ShapeDtypeStruct((er_rows, width), F32),
        ),
        in_specs=[vmem, vmem],
        out_specs=(hbm, hbm),
        scratch_shapes=[dma((2,))],
        compiler_params=pltpu.CompilerParams(vmem_limit_bytes=16 * 1024 * 1024),
    )(*held)
    return in_grad, expert_grad.reshape(n_exp, rows, width)


def plain(inputs, out_grad, coeff_fixed, atom_counts, experts):
    both = ("dp", "fsdp")
    n_sys, n_slots, width = inputs.shape
    n_exp, rows, _ = experts.shape
    coeffs = lax.all_gather(coeff_fixed, both, axis=0, tiled=True).astype(F32) / 4096.0
    valid = lax.broadcasted_iota(jnp.int32, (n_sys, n_slots), 1) < atom_counts[:, None]
    masked = jnp.where(valid[:, :, None], out_grad, jnp.zeros_like(out_grad))
    merged = jnp.einsum("se,eij->sij", coeffs, experts.astype(F32), precision=HIGH).astype(BF16)
    merged = lax.all_to_all(merged, both, split_axis=0, concat_axis=1, tiled=True)
    per_system = jnp.einsum("smi,smj->sij", inputs, masked, preferred_element_type=F32)
    per_system = lax.all_to_all(per_system, both, split_axis=1, concat_axis=0, tiled=True)
    expert_grad = jnp.einsum("se,sij->eij", coeffs, per_system, precision=HIGH)
    in_grad = jnp.einsum("smj,sij->smi", masked, merged, preferred_element_type=F32).astype(BF16)
    return in_grad, expert_grad


def solution(mesh):
    n_dp, n_fsdp = mesh.shape["dp"], mesh.shape["fsdp"]

    def shards(inputs, out_grad, coeff_fixed, atom_counts, experts):
        n_sys, _, width = inputs.shape
        n_exp, rows, _ = experts.shape
        if n_dp == 16 and n_fsdp == 2 and rows % 16 == 0 and n_sys <= 16 and n_exp <= 128 and width % 512 == 0:
            return fused(inputs, out_grad, coeff_fixed, atom_counts, experts, n_dp // 4)
        return plain(inputs, out_grad, coeff_fixed, atom_counts, experts)

    placed = (
        P(("dp", "fsdp"), None, None),
        P(("dp", "fsdp"), None, None),
        P(("dp", "fsdp"), None),
        P(("dp", "fsdp")),
        P(None, ("dp", "fsdp"), None),
    )
    return jax.shard_map(
        shards,
        mesh=mesh,
        in_specs=placed,
        out_specs=(P(("dp", "fsdp"), None, None), P(None, ("dp", "fsdp"), None)),
        check_vma=False,
    )
```

```python
import functools

import jax
import jax.numpy as jnp
from jax import lax
from jax.experimental import pallas as pl
from jax.experimental.pallas import tpu as pltpu
from jax.sharding import PartitionSpec as P

HIGH = lax.Precision.HIGHEST
MESH = pl.DeviceIdType.MESH
BF16 = jnp.bfloat16
F32 = jnp.float32
NEAR_ORDER = (5, 7, 4, 1, 6, 3, 2)


def dot(a, b, ca, cb):
    return lax.dot_general(a, b, (((ca,), (cb,)), ((), ())), preferred_element_type=F32)


def kernel(nz, n_sys, n_exp, rows, width,
           counts_hbm, co_hbm, in_hbm, og_hbm, ex_hbm,
           ig_ref, eg_ref,
           counts_ref, co_ref, in_ref, ex_ref, mk, cl, ca, ka, kt, kp, kq, pb, g, pc, gc, eo, zs, zr, xg, xq, mb, mc, mr, mq, ps, pr,
           ld, loc, ka_s, ka_r, xp_s, xp_r, xz_s, xz_r, pb_s, pb_r, pc_s, pc_r, zs_s, zs_r,
           mb_s, mb_r, mc_s, mc_r, ps_s, ps_r):
    dp = lax.axis_index("dp")
    y = lax.axis_index("fsdp")
    z = dp // 4
    x = lax.rem(dp // 2, 2)
    c = lax.rem(dp, 2)
    me = x * 4 + c * 2 + y
    sr = n_sys * rows
    half_w, quarter_w = width // 2, width // 4
    span = 8 * rows
    lo_cols, hi_cols = pl.ds(0, half_w), pl.ds(half_w, half_w)
    second = slice(quarter_w, half_w)

    def cut(near_z):
        return quarter_w if near_z else half_w

    def rest(near_z):
        return slice(cut(near_z) - quarter_w, width - quarter_w)

    def flip(v, d):
        return lax.rem(v + d, 2)

    def place(fx, fc, fy):
        xx, cc, yy = flip(x, fx), flip(c, fc), flip(y, fy)
        return xx * 4 + cc * 2 + yy, ((z * 2 + xx) * 2 + cc, yy)

    def near(j):
        return place(j // 4, j // 2 % 2, j % 2)

    def turned(fp, fq, fc):
        return place(fp * (1 - c) + fq * c, fc, fq * (1 - c) + fp * c)

    p_at = x * (1 - c) + y * c
    q_at = y * (1 - c) + x * c

    half = z // 2
    zm = z + half * (3 - 2 * z)
    mid = zm == 1

    def actual(v):
        return v + half * (3 - 2 * v)

    def line(v):
        return (actual(v) * 2 + x) * 2 + c, y

    def arrival(n):
        return actual((zm, 1 - zm, 2, 3)[n])

    def target(n):
        return actual((3, 2, 1 - zm, zm)[n])

    plane = NEAR_ORDER
    peers = [near(j)[1] for j in plane] + [line(1 - zm)]
    barrier = pltpu.get_barrier_semaphore()
    for peer in peers:
        pl.semaphore_signal(barrier, inc=1, device_id=peer, device_id_type=MESH)

    @pl.when(mid)
    def _():
        pl.semaphore_signal(barrier, inc=1, device_id=line(2), device_id_type=MESH)

    def load(n, src, dst):
        copy = pltpu.make_async_copy(src, dst, ld.at[n])
        copy.start()
        return copy

    co_c = load(1 + 2 * n_sys, co_hbm, co_ref)
    counts_c = load(2 + 2 * n_sys, counts_hbm, counts_ref)
    ex_c = load(0, ex_hbm, ex_ref)
    og_c = [load(1 + s, og_hbm.at[s], mk.at[s]) for s in range(n_sys)]
    in_c = [load(1 + n_sys + s, in_hbm.at[s], in_ref.at[s]) for s in range(n_sys)]

    ex_c.wait()
    pl.semaphore_wait(barrier, len(peers) + zm)

    def remote(src, dst, s, r, peer):
        return pltpu.make_async_remote_copy(
            src_ref=src, dst_ref=dst, send_sem=s, recv_sem=r, device_id=peer, device_id_type=MESH
        )

    sent = []

    def send(src, dst, s, r, peer):
        copy = remote(src, dst, s, r, peer)
        copy.start()
        sent.append(copy)
        return copy

    n_loc = [0]

    def local(src, dst):
        copy = pltpu.make_async_copy(src, dst, loc.at[n_loc[0]])
        n_loc[0] += 1
        copy.start()
        return copy

    def own(i):
        return ex_ref.at[:, (lo_cols, hi_cols)[i]] if i < 2 else xg.at[2, z]

    def relay(i, src, block, n, to):
        return remote(src, xg.at[i, block], xz_s.at[i, n], xz_r.at[i, block], to)

    def offer(i):
        relay(i, own(i), z, 0, line(1 - zm)).start()

        @pl.when(mid)
        def _():
            relay(i, own(i), z, nz, line(2)).start()

    xp = send(own(1), xg.at[2, z], xp_s.at[0], xp_r.at[0], turned(1, 0, 0)[1])
    offer(0)
    offer(1)
    xq_c = send(ex_ref.at[:, second], xq.at[0], xp_s.at[1], xp_r.at[1], turned(1, 0, 0)[1])
    col = lax.broadcasted_iota(jnp.int32, cl.shape[1:], 1)
    row = lax.broadcasted_iota(jnp.int32, cl.shape[1:], 0)
    fixed = jnp.zeros(cl.shape[1:], jnp.int32)
    co_c.wait()
    counts_c.wait()
    for s in range(n_sys):
        for e in range(n_exp):
            fixed = jnp.where((row == s) & (col == e), co_ref[s, e], fixed)
    cl[0] = ((fixed >> 6).astype(F32) / 64.0).astype(BF16)
    cl[1] = ((fixed & 63).astype(F32) / 4096.0).astype(BF16)
    ca_c = [send(cl, ca.at[me], ka_s.at[j - 1], ka_r.at[j - 1], near(j)[1]) for j in plane]
    ca_own = local(cl, ca.at[me])

    for s in range(n_sys):
        og_c[s].wait()
        slot = lax.broadcasted_iota(jnp.int32, mk.shape[1:], 0)
        mk[s] = jnp.where(slot < counts_ref[s], mk[s], jnp.zeros(mk.shape[1:], BF16))
    for copy in in_c:
        copy.wait()

    pb_c, g_own, pc_c, gc_own = {}, {}, {}, {}
    takers = ((0, 0, 0), (0, 0, 1), (0, 1, 0), (1, 0, 1))

    def seat(b):
        fx, fc, fy = flip(x, b // 4), flip(c, b // 2 % 2), flip(y, b % 2)
        fp, fq = fx * (1 - c) + fy * c, fy * (1 - c) + fx * c
        return (1 - fc) * (4 * fq + fp) + fc * (2 + 4 * fp + fq)

    def produce(k):
        lanes = pl.ds(pl.multiple_of(target(k) * span, span), span)
        n = half_w
        for s in range(n_sys):
            prod = dot(in_ref[s, :, lanes], mk[s], 0, 0).astype(BF16)
            for b in range(8):
                pb[b, k, s * rows:(s + 1) * rows, :] = prod[b * rows:(b + 1) * rows, :n]
                pc[k, seat(b), s * rows:(s + 1) * rows, :] = prod[b * rows:(b + 1) * rows, n:]
        for v in (2, 3, 1):
            at = (p_at if v % 2 else q_at) * 2 + c
            pc_c[k, v] = send(pc.at[k, 2 * v:2 * v + 2], gc.at[k, :, at], pc_s.at[k, v - 1], pc_r.at[k, v - 1],
                              turned(*takers[v])[1])
        gc_own[k] = local(pc.at[k, 0:2], gc.at[k, :, q_at * 2 + c])

    def deal(h):
        two = slice(2 * h, 2 * h + 2)
        for j in plane:
            to, peer = near(j)
            pb_c[h, j] = send(pb.at[to, two], g.at[two, me], pb_s.at[h, j - 1], pb_r.at[h, j - 1], peer)
        g_own[h] = local(pb.at[me, two], g.at[two, me])

    mb_c, m_own, mc_c, mc_own = {}, {}, {}, {}

    def held(k, i):
        return ex_ref[:, (lo_cols, hi_cols)[i]] if k == 0 and i < 2 else xg[i, arrival(k)]

    def mixed(weights, block):
        return (dot(weights[0], block, 1, 0) + dot(weights[1], block, 1, 0)).astype(BF16)

    def merge(*ks):
        span_k = slice(ks[0], ks[-1] + 1)
        close = ks[0] < 2
        n, others = cut(close), rest(close)
        for k in ks:
            for i in (1, 2):
                to = flip(p_at, i - 1)
                mc[:, :, k, to, :, quarter_w:] = mixed(kp, held(k, i)).reshape(4, n_sys, rows, half_w)
                if close:
                    piece = xq[k] if i == 2 else held(k, 0)[:, second]
                    mc[:, :, k, to, :, :quarter_w] = mixed(kp, piece).reshape(4, n_sys, rows, quarter_w)
        k = ks[-1]
        at = 2 * c + q_at
        for v, (fq, fc) in ((2, (1, 0)), (3, (1, 1)), (1, (0, 1))):
            u = flip(q_at, fq) * 2 + flip(c, fc)
            mc_c[k, v] = send(mc.at[u, :, span_k, :, :, others], mq.at[:, span_k, at, :, :, others],
                              mc_s.at[k, v - 1], mc_r.at[k, v - 1], turned(0, fq, fc)[1])
        mc_own[k] = local(mc.at[q_at * 2 + c, :, span_k, :, :, others], mq.at[:, span_k, at, :, :, others])
        for k in ks:
            mb[:, :, k, :, :n] = mixed(ka, held(k, 0)[:, :n]).reshape(8, n_sys, rows, n)
        for j in plane:
            to, peer = near(j)
            mb_c[k, j] = send(mb.at[to, :, span_k, :, :n], mr.at[:, span_k, me, :, :n],
                              mb_s.at[k, j - 1], mb_r.at[k, j - 1], peer)
        m_own[k] = local(mb.at[me, :, span_k, :, :n], mr.at[:, span_k, me, :, :n])

    def landed(slot, i):
        remote(zs.at[0, i], zr.at[slot, i], zs_s.at[0, i], zs_r.at[slot, i], line(1 - zm)).wait_recv()
        return zr[slot, i].astype(F32)

    def reduce(k):
        gc_own[k].wait()
        for v in (1, 2, 3):
            pc_c[k, v].wait_recv()
        for i in (1, 0):
            block = gc[k, i].reshape(4 * sr, half_w)
            eo[k, i + 1] = dot(kq[0], block, 1, 0) + dot(kq[1], block, 1, 0)
            begin(k, i + 1)
        if k % 2 == 0:
            g_own[k // 2].wait()
            for j in plane:
                pb_c[k // 2, j].wait_recv()
        block = g[k].reshape(8 * sr, half_w)
        eo[k, 0] = dot(kt[0], block, 1, 0) + dot(kt[1], block, 1, 0)
        begin(k, 0)

    def onward(k, i):
        slot = (2 * zm, 1 + 3 * zm, 3)[k]
        return remote(zs.at[k, i], zr.at[slot, i], zs_s.at[k, i], zs_r.at[slot, i],
                      line((zm + 1, zm + 1, 1 - zm)[k]))

    def begin(k, i):
        if k < nz - 1:
            @pl.when(zm == 0)
            def _():
                zs[k, i] = eo[k, i].astype(BF16)
                onward(k, i).start()

    def proceed(k, i):
        @pl.when(mid)
        def _():
            zs[k, i] = (eo[k, i] + landed(k, i)).astype(BF16)
            onward(k, i).start()

    def finish(k):
        if k in m_own:
            m_own[k].wait()
            mc_own[k].wait()
            for j in plane:
                mb_c[k, j].wait_recv()
            for v in (1, 2, 3):
                mc_c[k, v].wait_recv()
        lanes = pl.ds(pl.multiple_of(arrival(k) * span, span), span)
        for s in range(n_sys):
            first = mr[s, k, :, :, :cut(k < 2)].reshape(span, cut(k < 2))
            last = jnp.concatenate(
                [mq[s, k, (b % 2, 2 + b // 4)[b // 2 % 2], (b // 4, b % 2)[b // 2 % 2], :, rest(k < 2)]
                 for b in range(8)], axis=0)
            ig_ref[s, :, lanes] = dot(mk[s], jnp.concatenate([first, last], axis=1), 1, 1).astype(BF16)

    def came(n, i):
        block = arrival(n)
        relay(i, own(0), block, n, line(1 - zm)).wait_recv()

    def handed(n, i):
        block = arrival(n)

        @pl.when(mid)
        def _():
            came(n, i)
            relay(i, xg.at[i, block], block, n, line(2 if n == 1 else 0)).start()

    def awaited(n):
        @pl.when(zm == 0)
        def _():
            for i in range(3):
                came(n, i)

    produce(0)
    xp.wait_recv()
    offer(2)
    produce(1)
    deal(0)
    produce(2)
    produce(3)
    deal(1)
    xq_c.wait_recv()
    xq_n = send(xq.at[0], xq.at[1], xp_s.at[2], xp_r.at[2], line(1 - zm))

    ca_own.wait()
    for copy in ca_c:
        copy.wait_recv()
    er_rows = n_exp * rows
    lane = lax.broadcasted_iota(jnp.int32, (cl.shape[2], er_rows), 1)
    first = lax.broadcasted_iota(jnp.int32, (cl.shape[2], er_rows), 0) * rows
    pick = jnp.where((lane >= first) & (lane < first + rows), 1.0, 0.0).astype(BF16)
    wide = dot(ca[...].reshape(16 * cl.shape[1], cl.shape[2]), pick, 1, 0)
    across = lax.broadcasted_iota(jnp.int32, (rows, er_rows), 1) % rows
    diagonal = across == lax.broadcasted_iota(jnp.int32, (rows, er_rows), 0)
    for d in range(8):
        for h in range(2):
            for s in range(n_sys):
                at = (d * 2 + h) * cl.shape[1] + s
                value = jnp.broadcast_to(wide[at:at + 1, :], (rows, er_rows))
                spot = (d * n_sys + s) * rows
                ka[h, spot:spot + rows, :] = jnp.where(diagonal, value, 0.0).astype(BF16)
    for h in range(2):
        for u in range(4):
            uq, uc = u // 2, u % 2
            at = (x * (1 - c) + uq * c) * 4 + uc * 2 + uq * (1 - c) + y * c
            kp[h, u * sr:(u + 1) * sr, :] = ka[h, pl.ds(pl.multiple_of(at * sr, sr), sr), :]
    for h in range(2):
        kt[h] = ka[h].T
        kq[h] = kp[h].T

    for i in range(2):
        handed(1, i)
        handed(2, i)
    reduce(0)
    handed(1, 2)
    handed(2, 2)
    reduce(1)
    awaited(1)
    xq_n.wait_recv()
    merge(0, 1)
    handed(3, 0)
    proceed(0, 2)
    handed(3, 1)
    proceed(0, 1)
    reduce(2)
    handed(3, 2)
    proceed(0, 0)
    awaited(2)
    merge(2)
    reduce(3)
    awaited(3)
    merge(3)
    for i in (2, 1, 0):
        proceed(1, i)
        proceed(2, i)
    finish(1)
    finish(0)

    def total(i):
        eo[nz - 1, i] += landed(3, i)

        @pl.when(mid)
        def _():
            eo[nz - 1, i] += landed(4, i)

    total(2)
    ps[...] = eo[nz - 1, 2].astype(BF16)
    ps_c = send(ps, pr, ps_s.at[0], ps_r.at[0], turned(1, 0, 0)[1])
    total(1)
    finish(2)
    finish(3)
    total(0)
    eg_ref[:, lo_cols] = eo[nz - 1, 0]
    ps_c.wait_recv()
    eg_ref[:, hi_cols] = eo[nz - 1, 1] + pr[...].astype(F32)

    for i in range(3):
        relay(i, own(0), z, 0, line(1 - zm)).wait_send()
        for k in range(nz - 1):
            onward(k, i).wait_send()

        @pl.when(mid)
        def _():
            relay(i, own(0), z, nz, line(2)).wait_send()
            for n in range(1, nz):
                relay(i, own(0), z, n, line(0)).wait_send()

    for copy in sent:
        copy.wait_send()


def settle(ig_ref, eg_ref, ig_hbm, eg_hbm, done):
    copies = [pltpu.make_async_copy(ig_ref, ig_hbm, done.at[0]), pltpu.make_async_copy(eg_ref, eg_hbm, done.at[1])]
    for copy in copies:
        copy.start()
    for copy in copies:
        copy.wait()


def fused(inputs, out_grad, coeff_fixed, atom_counts, experts, nz):
    n_sys, n_slots, width = inputs.shape
    n_exp, rows, _ = experts.shape
    sr, er_rows = n_sys * rows, n_exp * rows
    half_w, quarter_w = width // 2, width // 4
    most_w = width - quarter_w
    vmem = pl.BlockSpec(memory_space=pltpu.VMEM)
    hbm = pl.BlockSpec(memory_space=pltpu.HBM)
    dma = pltpu.SemaphoreType.DMA
    in_grad, expert_grad = pl.pallas_call(
        functools.partial(kernel, nz, n_sys, n_exp, rows, width),
        out_shape=(
            pltpu.VMEM(inputs.shape, BF16),
            pltpu.VMEM((er_rows, width), F32),
        ),
        in_specs=[hbm] * 5,
        out_specs=(vmem, vmem),
        scratch_shapes=[
            pltpu.SMEM(atom_counts.shape, jnp.int32),
            pltpu.SMEM(coeff_fixed.shape, jnp.int32),
            pltpu.VMEM(inputs.shape, BF16),
            pltpu.VMEM((er_rows, width), BF16),
            pltpu.VMEM(out_grad.shape, BF16),
            pltpu.VMEM((2, 16, 128), BF16),
            pltpu.VMEM((8, 2, 16, 128), BF16),
            pltpu.VMEM((2, 8 * sr, er_rows), BF16),
            pltpu.VMEM((2, er_rows, 8 * sr), BF16),
            pltpu.VMEM((2, 4 * sr, er_rows), BF16),
            pltpu.VMEM((2, er_rows, 4 * sr), BF16),
            pltpu.VMEM((8, nz, sr, half_w), BF16),
            pltpu.VMEM((nz, 8, sr, half_w), BF16),
            pltpu.VMEM((nz, 8, sr, half_w), BF16),
            pltpu.VMEM((nz, 2, 4, sr, half_w), BF16),
            pltpu.VMEM((nz, 3, er_rows, half_w), F32),
            pltpu.VMEM((nz - 1, 3, er_rows, half_w), BF16),
            pltpu.VMEM((nz + 1, 3, er_rows, half_w), BF16),
            pltpu.VMEM((3, nz, er_rows, half_w), BF16),
            pltpu.VMEM((2, er_rows, quarter_w), BF16),
            pltpu.VMEM((8, n_sys, nz, rows, half_w), BF16),
            pltpu.VMEM((4, n_sys, nz, 2, rows, most_w), BF16),
            pltpu.VMEM((n_sys, nz, 8, rows, half_w), BF16),
            pltpu.VMEM((n_sys, nz, 4, 2, rows, most_w), BF16),
            pltpu.VMEM((er_rows, half_w), BF16),
            pltpu.VMEM((er_rows, half_w), BF16),
            dma((3 + 2 * n_sys,)), dma((1 + 4 * nz,)),
            dma((7,)), dma((7,)), dma((3,)), dma((3,)), dma((3, nz + 1)), dma((3, nz)),
            dma((nz // 2, 7)), dma((nz // 2, 7)), dma((nz, 3)), dma((nz, 3)),
            dma((nz - 1, 3)), dma((nz + 1, 3)),
            dma((nz, 7)), dma((nz, 7)), dma((nz, 3)), dma((nz, 3)), dma((1,)), dma((1,)),
        ],
        compiler_params=pltpu.CompilerParams(
            collective_id=0, has_side_effects=True, vmem_limit_bytes=48 * 1024 * 1024),
    )(*(
        pltpu.with_memory_space_constraint(a, pltpu.HBM)
        for a in (atom_counts, coeff_fixed, inputs, out_grad, experts.reshape(er_rows, width))))
    held = [pltpu.with_memory_space_constraint(a, pltpu.VMEM) for a in (in_grad, expert_grad)]
    in_grad, expert_grad = pl.pallas_call(
        settle,
        out_shape=(
            jax.ShapeDtypeStruct(inputs.shape, BF16),
            jax.ShapeDtypeStruct((er_rows, width), F32),
        ),
        in_specs=[vmem, vmem],
        out_specs=(hbm, hbm),
        scratch_shapes=[dma((2,))],
        compiler_params=pltpu.CompilerParams(vmem_limit_bytes=16 * 1024 * 1024),
    )(*held)
    return in_grad, expert_grad.reshape(n_exp, rows, width)


def plain(inputs, out_grad, coeff_fixed, atom_counts, experts):
    both = ("dp", "fsdp")
    n_sys, n_slots, width = inputs.shape
    n_exp, rows, _ = experts.shape
    coeffs = lax.all_gather(coeff_fixed, both, axis=0, tiled=True).astype(F32) / 4096.0
    valid = lax.broadcasted_iota(jnp.int32, (n_sys, n_slots), 1) < atom_counts[:, None]
    masked = jnp.where(valid[:, :, None], out_grad, jnp.zeros_like(out_grad))
    merged = jnp.einsum("se,eij->sij", coeffs, experts.astype(F32), precision=HIGH).astype(BF16)
    merged = lax.all_to_all(merged, both, split_axis=0, concat_axis=1, tiled=True)
    per_system = jnp.einsum("smi,smj->sij", inputs, masked, preferred_element_type=F32)
    per_system = lax.all_to_all(per_system, both, split_axis=1, concat_axis=0, tiled=True)
    expert_grad = jnp.einsum("se,sij->eij", coeffs, per_system, precision=HIGH)
    in_grad = jnp.einsum("smj,sij->smi", masked, merged, preferred_element_type=F32).astype(BF16)
    return in_grad, expert_grad


def solution(mesh):
    n_dp, n_fsdp = mesh.shape["dp"], mesh.shape["fsdp"]

    def shards(inputs, out_grad, coeff_fixed, atom_counts, experts):
        n_sys, _, width = inputs.shape
        n_exp, rows, _ = experts.shape
        if n_dp == 16 and n_fsdp == 2 and rows % 16 == 0 and n_sys <= 16 and n_exp <= 128 and width % 512 == 0:
            return fused(inputs, out_grad, coeff_fixed, atom_counts, experts, n_dp // 4)
        return plain(inputs, out_grad, coeff_fixed, atom_counts, experts)

    placed = (
        P(("dp", "fsdp"), None, None),
        P(("dp", "fsdp"), None, None),
        P(("dp", "fsdp"), None),
        P(("dp", "fsdp")),
        P(None, ("dp", "fsdp"), None),
    )
    return jax.shard_map(
        shards,
        mesh=mesh,
        in_specs=placed,
        out_specs=(P(("dp", "fsdp"), None, None), P(None, ("dp", "fsdp"), None)),
        check_vma=False,
    )
```

```python
import functools

import jax
import jax.numpy as jnp
from jax import lax
from jax.experimental import pallas as pl
from jax.experimental.pallas import tpu as pltpu
from jax.sharding import PartitionSpec as P

HIGH = lax.Precision.HIGHEST
MESH = pl.DeviceIdType.MESH
BF16 = jnp.bfloat16
F32 = jnp.float32
NEAR_ORDER = (5, 7, 4, 1, 6, 3, 2)


def dot(a, b, ca, cb):
    return lax.dot_general(a, b, (((ca,), (cb,)), ((), ())), preferred_element_type=F32)


def kernel(nz, n_sys, n_exp, rows, width,
           counts_hbm, co_hbm, in_hbm, og_hbm, ex_hbm,
           ig_ref, eg_ref,
           counts_ref, co_ref, in_ref, ex_ref, mk, cl, ca, ka, kt, kp, kq, pb, g, pc, gc, eo, zs, zr, xg, xq, mb, mc, mr, mq, ps, pr,
           ld, loc, ka_s, ka_r, xp_s, xp_r, xz_s, xz_r, pb_s, pb_r, pc_s, pc_r, zs_s, zs_r,
           mb_s, mb_r, mc_s, mc_r, ps_s, ps_r):
    dp = lax.axis_index("dp")
    y = lax.axis_index("fsdp")
    z = dp // 4
    x = lax.rem(dp // 2, 2)
    c = lax.rem(dp, 2)
    me = x * 4 + c * 2 + y
    sr = n_sys * rows
    half_w, quarter_w = width // 2, width // 4
    span = 8 * rows
    lo_cols, hi_cols = pl.ds(0, half_w), pl.ds(half_w, half_w)
    second = slice(quarter_w, half_w)

    def cut(near_z):
        return quarter_w if near_z else half_w

    def rest(near_z):
        return slice(cut(near_z) - quarter_w, width - quarter_w)

    def flip(v, d):
        return lax.rem(v + d, 2)

    def place(fx, fc, fy):
        xx, cc, yy = flip(x, fx), flip(c, fc), flip(y, fy)
        return xx * 4 + cc * 2 + yy, ((z * 2 + xx) * 2 + cc, yy)

    def near(j):
        return place(j // 4, j // 2 % 2, j % 2)

    def turned(fp, fq, fc):
        return place(fp * (1 - c) + fq * c, fc, fq * (1 - c) + fp * c)

    p_at = x * (1 - c) + y * c
    q_at = y * (1 - c) + x * c

    half = z // 2
    zm = z + half * (3 - 2 * z)
    mid = zm == 1

    def actual(v):
        return v + half * (3 - 2 * v)

    def line(v):
        return (actual(v) * 2 + x) * 2 + c, y

    def arrival(n):
        return actual((zm, 1 - zm, 2, 3)[n])

    def target(n):
        return actual((3, 2, 1 - zm, zm)[n])

    plane = NEAR_ORDER
    peers = [near(j)[1] for j in plane] + [line(1 - zm)]
    barrier = pltpu.get_barrier_semaphore()
    for peer in peers:
        pl.semaphore_signal(barrier, inc=1, device_id=peer, device_id_type=MESH)

    @pl.when(mid)
    def _():
        pl.semaphore_signal(barrier, inc=1, device_id=line(2), device_id_type=MESH)

    def load(n, src, dst):
        copy = pltpu.make_async_copy(src, dst, ld.at[n])
        copy.start()
        return copy

    co_c = load(1 + 2 * n_sys, co_hbm, co_ref)
    counts_c = load(2 + 2 * n_sys, counts_hbm, counts_ref)
    ex_c = load(0, ex_hbm, ex_ref)
    og_c = [load(1 + s, og_hbm.at[s], mk.at[s]) for s in range(n_sys)]
    in_c = [load(1 + n_sys + s, in_hbm.at[s], in_ref.at[s]) for s in range(n_sys)]

    ex_c.wait()
    pl.semaphore_wait(barrier, len(peers) + zm)

    def remote(src, dst, s, r, peer):
        return pltpu.make_async_remote_copy(
            src_ref=src, dst_ref=dst, send_sem=s, recv_sem=r, device_id=peer, device_id_type=MESH
        )

    sent = []

    def send(src, dst, s, r, peer):
        copy = remote(src, dst, s, r, peer)
        copy.start()
        sent.append(copy)
        return copy

    n_loc = [0]

    def local(src, dst):
        copy = pltpu.make_async_copy(src, dst, loc.at[n_loc[0]])
        n_loc[0] += 1
        copy.start()
        return copy

    def own(i):
        return ex_ref.at[:, (lo_cols, hi_cols)[i]] if i < 2 else xg.at[2, z]

    def relay(i, src, block, n, to):
        return remote(src, xg.at[i, block], xz_s.at[i, n], xz_r.at[i, block], to)

    def offer(i):
        relay(i, own(i), z, 0, line(1 - zm)).start()

        @pl.when(mid)
        def _():
            relay(i, own(i), z, nz, line(2)).start()

    xp = send(own(1), xg.at[2, z], xp_s.at[0], xp_r.at[0], turned(1, 0, 0)[1])
    offer(0)
    offer(1)
    xq_c = send(ex_ref.at[:, second], xq.at[0], xp_s.at[1], xp_r.at[1], turned(1, 0, 0)[1])
    col = lax.broadcasted_iota(jnp.int32, cl.shape, 1)
    row = lax.broadcasted_iota(jnp.int32, cl.shape, 0)
    system = lax.rem(row, n_sys)
    fixed = jnp.zeros(cl.shape, jnp.int32)
    co_c.wait()
    counts_c.wait()
    for s in range(n_sys):
        for e in range(n_exp):
            fixed = jnp.where((system == s) & (col == e), co_ref[s, e], fixed)
    high, low = (fixed >> 6).astype(F32) / 64.0, (fixed & 63).astype(F32) / 4096.0
    cl[...] = jnp.where(row < n_sys, high, low).astype(BF16)
    ca_c = [send(cl, ca.at[me], ka_s.at[j - 1], ka_r.at[j - 1], near(j)[1]) for j in plane]
    ca_own = local(cl, ca.at[me])

    for s in range(n_sys):
        og_c[s].wait()
        slot = lax.broadcasted_iota(jnp.int32, mk.shape[1:], 0)
        mk[s] = jnp.where(slot < counts_ref[s], mk[s], jnp.zeros(mk.shape[1:], BF16))
    for copy in in_c:
        copy.wait()

    pb_c, g_own, pc_c, gc_own = {}, {}, {}, {}
    takers = ((0, 0, 0), (0, 0, 1), (0, 1, 0), (1, 0, 1))

    def seat(b):
        fx, fc, fy = flip(x, b // 4), flip(c, b // 2 % 2), flip(y, b % 2)
        fp, fq = fx * (1 - c) + fy * c, fy * (1 - c) + fx * c
        return (1 - fc) * (4 * fq + fp) + fc * (2 + 4 * fp + fq)

    def produce(k):
        lanes = pl.ds(pl.multiple_of(target(k) * span, span), span)
        n = half_w
        for s in range(n_sys):
            prod = dot(in_ref[s, :, lanes], mk[s], 0, 0).astype(BF16)
            for b in range(8):
                pb[b, k, s * rows:(s + 1) * rows, :] = prod[b * rows:(b + 1) * rows, :n]
                pc[k, seat(b), s * rows:(s + 1) * rows, :] = prod[b * rows:(b + 1) * rows, n:]
        for v in (2, 3, 1):
            at = (p_at if v % 2 else q_at) * 2 + c
            pc_c[k, v] = send(pc.at[k, 2 * v:2 * v + 2], gc.at[k, :, at], pc_s.at[k, v - 1], pc_r.at[k, v - 1],
                              turned(*takers[v])[1])
        gc_own[k] = local(pc.at[k, 0:2], gc.at[k, :, q_at * 2 + c])

    def deal(h):
        two = slice(2 * h, 2 * h + 2)
        for j in plane:
            to, peer = near(j)
            pb_c[h, j] = send(pb.at[to, two], g.at[two, me], pb_s.at[h, j - 1], pb_r.at[h, j - 1], peer)
        g_own[h] = local(pb.at[me, two], g.at[two, me])

    mb_c, m_own, mc_c, mc_own = {}, {}, {}, {}

    def held(k, i):
        return ex_ref[:, (lo_cols, hi_cols)[i]] if k == 0 and i < 2 else xg[i, arrival(k)]

    def mixed(weights, block):
        return (dot(weights[0], block, 1, 0) + dot(weights[1], block, 1, 0)).astype(BF16)

    def merge(*ks):
        span_k = slice(ks[0], ks[-1] + 1)
        close = ks[0] < 2
        n, others = cut(close), rest(close)
        for k in ks:
            for i in (1, 2):
                to = flip(p_at, i - 1)
                mc[:, :, k, to, :, quarter_w:] = mixed(kp, held(k, i)).reshape(4, n_sys, rows, half_w)
                if close:
                    piece = xq[k] if i == 2 else held(k, 0)[:, second]
                    mc[:, :, k, to, :, :quarter_w] = mixed(kp, piece).reshape(4, n_sys, rows, quarter_w)
        k = ks[-1]
        at = 2 * c + q_at
        for v, (fq, fc) in ((2, (1, 0)), (3, (1, 1)), (1, (0, 1))):
            u = flip(q_at, fq) * 2 + flip(c, fc)
            mc_c[k, v] = send(mc.at[u, :, span_k, :, :, others], mq.at[:, span_k, at, :, :, others],
                              mc_s.at[k, v - 1], mc_r.at[k, v - 1], turned(0, fq, fc)[1])
        mc_own[k] = local(mc.at[q_at * 2 + c, :, span_k, :, :, others], mq.at[:, span_k, at, :, :, others])
        for k in ks:
            mb[:, :, k, :, :n] = mixed(ka, held(k, 0)[:, :n]).reshape(8, n_sys, rows, n)
        for j in plane:
            to, peer = near(j)
            mb_c[k, j] = send(mb.at[to, :, span_k, :, :n], mr.at[:, span_k, me, :, :n],
                              mb_s.at[k, j - 1], mb_r.at[k, j - 1], peer)
        m_own[k] = local(mb.at[me, :, span_k, :, :n], mr.at[:, span_k, me, :, :n])

    def landed(slot, i):
        remote(zs.at[0, i], zr.at[slot, i], zs_s.at[0, i], zs_r.at[slot, i], line(1 - zm)).wait_recv()
        return zr[slot, i].astype(F32)

    def reduce(k):
        gc_own[k].wait()
        for v in (1, 2, 3):
            pc_c[k, v].wait_recv()
        for i in (1, 0):
            block = gc[k, i].reshape(4 * sr, half_w)
            eo[k, i + 1] = dot(kq[0], block, 1, 0) + dot(kq[1], block, 1, 0)
            begin(k, i + 1)
        if k % 2 == 0:
            g_own[k // 2].wait()
            for j in plane:
                pb_c[k // 2, j].wait_recv()
        block = g[k].reshape(8 * sr, half_w)
        eo[k, 0] = dot(kt[0], block, 1, 0) + dot(kt[1], block, 1, 0)
        begin(k, 0)

    def onward(k, i):
        slot = (2 * zm, 1 + 3 * zm, 3)[k]
        return remote(zs.at[k, i], zr.at[slot, i], zs_s.at[k, i], zs_r.at[slot, i],
                      line((zm + 1, zm + 1, 1 - zm)[k]))

    def begin(k, i):
        if k < nz - 1:
            @pl.when(zm == 0)
            def _():
                zs[k, i] = eo[k, i].astype(BF16)
                onward(k, i).start()

    def proceed(k, i):
        @pl.when(mid)
        def _():
            zs[k, i] = (eo[k, i] + landed(k, i)).astype(BF16)
            onward(k, i).start()

    def finish(k):
        if k in m_own:
            m_own[k].wait()
            mc_own[k].wait()
            for j in plane:
                mb_c[k, j].wait_recv()
            for v in (1, 2, 3):
                mc_c[k, v].wait_recv()
        lanes = pl.ds(pl.multiple_of(arrival(k) * span, span), span)
        for s in range(n_sys):
            first = mr[s, k, :, :, :cut(k < 2)].reshape(span, cut(k < 2))
            last = jnp.concatenate(
                [mq[s, k, (b % 2, 2 + b // 4)[b // 2 % 2], (b // 4, b % 2)[b // 2 % 2], :, rest(k < 2)]
                 for b in range(8)], axis=0)
            ig_ref[s, :, lanes] = dot(mk[s], jnp.concatenate([first, last], axis=1), 1, 1).astype(BF16)

    def came(n, i):
        block = arrival(n)
        relay(i, own(0), block, n, line(1 - zm)).wait_recv()

    def handed(n, i):
        block = arrival(n)

        @pl.when(mid)
        def _():
            came(n, i)
            relay(i, xg.at[i, block], block, n, line(2 if n == 1 else 0)).start()

    def awaited(n):
        @pl.when(zm == 0)
        def _():
            for i in range(3):
                came(n, i)

    produce(0)
    xp.wait_recv()
    offer(2)
    produce(1)
    deal(0)
    produce(2)
    produce(3)
    deal(1)
    xq_c.wait_recv()
    xq_n = send(xq.at[0], xq.at[1], xp_s.at[2], xp_r.at[2], line(1 - zm))

    ca_own.wait()
    for copy in ca_c:
        copy.wait_recv()
    er_rows = n_exp * rows
    lane = lax.broadcasted_iota(jnp.int32, (cl.shape[1], er_rows), 1)
    first = lax.broadcasted_iota(jnp.int32, (cl.shape[1], er_rows), 0) * rows
    pick = jnp.where((lane >= first) & (lane < first + rows), 1.0, 0.0).astype(BF16)
    told = ca[...].astype(F32).reshape(8 * cl.shape[0], cl.shape[1]).astype(BF16)
    wide = dot(told, pick, 1, 0)
    across = lax.broadcasted_iota(jnp.int32, (rows, er_rows), 1) % rows
    diagonal = across == lax.broadcasted_iota(jnp.int32, (rows, er_rows), 0)
    for d in range(8):
        for h in range(2):
            for s in range(n_sys):
                at = d * cl.shape[0] + h * n_sys + s
                value = jnp.broadcast_to(wide[at:at + 1, :], (rows, er_rows))
                spot = (d * n_sys + s) * rows
                ka[h, spot:spot + rows, :] = jnp.where(diagonal, value, 0.0).astype(BF16)
    for h in range(2):
        for u in range(4):
            uq, uc = u // 2, u % 2
            at = (x * (1 - c) + uq * c) * 4 + uc * 2 + uq * (1 - c) + y * c
            kp[h, u * sr:(u + 1) * sr, :] = ka[h, pl.ds(pl.multiple_of(at * sr, sr), sr), :]
    for h in range(2):
        kt[h] = ka[h].T
        kq[h] = kp[h].T

    for i in range(2):
        handed(1, i)
        handed(2, i)
    reduce(0)
    handed(1, 2)
    handed(2, 2)
    reduce(1)
    awaited(1)
    xq_n.wait_recv()
    merge(0, 1)
    handed(3, 0)
    proceed(0, 2)
    handed(3, 1)
    proceed(0, 1)
    reduce(2)
    handed(3, 2)
    proceed(0, 0)
    awaited(2)
    merge(2)
    reduce(3)
    awaited(3)
    merge(3)
    for i in (2, 1, 0):
        proceed(1, i)
        proceed(2, i)
    finish(1)
    finish(0)

    def total(i):
        eo[nz - 1, i] += landed(3, i)

        @pl.when(mid)
        def _():
            eo[nz - 1, i] += landed(4, i)

    total(2)
    ps[...] = eo[nz - 1, 2].astype(BF16)
    ps_c = send(ps, pr, ps_s.at[0], ps_r.at[0], turned(1, 0, 0)[1])
    total(1)
    finish(2)
    finish(3)
    total(0)
    eg_ref[:, lo_cols] = eo[nz - 1, 0]
    ps_c.wait_recv()
    eg_ref[:, hi_cols] = eo[nz - 1, 1] + pr[...].astype(F32)

    for i in range(3):
        relay(i, own(0), z, 0, line(1 - zm)).wait_send()
        for k in range(nz - 1):
            onward(k, i).wait_send()

        @pl.when(mid)
        def _():
            relay(i, own(0), z, nz, line(2)).wait_send()
            for n in range(1, nz):
                relay(i, own(0), z, n, line(0)).wait_send()

    for copy in sent:
        copy.wait_send()


def settle(ig_ref, eg_ref, ig_hbm, eg_hbm, done):
    copies = [pltpu.make_async_copy(ig_ref, ig_hbm, done.at[0]), pltpu.make_async_copy(eg_ref, eg_hbm, done.at[1])]
    for copy in copies:
        copy.start()
    for copy in copies:
        copy.wait()


def fused(inputs, out_grad, coeff_fixed, atom_counts, experts, nz):
    n_sys, n_slots, width = inputs.shape
    n_exp, rows, _ = experts.shape
    sr, er_rows = n_sys * rows, n_exp * rows
    half_w, quarter_w = width // 2, width // 4
    most_w = width - quarter_w
    vmem = pl.BlockSpec(memory_space=pltpu.VMEM)
    hbm = pl.BlockSpec(memory_space=pltpu.HBM)
    dma = pltpu.SemaphoreType.DMA
    in_grad, expert_grad = pl.pallas_call(
        functools.partial(kernel, nz, n_sys, n_exp, rows, width),
        out_shape=(
            pltpu.VMEM(inputs.shape, BF16),
            pltpu.VMEM((er_rows, width), F32),
        ),
        in_specs=[hbm] * 5,
        out_specs=(vmem, vmem),
        scratch_shapes=[
            pltpu.SMEM(atom_counts.shape, jnp.int32),
            pltpu.SMEM(coeff_fixed.shape, jnp.int32),
            pltpu.VMEM(inputs.shape, BF16),
            pltpu.VMEM((er_rows, width), BF16),
            pltpu.VMEM(out_grad.shape, BF16),
            pltpu.VMEM((8, 128), BF16),
            pltpu.VMEM((8, 8, 128), BF16),
            pltpu.VMEM((2, 8 * sr, er_rows), BF16),
            pltpu.VMEM((2, er_rows, 8 * sr), BF16),
            pltpu.VMEM((2, 4 * sr, er_rows), BF16),
            pltpu.VMEM((2, er_rows, 4 * sr), BF16),
            pltpu.VMEM((8, nz, sr, half_w), BF16),
            pltpu.VMEM((nz, 8, sr, half_w), BF16),
            pltpu.VMEM((nz, 8, sr, half_w), BF16),
            pltpu.VMEM((nz, 2, 4, sr, half_w), BF16),
            pltpu.VMEM((nz, 3, er_rows, half_w), F32),
            pltpu.VMEM((nz - 1, 3, er_rows, half_w), BF16),
            pltpu.VMEM((nz + 1, 3, er_rows, half_w), BF16),
            pltpu.VMEM((3, nz, er_rows, half_w), BF16),
            pltpu.VMEM((2, er_rows, quarter_w), BF16),
            pltpu.VMEM((8, n_sys, nz, rows, half_w), BF16),
            pltpu.VMEM((4, n_sys, nz, 2, rows, most_w), BF16),
            pltpu.VMEM((n_sys, nz, 8, rows, half_w), BF16),
            pltpu.VMEM((n_sys, nz, 4, 2, rows, most_w), BF16),
            pltpu.VMEM((er_rows, half_w), BF16),
            pltpu.VMEM((er_rows, half_w), BF16),
            dma((3 + 2 * n_sys,)), dma((1 + 4 * nz,)),
            dma((7,)), dma((7,)), dma((3,)), dma((3,)), dma((3, nz + 1)), dma((3, nz)),
            dma((nz // 2, 7)), dma((nz // 2, 7)), dma((nz, 3)), dma((nz, 3)),
            dma((nz - 1, 3)), dma((nz + 1, 3)),
            dma((nz, 7)), dma((nz, 7)), dma((nz, 3)), dma((nz, 3)), dma((1,)), dma((1,)),
        ],
        compiler_params=pltpu.CompilerParams(
            collective_id=0, has_side_effects=True, vmem_limit_bytes=48 * 1024 * 1024),
    )(*(
        pltpu.with_memory_space_constraint(a, pltpu.HBM)
        for a in (atom_counts, coeff_fixed, inputs, out_grad, experts.reshape(er_rows, width))))
    held = [pltpu.with_memory_space_constraint(a, pltpu.VMEM) for a in (in_grad, expert_grad)]
    in_grad, expert_grad = pl.pallas_call(
        settle,
        out_shape=(
            jax.ShapeDtypeStruct(inputs.shape, BF16),
            jax.ShapeDtypeStruct((er_rows, width), F32),
        ),
        in_specs=[vmem, vmem],
        out_specs=(hbm, hbm),
        scratch_shapes=[dma((2,))],
        compiler_params=pltpu.CompilerParams(vmem_limit_bytes=16 * 1024 * 1024),
    )(*held)
    return in_grad, expert_grad.reshape(n_exp, rows, width)


def plain(inputs, out_grad, coeff_fixed, atom_counts, experts):
    both = ("dp", "fsdp")
    n_sys, n_slots, width = inputs.shape
    n_exp, rows, _ = experts.shape
    coeffs = lax.all_gather(coeff_fixed, both, axis=0, tiled=True).astype(F32) / 4096.0
    valid = lax.broadcasted_iota(jnp.int32, (n_sys, n_slots), 1) < atom_counts[:, None]
    masked = jnp.where(valid[:, :, None], out_grad, jnp.zeros_like(out_grad))
    merged = jnp.einsum("se,eij->sij", coeffs, experts.astype(F32), precision=HIGH).astype(BF16)
    merged = lax.all_to_all(merged, both, split_axis=0, concat_axis=1, tiled=True)
    per_system = jnp.einsum("smi,smj->sij", inputs, masked, preferred_element_type=F32)
    per_system = lax.all_to_all(per_system, both, split_axis=1, concat_axis=0, tiled=True)
    expert_grad = jnp.einsum("se,sij->eij", coeffs, per_system, precision=HIGH)
    in_grad = jnp.einsum("smj,sij->smi", masked, merged, preferred_element_type=F32).astype(BF16)
    return in_grad, expert_grad


def solution(mesh):
    n_dp, n_fsdp = mesh.shape["dp"], mesh.shape["fsdp"]

    def shards(inputs, out_grad, coeff_fixed, atom_counts, experts):
        n_sys, _, width = inputs.shape
        n_exp, rows, _ = experts.shape
        if n_dp == 16 and n_fsdp == 2 and rows % 16 == 0 and n_sys <= 4 and n_exp <= 128 and width % 512 == 0:
            return fused(inputs, out_grad, coeff_fixed, atom_counts, experts, n_dp // 4)
        return plain(inputs, out_grad, coeff_fixed, atom_counts, experts)

    placed = (
        P(("dp", "fsdp"), None, None),
        P(("dp", "fsdp"), None, None),
        P(("dp", "fsdp"), None),
        P(("dp", "fsdp")),
        P(None, ("dp", "fsdp"), None),
    )
    return jax.shard_map(
        shards,
        mesh=mesh,
        in_specs=placed,
        out_specs=(P(("dp", "fsdp"), None, None), P(None, ("dp", "fsdp"), None)),
        check_vma=False,
    )
```

```python
import functools

import jax
import jax.numpy as jnp
from jax import lax
from jax.experimental import pallas as pl
from jax.experimental.pallas import tpu as pltpu
from jax.sharding import PartitionSpec as P

HIGH = lax.Precision.HIGHEST
MESH = pl.DeviceIdType.MESH
BF16 = jnp.bfloat16
F32 = jnp.float32
NEAR_ORDER = (5, 7, 4, 1, 6, 3, 2)
DIAGONAL = (5, 7)


def dot(a, b, ca, cb):
    return lax.dot_general(a, b, (((ca,), (cb,)), ((), ())), preferred_element_type=F32)


def kernel(nz, n_sys, n_exp, rows, width,
           counts_hbm, co_hbm, in_hbm, og_hbm, ex_hbm,
           ig_ref, eg_ref,
           counts_ref, co_ref, in_ref, ex_ref, mk, cl, ca, ka, kt, kp, kq, pb, g, pc, gc, eo, zs, zr, xg, xq, mb, mc, mr, mq, ps, pr,
           vouched, ld, loc, ka_s, ka_r, xp_s, xp_r, xz_s, xz_r, pb_s, pb_r, pc_s, pc_r, zs_s, zs_r,
           mb_s, mb_r, mc_s, mc_r, ps_s, ps_r):
    dp = lax.axis_index("dp")
    y = lax.axis_index("fsdp")
    z = dp // 4
    x = lax.rem(dp // 2, 2)
    c = lax.rem(dp, 2)
    me = x * 4 + c * 2 + y
    sr = n_sys * rows
    half_w, quarter_w = width // 2, width // 4
    span = 8 * rows
    lo_cols, hi_cols = pl.ds(0, half_w), pl.ds(half_w, half_w)
    second = slice(quarter_w, half_w)

    def cut(near_z):
        return quarter_w if near_z else half_w

    def rest(near_z):
        return slice(cut(near_z) - quarter_w, width - quarter_w)

    def flip(v, d):
        return lax.rem(v + d, 2)

    def place(fx, fc, fy):
        xx, cc, yy = flip(x, fx), flip(c, fc), flip(y, fy)
        return xx * 4 + cc * 2 + yy, ((z * 2 + xx) * 2 + cc, yy)

    def near(j):
        return place(j // 4, j // 2 % 2, j % 2)

    def turned(fp, fq, fc):
        return place(fp * (1 - c) + fq * c, fc, fq * (1 - c) + fp * c)

    p_at = x * (1 - c) + y * c
    q_at = y * (1 - c) + x * c

    half = z // 2
    zm = z + half * (3 - 2 * z)
    mid = zm == 1

    def actual(v):
        return v + half * (3 - 2 * v)

    def line(v):
        return (actual(v) * 2 + x) * 2 + c, y

    def arrival(n):
        return actual((zm, 1 - zm, 2, 3)[n])

    def target(n):
        return actual((3, 2, 1 - zm, zm)[n])

    plane = NEAR_ORDER
    peers = [near(j)[1] for j in plane if j not in DIAGONAL] + [line(1 - zm)]
    barrier = pltpu.get_barrier_semaphore()
    for peer in peers:
        pl.semaphore_signal(barrier, inc=1, device_id=peer, device_id_type=MESH)

    @pl.when(mid)
    def _():
        pl.semaphore_signal(barrier, inc=1, device_id=line(2), device_id_type=MESH)

    def load(n, src, dst):
        copy = pltpu.make_async_copy(src, dst, ld.at[n])
        copy.start()
        return copy

    co_c = load(1 + 2 * n_sys, co_hbm, co_ref)
    counts_c = load(2 + 2 * n_sys, counts_hbm, counts_ref)
    ex_c = load(0, ex_hbm, ex_ref)
    og_c = [load(1 + s, og_hbm.at[s], mk.at[s]) for s in range(n_sys)]
    in_c = [load(1 + n_sys + s, in_hbm.at[s], in_ref.at[s]) for s in range(n_sys)]

    ex_c.wait()
    pl.semaphore_wait(barrier, len(peers) + zm)

    def remote(src, dst, s, r, peer):
        return pltpu.make_async_remote_copy(
            src_ref=src, dst_ref=dst, send_sem=s, recv_sem=r, device_id=peer, device_id_type=MESH
        )

    sent = []

    def send(src, dst, s, r, peer):
        copy = remote(src, dst, s, r, peer)
        copy.start()
        sent.append(copy)
        return copy

    n_loc = [0]

    def local(src, dst):
        copy = pltpu.make_async_copy(src, dst, loc.at[n_loc[0]])
        n_loc[0] += 1
        copy.start()
        return copy

    def own(i):
        return ex_ref.at[:, (lo_cols, hi_cols)[i]] if i < 2 else xg.at[2, z]

    def relay(i, src, block, n, to):
        return remote(src, xg.at[i, block], xz_s.at[i, n], xz_r.at[i, block], to)

    def offer(i):
        relay(i, own(i), z, 0, line(1 - zm)).start()

        @pl.when(mid)
        def _():
            relay(i, own(i), z, nz, line(2)).start()

    pl.semaphore_signal(vouched, inc=1, device_id=near(4)[1], device_id_type=MESH)
    xp = send(own(1), xg.at[2, z], xp_s.at[0], xp_r.at[0], turned(1, 0, 0)[1])
    offer(0)
    offer(1)
    xq_c = send(ex_ref.at[:, second], xq.at[0], xp_s.at[1], xp_r.at[1], turned(1, 0, 0)[1])
    col = lax.broadcasted_iota(jnp.int32, cl.shape, 1)
    row = lax.broadcasted_iota(jnp.int32, cl.shape, 0)
    system = lax.rem(row, n_sys)
    fixed = jnp.zeros(cl.shape, jnp.int32)
    co_c.wait()
    counts_c.wait()
    for s in range(n_sys):
        for e in range(n_exp):
            fixed = jnp.where((system == s) & (col == e), co_ref[s, e], fixed)
    high, low = (fixed >> 6).astype(F32) / 64.0, (fixed & 63).astype(F32) / 4096.0
    cl[...] = jnp.where(row < n_sys, high, low).astype(BF16)
    ca_c = []

    def tell(j):
        ca_c.append(send(cl, ca.at[me], ka_s.at[j - 1], ka_r.at[j - 1], near(j)[1]))

    for j in plane:
        if j not in DIAGONAL:
            tell(j)
    ca_own = local(cl, ca.at[me])

    for s in range(n_sys):
        og_c[s].wait()
        slot = lax.broadcasted_iota(jnp.int32, mk.shape[1:], 0)
        mk[s] = jnp.where(slot < counts_ref[s], mk[s], jnp.zeros(mk.shape[1:], BF16))
    for copy in in_c:
        copy.wait()

    pb_c, g_own, pc_c, gc_own = {}, {}, {}, {}
    takers = ((0, 0, 0), (0, 0, 1), (0, 1, 0), (1, 0, 1))

    def seat(b):
        fx, fc, fy = flip(x, b // 4), flip(c, b // 2 % 2), flip(y, b % 2)
        fp, fq = fx * (1 - c) + fy * c, fy * (1 - c) + fx * c
        return (1 - fc) * (4 * fq + fp) + fc * (2 + 4 * fp + fq)

    def produce(k):
        lanes = pl.ds(pl.multiple_of(target(k) * span, span), span)
        n = half_w
        for s in range(n_sys):
            prod = dot(in_ref[s, :, lanes], mk[s], 0, 0).astype(BF16)
            for b in range(8):
                pb[b, k, s * rows:(s + 1) * rows, :] = prod[b * rows:(b + 1) * rows, :n]
                pc[k, seat(b), s * rows:(s + 1) * rows, :] = prod[b * rows:(b + 1) * rows, n:]
        for v in (2, 3, 1):
            at = (p_at if v % 2 else q_at) * 2 + c
            pc_c[k, v] = send(pc.at[k, 2 * v:2 * v + 2], gc.at[k, :, at], pc_s.at[k, v - 1], pc_r.at[k, v - 1],
                              turned(*takers[v])[1])
        gc_own[k] = local(pc.at[k, 0:2], gc.at[k, :, q_at * 2 + c])

    def deal(h):
        two = slice(2 * h, 2 * h + 2)
        for j in plane:
            to, peer = near(j)
            pb_c[h, j] = send(pb.at[to, two], g.at[two, me], pb_s.at[h, j - 1], pb_r.at[h, j - 1], peer)
        g_own[h] = local(pb.at[me, two], g.at[two, me])

    mb_c, m_own, mc_c, mc_own = {}, {}, {}, {}

    def held(k, i):
        return ex_ref[:, (lo_cols, hi_cols)[i]] if k == 0 and i < 2 else xg[i, arrival(k)]

    def mixed(weights, block):
        return (dot(weights[0], block, 1, 0) + dot(weights[1], block, 1, 0)).astype(BF16)

    def merge(*ks):
        span_k = slice(ks[0], ks[-1] + 1)
        close = ks[0] < 2
        n, others = cut(close), rest(close)
        for k in ks:
            for i in (1, 2):
                to = flip(p_at, i - 1)
                mc[:, :, k, to, :, quarter_w:] = mixed(kp, held(k, i)).reshape(4, n_sys, rows, half_w)
                if close:
                    piece = xq[k] if i == 2 else held(k, 0)[:, second]
                    mc[:, :, k, to, :, :quarter_w] = mixed(kp, piece).reshape(4, n_sys, rows, quarter_w)
        k = ks[-1]
        at = 2 * c + q_at
        for v, (fq, fc) in ((2, (1, 0)), (3, (1, 1)), (1, (0, 1))):
            u = flip(q_at, fq) * 2 + flip(c, fc)
            mc_c[k, v] = send(mc.at[u, :, span_k, :, :, others], mq.at[:, span_k, at, :, :, others],
                              mc_s.at[k, v - 1], mc_r.at[k, v - 1], turned(0, fq, fc)[1])
        mc_own[k] = local(mc.at[q_at * 2 + c, :, span_k, :, :, others], mq.at[:, span_k, at, :, :, others])
        for k in ks:
            mb[:, :, k, :, :n] = mixed(ka, held(k, 0)[:, :n]).reshape(8, n_sys, rows, n)
        for j in plane:
            to, peer = near(j)
            mb_c[k, j] = send(mb.at[to, :, span_k, :, :n], mr.at[:, span_k, me, :, :n],
                              mb_s.at[k, j - 1], mb_r.at[k, j - 1], peer)
        m_own[k] = local(mb.at[me, :, span_k, :, :n], mr.at[:, span_k, me, :, :n])

    def landed(slot, i):
        remote(zs.at[0, i], zr.at[slot, i], zs_s.at[0, i], zs_r.at[slot, i], line(1 - zm)).wait_recv()
        return zr[slot, i].astype(F32)

    def reduce(k):
        gc_own[k].wait()
        for v in (1, 2, 3):
            pc_c[k, v].wait_recv()
        for i in (1, 0):
            block = gc[k, i].reshape(4 * sr, half_w)
            eo[k, i + 1] = dot(kq[0], block, 1, 0) + dot(kq[1], block, 1, 0)
            begin(k, i + 1)
        if k % 2 == 0:
            g_own[k // 2].wait()
            for j in plane:
                pb_c[k // 2, j].wait_recv()
        block = g[k].reshape(8 * sr, half_w)
        eo[k, 0] = dot(kt[0], block, 1, 0) + dot(kt[1], block, 1, 0)
        begin(k, 0)

    def onward(k, i):
        slot = (2 * zm, 1 + 3 * zm, 3)[k]
        return remote(zs.at[k, i], zr.at[slot, i], zs_s.at[k, i], zs_r.at[slot, i],
                      line((zm + 1, zm + 1, 1 - zm)[k]))

    def begin(k, i):
        if k < nz - 1:
            @pl.when(zm == 0)
            def _():
                zs[k, i] = eo[k, i].astype(BF16)
                onward(k, i).start()

    def proceed(k, i):
        @pl.when(mid)
        def _():
            zs[k, i] = (eo[k, i] + landed(k, i)).astype(BF16)
            onward(k, i).start()

    def finish(k):
        if k in m_own:
            m_own[k].wait()
            mc_own[k].wait()
            for j in plane:
                mb_c[k, j].wait_recv()
            for v in (1, 2, 3):
                mc_c[k, v].wait_recv()
        lanes = pl.ds(pl.multiple_of(arrival(k) * span, span), span)
        for s in range(n_sys):
            first = mr[s, k, :, :, :cut(k < 2)].reshape(span, cut(k < 2))
            last = jnp.concatenate(
                [mq[s, k, (b % 2, 2 + b // 4)[b // 2 % 2], (b // 4, b % 2)[b // 2 % 2], :, rest(k < 2)]
                 for b in range(8)], axis=0)
            ig_ref[s, :, lanes] = dot(mk[s], jnp.concatenate([first, last], axis=1), 1, 1).astype(BF16)

    def came(n, i):
        block = arrival(n)
        relay(i, own(0), block, n, line(1 - zm)).wait_recv()

    def handed(n, i):
        block = arrival(n)

        @pl.when(mid)
        def _():
            came(n, i)
            relay(i, xg.at[i, block], block, n, line(2 if n == 1 else 0)).start()

    def awaited(n):
        @pl.when(zm == 0)
        def _():
            for i in range(3):
                came(n, i)

    produce(0)
    xp.wait_recv()
    offer(2)
    produce(1)
    pl.semaphore_wait(vouched, 1)
    for j in DIAGONAL:
        tell(j)
    deal(0)
    produce(2)
    produce(3)
    deal(1)
    xq_c.wait_recv()
    xq_n = send(xq.at[0], xq.at[1], xp_s.at[2], xp_r.at[2], line(1 - zm))

    ca_own.wait()
    for copy in ca_c:
        copy.wait_recv()
    er_rows = n_exp * rows
    lane = lax.broadcasted_iota(jnp.int32, (cl.shape[1], er_rows), 1)
    first = lax.broadcasted_iota(jnp.int32, (cl.shape[1], er_rows), 0) * rows
    pick = jnp.where((lane >= first) & (lane < first + rows), 1.0, 0.0).astype(BF16)
    told = ca[...].astype(F32).reshape(8 * cl.shape[0], cl.shape[1]).astype(BF16)
    wide = dot(told, pick, 1, 0)
    across = lax.broadcasted_iota(jnp.int32, (rows, er_rows), 1) % rows
    diagonal = across == lax.broadcasted_iota(jnp.int32, (rows, er_rows), 0)
    for d in range(8):
        for h in range(2):
            for s in range(n_sys):
                at = d * cl.shape[0] + h * n_sys + s
                value = jnp.broadcast_to(wide[at:at + 1, :], (rows, er_rows))
                spot = (d * n_sys + s) * rows
                ka[h, spot:spot + rows, :] = jnp.where(diagonal, value, 0.0).astype(BF16)
    for h in range(2):
        for u in range(4):
            uq, uc = u // 2, u % 2
            at = (x * (1 - c) + uq * c) * 4 + uc * 2 + uq * (1 - c) + y * c
            kp[h, u * sr:(u + 1) * sr, :] = ka[h, pl.ds(pl.multiple_of(at * sr, sr), sr), :]
    for h in range(2):
        kt[h] = ka[h].T
        kq[h] = kp[h].T

    for i in range(2):
        handed(1, i)
        handed(2, i)
    reduce(0)
    handed(1, 2)
    handed(2, 2)
    reduce(1)
    awaited(1)
    xq_n.wait_recv()
    merge(0, 1)
    handed(3, 0)
    proceed(0, 2)
    handed(3, 1)
    proceed(0, 1)
    reduce(2)
    handed(3, 2)
    proceed(0, 0)
    awaited(2)
    merge(2)
    reduce(3)
    awaited(3)
    merge(3)
    for i in (2, 1, 0):
        proceed(1, i)
        proceed(2, i)
    finish(1)
    finish(0)

    def total(i):
        eo[nz - 1, i] += landed(3, i)

        @pl.when(mid)
        def _():
            eo[nz - 1, i] += landed(4, i)

    total(2)
    ps[...] = eo[nz - 1, 2].astype(BF16)
    ps_c = send(ps, pr, ps_s.at[0], ps_r.at[0], turned(1, 0, 0)[1])
    total(1)
    finish(2)
    finish(3)
    total(0)
    eg_ref[:, lo_cols] = eo[nz - 1, 0]
    ps_c.wait_recv()
    eg_ref[:, hi_cols] = eo[nz - 1, 1] + pr[...].astype(F32)

    for i in range(3):
        relay(i, own(0), z, 0, line(1 - zm)).wait_send()
        for k in range(nz - 1):
            onward(k, i).wait_send()

        @pl.when(mid)
        def _():
            relay(i, own(0), z, nz, line(2)).wait_send()
            for n in range(1, nz):
                relay(i, own(0), z, n, line(0)).wait_send()

    for copy in sent:
        copy.wait_send()


def settle(ig_ref, eg_ref, ig_hbm, eg_hbm, done):
    copies = [pltpu.make_async_copy(ig_ref, ig_hbm, done.at[0]), pltpu.make_async_copy(eg_ref, eg_hbm, done.at[1])]
    for copy in copies:
        copy.start()
    for copy in copies:
        copy.wait()


def fused(inputs, out_grad, coeff_fixed, atom_counts, experts, nz):
    n_sys, n_slots, width = inputs.shape
    n_exp, rows, _ = experts.shape
    sr, er_rows = n_sys * rows, n_exp * rows
    half_w, quarter_w = width // 2, width // 4
    most_w = width - quarter_w
    vmem = pl.BlockSpec(memory_space=pltpu.VMEM)
    hbm = pl.BlockSpec(memory_space=pltpu.HBM)
    dma = pltpu.SemaphoreType.DMA
    in_grad, expert_grad = pl.pallas_call(
        functools.partial(kernel, nz, n_sys, n_exp, rows, width),
        out_shape=(
            pltpu.VMEM(inputs.shape, BF16),
            pltpu.VMEM((er_rows, width), F32),
        ),
        in_specs=[hbm] * 5,
        out_specs=(vmem, vmem),
        scratch_shapes=[
            pltpu.SMEM(atom_counts.shape, jnp.int32),
            pltpu.SMEM(coeff_fixed.shape, jnp.int32),
            pltpu.VMEM(inputs.shape, BF16),
            pltpu.VMEM((er_rows, width), BF16),
            pltpu.VMEM(out_grad.shape, BF16),
            pltpu.VMEM((8, 128), BF16),
            pltpu.VMEM((8, 8, 128), BF16),
            pltpu.VMEM((2, 8 * sr, er_rows), BF16),
            pltpu.VMEM((2, er_rows, 8 * sr), BF16),
            pltpu.VMEM((2, 4 * sr, er_rows), BF16),
            pltpu.VMEM((2, er_rows, 4 * sr), BF16),
            pltpu.VMEM((8, nz, sr, half_w), BF16),
            pltpu.VMEM((nz, 8, sr, half_w), BF16),
            pltpu.VMEM((nz, 8, sr, half_w), BF16),
            pltpu.VMEM((nz, 2, 4, sr, half_w), BF16),
            pltpu.VMEM((nz, 3, er_rows, half_w), F32),
            pltpu.VMEM((nz - 1, 3, er_rows, half_w), BF16),
            pltpu.VMEM((nz + 1, 3, er_rows, half_w), BF16),
            pltpu.VMEM((3, nz, er_rows, half_w), BF16),
            pltpu.VMEM((2, er_rows, quarter_w), BF16),
            pltpu.VMEM((8, n_sys, nz, rows, half_w), BF16),
            pltpu.VMEM((4, n_sys, nz, 2, rows, most_w), BF16),
            pltpu.VMEM((n_sys, nz, 8, rows, half_w), BF16),
            pltpu.VMEM((n_sys, nz, 4, 2, rows, most_w), BF16),
            pltpu.VMEM((er_rows, half_w), BF16),
            pltpu.VMEM((er_rows, half_w), BF16),
            pltpu.SemaphoreType.REGULAR, dma((3 + 2 * n_sys,)), dma((1 + 4 * nz,)),
            dma((7,)), dma((7,)), dma((3,)), dma((3,)), dma((3, nz + 1)), dma((3, nz)),
            dma((nz // 2, 7)), dma((nz // 2, 7)), dma((nz, 3)), dma((nz, 3)),
            dma((nz - 1, 3)), dma((nz + 1, 3)),
            dma((nz, 7)), dma((nz, 7)), dma((nz, 3)), dma((nz, 3)), dma((1,)), dma((1,)),
        ],
        compiler_params=pltpu.CompilerParams(
            collective_id=0, has_side_effects=True, vmem_limit_bytes=48 * 1024 * 1024),
    )(*(
        pltpu.with_memory_space_constraint(a, pltpu.HBM)
        for a in (atom_counts, coeff_fixed, inputs, out_grad, experts.reshape(er_rows, width))))
    held = [pltpu.with_memory_space_constraint(a, pltpu.VMEM) for a in (in_grad, expert_grad)]
    in_grad, expert_grad = pl.pallas_call(
        settle,
        out_shape=(
            jax.ShapeDtypeStruct(inputs.shape, BF16),
            jax.ShapeDtypeStruct((er_rows, width), F32),
        ),
        in_specs=[vmem, vmem],
        out_specs=(hbm, hbm),
        scratch_shapes=[dma((2,))],
        compiler_params=pltpu.CompilerParams(vmem_limit_bytes=16 * 1024 * 1024),
    )(*held)
    return in_grad, expert_grad.reshape(n_exp, rows, width)


def plain(inputs, out_grad, coeff_fixed, atom_counts, experts):
    both = ("dp", "fsdp")
    n_sys, n_slots, width = inputs.shape
    n_exp, rows, _ = experts.shape
    coeffs = lax.all_gather(coeff_fixed, both, axis=0, tiled=True).astype(F32) / 4096.0
    valid = lax.broadcasted_iota(jnp.int32, (n_sys, n_slots), 1) < atom_counts[:, None]
    masked = jnp.where(valid[:, :, None], out_grad, jnp.zeros_like(out_grad))
    merged = jnp.einsum("se,eij->sij", coeffs, experts.astype(F32), precision=HIGH).astype(BF16)
    merged = lax.all_to_all(merged, both, split_axis=0, concat_axis=1, tiled=True)
    per_system = jnp.einsum("smi,smj->sij", inputs, masked, preferred_element_type=F32)
    per_system = lax.all_to_all(per_system, both, split_axis=1, concat_axis=0, tiled=True)
    expert_grad = jnp.einsum("se,sij->eij", coeffs, per_system, precision=HIGH)
    in_grad = jnp.einsum("smj,sij->smi", masked, merged, preferred_element_type=F32).astype(BF16)
    return in_grad, expert_grad


def solution(mesh):
    n_dp, n_fsdp = mesh.shape["dp"], mesh.shape["fsdp"]

    def shards(inputs, out_grad, coeff_fixed, atom_counts, experts):
        n_sys, _, width = inputs.shape
        n_exp, rows, _ = experts.shape
        if n_dp == 16 and n_fsdp == 2 and rows % 16 == 0 and n_sys <= 4 and n_exp <= 128 and width % 512 == 0:
            return fused(inputs, out_grad, coeff_fixed, atom_counts, experts, n_dp // 4)
        return plain(inputs, out_grad, coeff_fixed, atom_counts, experts)

    placed = (
        P(("dp", "fsdp"), None, None),
        P(("dp", "fsdp"), None, None),
        P(("dp", "fsdp"), None),
        P(("dp", "fsdp")),
        P(None, ("dp", "fsdp"), None),
    )
    return jax.shard_map(
        shards,
        mesh=mesh,
        in_specs=placed,
        out_specs=(P(("dp", "fsdp"), None, None), P(None, ("dp", "fsdp"), None)),
        check_vma=False,
    )
```

```python
import functools

import jax
import jax.numpy as jnp
from jax import lax
from jax.experimental import pallas as pl
from jax.experimental.pallas import tpu as pltpu
from jax.sharding import PartitionSpec as P

HIGH = lax.Precision.HIGHEST
MESH = pl.DeviceIdType.MESH
BF16 = jnp.bfloat16
F32 = jnp.float32
NEAR_ORDER = (5, 7, 4, 1, 6, 3, 2)
DIAGONAL = (5, 7)


def dot(a, b, ca, cb):
    return lax.dot_general(a, b, (((ca,), (cb,)), ((), ())), preferred_element_type=F32)


def kernel(nz, n_sys, n_exp, rows, width,
           counts_hbm, co_hbm, in_hbm, og_hbm, ex_hbm,
           ig_ref, eg_ref,
           counts_ref, co_ref, in_ref, ex_ref, mk, cl, ca, ka, kt, kp, kq, pb, g, pc, gc, eo, zs, zr, xg, xq, mb, mc, mr, mq, ps, pr,
           vouched, ld, loc, ka_s, ka_r, xp_s, xp_r, xz_s, xz_r, pb_s, pb_r, pc_s, pc_r, zs_s, zs_r,
           mb_s, mb_r, mc_s, mc_r, ps_s, ps_r):
    dp = lax.axis_index("dp")
    y = lax.axis_index("fsdp")
    z = dp // 4
    x = lax.rem(dp // 2, 2)
    c = lax.rem(dp, 2)
    me = x * 4 + c * 2 + y
    sr = n_sys * rows
    half_w, quarter_w = width // 2, width // 4
    span = 8 * rows
    lo_cols, hi_cols = pl.ds(0, half_w), pl.ds(half_w, half_w)
    second = slice(quarter_w, half_w)

    def cut(near_z):
        return quarter_w if near_z else half_w

    def rest(near_z):
        return slice(cut(near_z) - quarter_w, width - quarter_w)

    def flip(v, d):
        return lax.rem(v + d, 2)

    def place(fx, fc, fy):
        xx, cc, yy = flip(x, fx), flip(c, fc), flip(y, fy)
        return xx * 4 + cc * 2 + yy, ((z * 2 + xx) * 2 + cc, yy)

    def near(j):
        return place(j // 4, j // 2 % 2, j % 2)

    def turned(fp, fq, fc):
        return place(fp * (1 - c) + fq * c, fc, fq * (1 - c) + fp * c)

    p_at = x * (1 - c) + y * c
    q_at = y * (1 - c) + x * c

    half = z // 2
    zm = z + half * (3 - 2 * z)
    mid = zm == 1

    def actual(v):
        return v + half * (3 - 2 * v)

    def line(v):
        return (actual(v) * 2 + x) * 2 + c, y

    def arrival(n):
        return actual((zm, 1 - zm, 2, 3)[n])

    def target(n):
        return actual((3, 2, 1 - zm, zm)[n])

    plane = NEAR_ORDER
    peers = [near(j)[1] for j in plane if j not in DIAGONAL] + [line(1 - zm)]
    barrier = pltpu.get_barrier_semaphore()
    for peer in peers:
        pl.semaphore_signal(barrier, inc=1, device_id=peer, device_id_type=MESH)

    @pl.when(mid)
    def _():
        pl.semaphore_signal(barrier, inc=1, device_id=line(2), device_id_type=MESH)

    def load(n, src, dst):
        copy = pltpu.make_async_copy(src, dst, ld.at[n])
        copy.start()
        return copy

    co_c = load(1 + 2 * n_sys, co_hbm, co_ref)
    counts_c = load(2 + 2 * n_sys, counts_hbm, counts_ref)
    ex_c = load(0, ex_hbm, ex_ref)
    og_c = [load(1 + s, og_hbm.at[s], mk.at[s]) for s in range(n_sys)]
    in_c = [load(1 + n_sys + s, in_hbm.at[s], in_ref.at[s]) for s in range(n_sys)]

    pl.semaphore_wait(barrier, len(peers) + zm)

    def remote(src, dst, s, r, peer):
        return pltpu.make_async_remote_copy(
            src_ref=src, dst_ref=dst, send_sem=s, recv_sem=r, device_id=peer, device_id_type=MESH
        )

    sent = []

    def send(src, dst, s, r, peer):
        copy = remote(src, dst, s, r, peer)
        copy.start()
        sent.append(copy)
        return copy

    n_loc = [0]

    def local(src, dst):
        copy = pltpu.make_async_copy(src, dst, loc.at[n_loc[0]])
        n_loc[0] += 1
        copy.start()
        return copy

    def own(i):
        return ex_hbm.at[:, (lo_cols, hi_cols)[i]] if i < 2 else xg.at[2, z]

    def relay(i, src, block, n, to):
        return remote(src, xg.at[i, block], xz_s.at[i, n], xz_r.at[i, block], to)

    def offer(i):
        relay(i, own(i), z, 0, line(1 - zm)).start()

        @pl.when(mid)
        def _():
            relay(i, own(i), z, nz, line(2)).start()

    pl.semaphore_signal(vouched, inc=1, device_id=near(4)[1], device_id_type=MESH)
    xp = send(own(1), xg.at[2, z], xp_s.at[0], xp_r.at[0], turned(1, 0, 0)[1])
    offer(0)
    offer(1)
    xq_c = send(ex_hbm.at[:, second], xq.at[0], xp_s.at[1], xp_r.at[1], turned(1, 0, 0)[1])
    col = lax.broadcasted_iota(jnp.int32, cl.shape, 1)
    row = lax.broadcasted_iota(jnp.int32, cl.shape, 0)
    system = lax.rem(row, n_sys)
    fixed = jnp.zeros(cl.shape, jnp.int32)
    co_c.wait()
    counts_c.wait()
    for s in range(n_sys):
        for e in range(n_exp):
            fixed = jnp.where((system == s) & (col == e), co_ref[s, e], fixed)
    high, low = (fixed >> 6).astype(F32) / 64.0, (fixed & 63).astype(F32) / 4096.0
    cl[...] = jnp.where(row < n_sys, high, low).astype(BF16)
    ca_c = []

    def tell(j):
        ca_c.append(send(cl, ca.at[me], ka_s.at[j - 1], ka_r.at[j - 1], near(j)[1]))

    for j in plane:
        if j not in DIAGONAL:
            tell(j)
    ca_own = local(cl, ca.at[me])

    for s in range(n_sys):
        og_c[s].wait()
        slot = lax.broadcasted_iota(jnp.int32, mk.shape[1:], 0)
        mk[s] = jnp.where(slot < counts_ref[s], mk[s], jnp.zeros(mk.shape[1:], BF16))
    for copy in in_c:
        copy.wait()

    pb_c, g_own, pc_c, gc_own = {}, {}, {}, {}
    takers = ((0, 0, 0), (0, 0, 1), (0, 1, 0), (1, 0, 1))

    def seat(b):
        fx, fc, fy = flip(x, b // 4), flip(c, b // 2 % 2), flip(y, b % 2)
        fp, fq = fx * (1 - c) + fy * c, fy * (1 - c) + fx * c
        return (1 - fc) * (4 * fq + fp) + fc * (2 + 4 * fp + fq)

    def produce(k):
        lanes = pl.ds(pl.multiple_of(target(k) * span, span), span)
        n = half_w
        for s in range(n_sys):
            prod = dot(in_ref[s, :, lanes], mk[s], 0, 0).astype(BF16)
            for b in range(8):
                pb[b, k, s * rows:(s + 1) * rows, :] = prod[b * rows:(b + 1) * rows, :n]
                pc[k, seat(b), s * rows:(s + 1) * rows, :] = prod[b * rows:(b + 1) * rows, n:]
        for v in (2, 3, 1):
            at = (p_at if v % 2 else q_at) * 2 + c
            pc_c[k, v] = send(pc.at[k, 2 * v:2 * v + 2], gc.at[k, :, at], pc_s.at[k, v - 1], pc_r.at[k, v - 1],
                              turned(*takers[v])[1])
        gc_own[k] = local(pc.at[k, 0:2], gc.at[k, :, q_at * 2 + c])

    def deal(h):
        two = slice(2 * h, 2 * h + 2)
        for j in plane:
            to, peer = near(j)
            pb_c[h, j] = send(pb.at[to, two], g.at[two, me], pb_s.at[h, j - 1], pb_r.at[h, j - 1], peer)
        g_own[h] = local(pb.at[me, two], g.at[two, me])

    mb_c, m_own, mc_c, mc_own = {}, {}, {}, {}

    def held(k, i):
        return ex_ref[:, (lo_cols, hi_cols)[i]] if k == 0 and i < 2 else xg[i, arrival(k)]

    def mixed(weights, block):
        return (dot(weights[0], block, 1, 0) + dot(weights[1], block, 1, 0)).astype(BF16)

    def merge(*ks):
        span_k = slice(ks[0], ks[-1] + 1)
        close = ks[0] < 2
        n, others = cut(close), rest(close)
        for k in ks:
            for i in (1, 2):
                to = flip(p_at, i - 1)
                mc[:, :, k, to, :, quarter_w:] = mixed(kp, held(k, i)).reshape(4, n_sys, rows, half_w)
                if close:
                    piece = xq[k] if i == 2 else held(k, 0)[:, second]
                    mc[:, :, k, to, :, :quarter_w] = mixed(kp, piece).reshape(4, n_sys, rows, quarter_w)
        k = ks[-1]
        at = 2 * c + q_at
        for v, (fq, fc) in ((2, (1, 0)), (3, (1, 1)), (1, (0, 1))):
            u = flip(q_at, fq) * 2 + flip(c, fc)
            mc_c[k, v] = send(mc.at[u, :, span_k, :, :, others], mq.at[:, span_k, at, :, :, others],
                              mc_s.at[k, v - 1], mc_r.at[k, v - 1], turned(0, fq, fc)[1])
        mc_own[k] = local(mc.at[q_at * 2 + c, :, span_k, :, :, others], mq.at[:, span_k, at, :, :, others])
        for k in ks:
            mb[:, :, k, :, :n] = mixed(ka, held(k, 0)[:, :n]).reshape(8, n_sys, rows, n)
        for j in plane:
            to, peer = near(j)
            mb_c[k, j] = send(mb.at[to, :, span_k, :, :n], mr.at[:, span_k, me, :, :n],
                              mb_s.at[k, j - 1], mb_r.at[k, j - 1], peer)
        m_own[k] = local(mb.at[me, :, span_k, :, :n], mr.at[:, span_k, me, :, :n])

    def landed(slot, i):
        remote(zs.at[0, i], zr.at[slot, i], zs_s.at[0, i], zs_r.at[slot, i], line(1 - zm)).wait_recv()
        return zr[slot, i].astype(F32)

    def reduce(k):
        gc_own[k].wait()
        for v in (1, 2, 3):
            pc_c[k, v].wait_recv()
        for i in (1, 0):
            block = gc[k, i].reshape(4 * sr, half_w)
            eo[k, i + 1] = dot(kq[0], block, 1, 0) + dot(kq[1], block, 1, 0)
            begin(k, i + 1)
        if k % 2 == 0:
            g_own[k // 2].wait()
            for j in plane:
                pb_c[k // 2, j].wait_recv()
        block = g[k].reshape(8 * sr, half_w)
        eo[k, 0] = dot(kt[0], block, 1, 0) + dot(kt[1], block, 1, 0)
        begin(k, 0)

    def onward(k, i):
        slot = (2 * zm, 1 + 3 * zm, 3)[k]
        return remote(zs.at[k, i], zr.at[slot, i], zs_s.at[k, i], zs_r.at[slot, i],
                      line((zm + 1, zm + 1, 1 - zm)[k]))

    def begin(k, i):
        if k < nz - 1:
            @pl.when(zm == 0)
            def _():
                zs[k, i] = eo[k, i].astype(BF16)
                onward(k, i).start()

    def proceed(k, i):
        @pl.when(mid)
        def _():
            zs[k, i] = (eo[k, i] + landed(k, i)).astype(BF16)
            onward(k, i).start()

    def finish(k):
        if k in m_own:
            m_own[k].wait()
            mc_own[k].wait()
            for j in plane:
                mb_c[k, j].wait_recv()
            for v in (1, 2, 3):
                mc_c[k, v].wait_recv()
        lanes = pl.ds(pl.multiple_of(arrival(k) * span, span), span)
        for s in range(n_sys):
            first = mr[s, k, :, :, :cut(k < 2)].reshape(span, cut(k < 2))
            last = jnp.concatenate(
                [mq[s, k, (b % 2, 2 + b // 4)[b // 2 % 2], (b // 4, b % 2)[b // 2 % 2], :, rest(k < 2)]
                 for b in range(8)], axis=0)
            ig_ref[s, :, lanes] = dot(mk[s], jnp.concatenate([first, last], axis=1), 1, 1).astype(BF16)

    def came(n, i):
        block = arrival(n)
        relay(i, own(0), block, n, line(1 - zm)).wait_recv()

    def handed(n, i):
        block = arrival(n)

        @pl.when(mid)
        def _():
            came(n, i)
            relay(i, xg.at[i, block], block, n, line(2 if n == 1 else 0)).start()

    def awaited(n):
        @pl.when(zm == 0)
        def _():
            for i in range(3):
                came(n, i)

    produce(0)
    xp.wait_recv()
    offer(2)
    produce(1)
    pl.semaphore_wait(vouched, 1)
    for j in DIAGONAL:
        tell(j)
    deal(0)
    produce(2)
    produce(3)
    deal(1)
    xq_c.wait_recv()
    xq_n = send(xq.at[0], xq.at[1], xp_s.at[2], xp_r.at[2], line(1 - zm))

    ex_c.wait()
    ca_own.wait()
    for copy in ca_c:
        copy.wait_recv()
    er_rows = n_exp * rows
    lane = lax.broadcasted_iota(jnp.int32, (cl.shape[1], er_rows), 1)
    first = lax.broadcasted_iota(jnp.int32, (cl.shape[1], er_rows), 0) * rows
    pick = jnp.where((lane >= first) & (lane < first + rows), 1.0, 0.0).astype(BF16)
    told = ca[...].astype(F32).reshape(8 * cl.shape[0], cl.shape[1]).astype(BF16)
    wide = dot(told, pick, 1, 0)
    across = lax.broadcasted_iota(jnp.int32, (rows, er_rows), 1) % rows
    diagonal = across == lax.broadcasted_iota(jnp.int32, (rows, er_rows), 0)
    for d in range(8):
        for h in range(2):
            for s in range(n_sys):
                at = d * cl.shape[0] + h * n_sys + s
                value = jnp.broadcast_to(wide[at:at + 1, :], (rows, er_rows))
                spot = (d * n_sys + s) * rows
                ka[h, spot:spot + rows, :] = jnp.where(diagonal, value, 0.0).astype(BF16)
    for h in range(2):
        for u in range(4):
            uq, uc = u // 2, u % 2
            at = (x * (1 - c) + uq * c) * 4 + uc * 2 + uq * (1 - c) + y * c
            kp[h, u * sr:(u + 1) * sr, :] = ka[h, pl.ds(pl.multiple_of(at * sr, sr), sr), :]
    for h in range(2):
        kt[h] = ka[h].T
        kq[h] = kp[h].T

    for i in range(2):
        handed(1, i)
        handed(2, i)
    reduce(0)
    handed(1, 2)
    handed(2, 2)
    reduce(1)
    awaited(1)
    xq_n.wait_recv()
    merge(0, 1)
    handed(3, 0)
    proceed(0, 2)
    handed(3, 1)
    proceed(0, 1)
    reduce(2)
    handed(3, 2)
    proceed(0, 0)
    awaited(2)
    merge(2)
    reduce(3)
    awaited(3)
    merge(3)
    for i in (2, 1, 0):
        proceed(1, i)
        proceed(2, i)
    finish(1)
    finish(0)

    def total(i):
        eo[nz - 1, i] += landed(3, i)

        @pl.when(mid)
        def _():
            eo[nz - 1, i] += landed(4, i)

    total(2)
    ps[...] = eo[nz - 1, 2].astype(BF16)
    ps_c = send(ps, pr, ps_s.at[0], ps_r.at[0], turned(1, 0, 0)[1])
    total(1)
    finish(2)
    finish(3)
    total(0)
    eg_ref[:, lo_cols] = eo[nz - 1, 0]
    ps_c.wait_recv()
    eg_ref[:, hi_cols] = eo[nz - 1, 1] + pr[...].astype(F32)

    for i in range(3):
        relay(i, own(0), z, 0, line(1 - zm)).wait_send()
        for k in range(nz - 1):
            onward(k, i).wait_send()

        @pl.when(mid)
        def _():
            relay(i, own(0), z, nz, line(2)).wait_send()
            for n in range(1, nz):
                relay(i, own(0), z, n, line(0)).wait_send()

    for copy in sent:
        copy.wait_send()


def settle(ig_ref, eg_ref, ig_hbm, eg_hbm, done):
    copies = [pltpu.make_async_copy(ig_ref, ig_hbm, done.at[0]), pltpu.make_async_copy(eg_ref, eg_hbm, done.at[1])]
    for copy in copies:
        copy.start()
    for copy in copies:
        copy.wait()


def fused(inputs, out_grad, coeff_fixed, atom_counts, experts, nz):
    n_sys, n_slots, width = inputs.shape
    n_exp, rows, _ = experts.shape
    sr, er_rows = n_sys * rows, n_exp * rows
    half_w, quarter_w = width // 2, width // 4
    most_w = width - quarter_w
    vmem = pl.BlockSpec(memory_space=pltpu.VMEM)
    hbm = pl.BlockSpec(memory_space=pltpu.HBM)
    dma = pltpu.SemaphoreType.DMA
    in_grad, expert_grad = pl.pallas_call(
        functools.partial(kernel, nz, n_sys, n_exp, rows, width),
        out_shape=(
            pltpu.VMEM(inputs.shape, BF16),
            pltpu.VMEM((er_rows, width), F32),
        ),
        in_specs=[hbm] * 5,
        out_specs=(vmem, vmem),
        scratch_shapes=[
            pltpu.SMEM(atom_counts.shape, jnp.int32),
            pltpu.SMEM(coeff_fixed.shape, jnp.int32),
            pltpu.VMEM(inputs.shape, BF16),
            pltpu.VMEM((er_rows, width), BF16),
            pltpu.VMEM(out_grad.shape, BF16),
            pltpu.VMEM((8, 128), BF16),
            pltpu.VMEM((8, 8, 128), BF16),
            pltpu.VMEM((2, 8 * sr, er_rows), BF16),
            pltpu.VMEM((2, er_rows, 8 * sr), BF16),
            pltpu.VMEM((2, 4 * sr, er_rows), BF16),
            pltpu.VMEM((2, er_rows, 4 * sr), BF16),
            pltpu.VMEM((8, nz, sr, half_w), BF16),
            pltpu.VMEM((nz, 8, sr, half_w), BF16),
            pltpu.VMEM((nz, 8, sr, half_w), BF16),
            pltpu.VMEM((nz, 2, 4, sr, half_w), BF16),
            pltpu.VMEM((nz, 3, er_rows, half_w), F32),
            pltpu.VMEM((nz - 1, 3, er_rows, half_w), BF16),
            pltpu.VMEM((nz + 1, 3, er_rows, half_w), BF16),
            pltpu.VMEM((3, nz, er_rows, half_w), BF16),
            pltpu.VMEM((2, er_rows, quarter_w), BF16),
            pltpu.VMEM((8, n_sys, nz, rows, half_w), BF16),
            pltpu.VMEM((4, n_sys, nz, 2, rows, most_w), BF16),
            pltpu.VMEM((n_sys, nz, 8, rows, half_w), BF16),
            pltpu.VMEM((n_sys, nz, 4, 2, rows, most_w), BF16),
            pltpu.VMEM((er_rows, half_w), BF16),
            pltpu.VMEM((er_rows, half_w), BF16),
            pltpu.SemaphoreType.REGULAR, dma((3 + 2 * n_sys,)), dma((1 + 4 * nz,)),
            dma((7,)), dma((7,)), dma((3,)), dma((3,)), dma((3, nz + 1)), dma((3, nz)),
            dma((nz // 2, 7)), dma((nz // 2, 7)), dma((nz, 3)), dma((nz, 3)),
            dma((nz - 1, 3)), dma((nz + 1, 3)),
            dma((nz, 7)), dma((nz, 7)), dma((nz, 3)), dma((nz, 3)), dma((1,)), dma((1,)),
        ],
        compiler_params=pltpu.CompilerParams(
            collective_id=0, has_side_effects=True, vmem_limit_bytes=48 * 1024 * 1024),
    )(*(
        pltpu.with_memory_space_constraint(a, pltpu.HBM)
        for a in (atom_counts, coeff_fixed, inputs, out_grad, experts.reshape(er_rows, width))))
    held = [pltpu.with_memory_space_constraint(a, pltpu.VMEM) for a in (in_grad, expert_grad)]
    in_grad, expert_grad = pl.pallas_call(
        settle,
        out_shape=(
            jax.ShapeDtypeStruct(inputs.shape, BF16),
            jax.ShapeDtypeStruct((er_rows, width), F32),
        ),
        in_specs=[vmem, vmem],
        out_specs=(hbm, hbm),
        scratch_shapes=[dma((2,))],
        compiler_params=pltpu.CompilerParams(vmem_limit_bytes=16 * 1024 * 1024),
    )(*held)
    return in_grad, expert_grad.reshape(n_exp, rows, width)


def plain(inputs, out_grad, coeff_fixed, atom_counts, experts):
    both = ("dp", "fsdp")
    n_sys, n_slots, width = inputs.shape
    n_exp, rows, _ = experts.shape
    coeffs = lax.all_gather(coeff_fixed, both, axis=0, tiled=True).astype(F32) / 4096.0
    valid = lax.broadcasted_iota(jnp.int32, (n_sys, n_slots), 1) < atom_counts[:, None]
    masked = jnp.where(valid[:, :, None], out_grad, jnp.zeros_like(out_grad))
    merged = jnp.einsum("se,eij->sij", coeffs, experts.astype(F32), precision=HIGH).astype(BF16)
    merged = lax.all_to_all(merged, both, split_axis=0, concat_axis=1, tiled=True)
    per_system = jnp.einsum("smi,smj->sij", inputs, masked, preferred_element_type=F32)
    per_system = lax.all_to_all(per_system, both, split_axis=1, concat_axis=0, tiled=True)
    expert_grad = jnp.einsum("se,sij->eij", coeffs, per_system, precision=HIGH)
    in_grad = jnp.einsum("smj,sij->smi", masked, merged, preferred_element_type=F32).astype(BF16)
    return in_grad, expert_grad


def solution(mesh):
    n_dp, n_fsdp = mesh.shape["dp"], mesh.shape["fsdp"]

    def shards(inputs, out_grad, coeff_fixed, atom_counts, experts):
        n_sys, _, width = inputs.shape
        n_exp, rows, _ = experts.shape
        if n_dp == 16 and n_fsdp == 2 and rows % 16 == 0 and n_sys <= 4 and n_exp <= 128 and width % 512 == 0:
            return fused(inputs, out_grad, coeff_fixed, atom_counts, experts, n_dp // 4)
        return plain(inputs, out_grad, coeff_fixed, atom_counts, experts)

    placed = (
        P(("dp", "fsdp"), None, None),
        P(("dp", "fsdp"), None, None),
        P(("dp", "fsdp"), None),
        P(("dp", "fsdp")),
        P(None, ("dp", "fsdp"), None),
    )
    return jax.shard_map(
        shards,
        mesh=mesh,
        in_specs=placed,
        out_specs=(P(("dp", "fsdp"), None, None), P(None, ("dp", "fsdp"), None)),
        check_vma=False,
    )
```
